256 devices in a mesh: grp: 16 (over x_hi, z), brick: 16 (over y, x_lo, core).
Axes of the slice: x: 4 (x_hi: 2, x_lo: 2; x = x_hi * 2 + x_lo), y: 4, z: 8, core: 2. Of those that a mesh axis runs over, the one named last changes fastest.
Arguments:
- deformation_vector: float32 [3, 64, 256, 256], P(None, 'grp', 'brick'), may hold values from -4 to 4
- applied_traction: float32 [3, 64, 256, 256], P(None, 'grp', 'brick'), may hold values from 4 to 16
- heat_level: float32 [64, 256, 256], P('grp', 'brick'), may hold values from -6 to 6
- stiffness_main_terms: float32 [3, 64, 256, 256], P(None, 'grp', 'brick'), may hold values from 8 to 10
- stiffness_cross_terms: float32 [3, 64, 256, 256], P(None, 'grp', 'brick'), may hold values from -0.8 to 0.8
- normal_clearance: float32 [64, 256, 256], P('grp', 'brick'), may hold values from -0.5 to 1
- touching_flag: int32 [64, 256, 256], P('grp', 'brick'), may hold values 0 or 1
- clipped_normal_flag: int32 [64, 256, 256], P('grp', 'brick'), may hold values 0 or 1
Outputs:
- moved: float32 [3, 64, 256, 256], P(None, 'grp', 'brick')
- residual: float32 [3, 64, 256, 256], P(None, 'grp', 'brick')
The draws below stay inside these ranges and needn't reach their ends.
All inputs are finite; a program needn't handle non-finite values. No bound on the sum of `touching_flag` or of `clipped_normal_flag` on one device may be relied on, other than what follows from the above.
Results may differ from the reference program's by a relative error of at most 0.00002.
Values sent between devices are 32-bit elements; how exact they have to be, the bound alone decides.
No kernel may reach another device: no remote copies, remote signals or barrier semaphores. Data moves between devices by JAX's collectives and lax.ppermute only.
A program may use at most 128 MiB of HBM per device.

```python
import jax
import jax.numpy as jnp

POINTS_ALONG_X = 64
POINTS_ALONG_Y = 256
POINTS_ALONG_Z = 256


def set_ends(entries, own_key, least, largest):
    longest = entries.shape.index(max(entries.shape))
    spots = []
    for shift in (0, 1):
        where = [jax.random.randint(jax.random.fold_in(own_key, axis), (), 0, length) for axis, length in enumerate(entries.shape)]
        where[longest] = (where[longest] + shift) % entries.shape[longest]
        spots.append(tuple(where))
    return entries.at[spots[0]].set(least).at[spots[1]].set(largest)


def levels(stream_key, dims, pieces, smallest, largest):
    gain, own = 1.0, jax.random.fold_in(stream_key, 6)
    for position, shards_of in pieces:
        draws = jnp.exp(jax.random.uniform(jax.random.fold_in(own, position), (shards_of,), jnp.float32, smallest / len(pieces), largest / len(pieces)))
        gain = gain * jnp.repeat(draws, dims[position] // shards_of).reshape([-1 if axis == position else 1 for axis in range(len(dims))])
    return gain


def normal_values(own_key, dims, deviation, reach, cuts=(), kind=jnp.bfloat16):
    result = deviation * jax.random.normal(own_key, dims, jnp.float32)
    if cuts:
        result = result * levels(own_key, dims, cuts, -0.22, 0.18)
    return jnp.clip(result, -reach, reach).astype(kind)


def setup_inputs(seed: int = 0) -> dict:
    arg_keys = jax.random.split(jax.random.key(seed), 9)
    return {
        "deformation_vector": normal_values(arg_keys[0], (3, POINTS_ALONG_X, POINTS_ALONG_Y, POINTS_ALONG_Z), 0.5, 4.0, ((1, 16), (2, 16)), jnp.float32),
        "applied_traction": jnp.clip(4.0 + 12.0 * jax.random.uniform(arg_keys[1], (3, POINTS_ALONG_X, POINTS_ALONG_Y, POINTS_ALONG_Z), jnp.float32) ** levels(arg_keys[1], (3, POINTS_ALONG_X, POINTS_ALONG_Y, POINTS_ALONG_Z), ((1, 16), (2, 16)), -0.2, 0.2), 4.0, 16.0),
        "heat_level": normal_values(arg_keys[2], (POINTS_ALONG_X, POINTS_ALONG_Y, POINTS_ALONG_Z), 1.0, 6.0, ((0, 16), (1, 16)), jnp.float32),
        "stiffness_main_terms": jnp.clip(8.0 + 2.0 * jax.random.uniform(arg_keys[3], (3, POINTS_ALONG_X, POINTS_ALONG_Y, POINTS_ALONG_Z), jnp.float32) ** levels(arg_keys[3], (3, POINTS_ALONG_X, POINTS_ALONG_Y, POINTS_ALONG_Z), ((1, 16), (2, 16)), -0.2, 0.2), 8.0, 10.0),
        "stiffness_cross_terms": jnp.clip(jax.random.uniform(arg_keys[4], (3, POINTS_ALONG_X, POINTS_ALONG_Y, POINTS_ALONG_Z), jnp.float32, -0.8, 0.8) * levels(arg_keys[4], (3, POINTS_ALONG_X, POINTS_ALONG_Y, POINTS_ALONG_Z), ((1, 16), (2, 16)), -0.4, 0.0), -0.8, 0.8),
        "normal_clearance": jnp.clip(-0.5 + 1.5 * jax.random.uniform(arg_keys[5], (POINTS_ALONG_X, POINTS_ALONG_Y, POINTS_ALONG_Z), jnp.float32) ** levels(arg_keys[5], (POINTS_ALONG_X, POINTS_ALONG_Y, POINTS_ALONG_Z), ((0, 16), (1, 16)), -0.2, 0.2), -0.5, 1.0),
        "touching_flag": set_ends((jax.random.randint(arg_keys[6], (POINTS_ALONG_X, POINTS_ALONG_Y, POINTS_ALONG_Z), 0, 3) < 1).astype(jnp.int32), jax.random.fold_in(arg_keys[6], 1), 0, 1),
        "clipped_normal_flag": set_ends((jax.random.randint(arg_keys[7], (POINTS_ALONG_X, POINTS_ALONG_Y, POINTS_ALONG_Z), 0, 2) < 1).astype(jnp.int32), jax.random.fold_in(arg_keys[7], 1), 0, 1),
    }


OMEGA = 0.6
FREE = 1000.0


def block_times(diag, off, field):
    a, b, c = diag[0], diag[1], diag[2]
    d, e, f = off[0], off[1], off[2]
    return jnp.stack([a * field[0] + d * field[1] + f * field[2],
                      d * field[0] + b * field[1] + e * field[2],
                      f * field[0] + e * field[1] + c * field[2]])


def inverse_entries(diag, off):
    a, b, c = diag[0], diag[1], diag[2]
    d, e, f = off[0], off[1], off[2]
    i00 = b * c - e * e
    i11 = a * c - f * f
    i22 = a * b - d * d
    i01 = f * e - d * c
    i12 = d * f - a * e
    i02 = d * e - b * f
    scale = 1.0 / (a * i00 + d * i01 + f * i02)
    return jnp.stack([i00 * scale, i11 * scale, i22 * scale, i01 * scale, i12 * scale, i02 * scale])


def inverse_times(inv, rest):
    return jnp.stack([inv[0] * rest[0] + inv[3] * rest[1] + inv[5] * rest[2],
                      inv[3] * rest[0] + inv[1] * rest[1] + inv[4] * rest[2],
                      inv[5] * rest[0] + inv[4] * rest[1] + inv[2] * rest[2]])


def operate(field, diag, off):
    padded = jnp.pad(field, ((0, 0), (1, 1), (1, 1), (1, 1)))
    beside = padded[:, 2:, 1:-1, 1:-1] + padded[:, :-2, 1:-1, 1:-1]
    beside = beside + padded[:, 1:-1, 2:, 1:-1] + padded[:, 1:-1, :-2, 1:-1]
    beside = beside + padded[:, 1:-1, 1:-1, 2:] + padded[:, 1:-1, 1:-1, :-2]
    return block_times(diag, off, field) - beside


def project(field, obstacle):
    return jnp.concatenate([jnp.minimum(field[0], obstacle)[None], field[1:]], 0)


def sweep(field, force, diag, off, inv, obstacle):
    rest = force - operate(field, diag, off)
    return project(field + OMEGA * inverse_times(inv, rest), obstacle)


def grouped(x):
    s = x.shape
    return x.reshape(s[:-3] + (s[-3] // 2, 2, s[-2] // 2, 2, s[-1] // 2, 2))


def group_sum(x):
    return jnp.sum(grouped(x), axis=(-5, -3, -1))


def group_min(x):
    return jnp.min(grouped(x), axis=(-5, -3, -1))


def spread(x):
    return jnp.repeat(jnp.repeat(jnp.repeat(x, 2, axis=-3), 2, axis=-2), 2, axis=-1)


def reference(deformation_vector, applied_traction, heat_level, stiffness_main_terms, stiffness_cross_terms, normal_clearance, touching_flag, clipped_normal_flag):
    heating_traction = jnp.pad(heat_level, 1)
    drift = jnp.stack([heating_traction[2:, 1:-1, 1:-1] - heating_traction[:-2, 1:-1, 1:-1],
                       heating_traction[1:-1, 2:, 1:-1] - heating_traction[1:-1, :-2, 1:-1],
                       heating_traction[1:-1, 1:-1, 2:] - heating_traction[1:-1, 1:-1, :-2]])
    force = applied_traction - drift
    inv1 = inverse_entries(stiffness_main_terms, stiffness_cross_terms)
    obstacle1 = jnp.where(touching_flag == 1, normal_clearance, FREE)
    field = sweep(deformation_vector, force, stiffness_main_terms, stiffness_cross_terms, inv1, obstacle1)
    field = sweep(field, force, stiffness_main_terms, stiffness_cross_terms, inv1, obstacle1)
    rest = force - operate(field, stiffness_main_terms, stiffness_cross_terms)
    rest = jnp.concatenate([jnp.where(clipped_normal_flag == 1, 0.0, rest[0])[None], rest[1:]], 0)
    force2 = 0.25 * group_sum(rest)
    diag2 = 0.125 * group_sum(stiffness_main_terms)
    off2 = 0.125 * group_sum(stiffness_cross_terms)
    allowed = (touching_flag == 1) & (clipped_normal_flag == 0)
    obstacle2 = group_min(jnp.where(allowed, normal_clearance - field[0], FREE))
    inv2 = inverse_entries(diag2, off2)
    middle = jnp.zeros_like(force2)
    middle = sweep(middle, force2, diag2, off2, inv2, obstacle2)
    middle = sweep(middle, force2, diag2, off2, inv2, obstacle2)
    force3 = 0.25 * group_sum(force2 - operate(middle, diag2, off2))
    diag3 = 0.125 * group_sum(diag2)
    off3 = 0.125 * group_sum(off2)
    obstacle3 = group_min(obstacle2 - middle[0])
    inv3 = inverse_entries(diag3, off3)
    lowest = jnp.zeros_like(force3)
    lowest = sweep(lowest, force3, diag3, off3, inv3, obstacle3)
    lowest = sweep(lowest, force3, diag3, off3, inv3, obstacle3)
    middle = middle + spread(lowest)
    middle = sweep(middle, force2, diag2, off2, inv2, obstacle2)
    middle = sweep(middle, force2, diag2, off2, inv2, obstacle2)
    correction = spread(middle)
    correction = jnp.concatenate([jnp.where(clipped_normal_flag == 1, 0.0, correction[0])[None], correction[1:]], 0)
    field = field + correction
    field = sweep(field, force, stiffness_main_terms, stiffness_cross_terms, inv1, obstacle1)
    field = sweep(field, force, stiffness_main_terms, stiffness_cross_terms, inv1, obstacle1)
    residual = force - operate(field, stiffness_main_terms, stiffness_cross_terms)
    return field, residual
```

```python
import jax
import jax.numpy as jnp
from jax import lax
from jax.experimental import pallas as pl
from jax.experimental.pallas import tpu as pltpu
from jax.sharding import PartitionSpec as P

OMEGA = 0.6
KEEP = 0.4
FREE = 1000.0
F32 = jnp.float32
HIGH = lax.Precision.HIGHEST
EVEN_SLOTS = (4, 5, 3, 2, 6, 7, 1, 0)


def inverse(a, b, c, d, e, f):
    i00 = b * c - e * e
    i11 = a * c - f * f
    i22 = a * b - d * d
    i01 = f * e - d * c
    i12 = d * f - a * e
    i02 = d * e - b * f
    det = a * i00 + d * i01 + f * i02
    scale = jnp.where(det == 0.0, 0.0, 1.0 / jnp.where(det == 0.0, 1.0, det))
    return [i00 * scale, i11 * scale, i22 * scale, i01 * scale, i12 * scale, i02 * scale]


def symmetric_times(m, r):
    return [
        m[0] * r[0] + m[3] * r[1] + m[5] * r[2],
        m[3] * r[0] + m[1] * r[1] + m[4] * r[2],
        m[5] * r[0] + m[4] * r[1] + m[2] * r[2],
    ]


def lanes(shape):
    return lax.broadcasted_iota(jnp.int32, shape, 1)


def rows(shape):
    return lax.broadcasted_iota(jnp.int32, shape, 0)


def beside(x, step=1):
    n, m = x.shape
    lane = lanes(x.shape)
    left = jnp.where(lane < step, 0.0, pltpu.roll(x, step, axis=1))
    right = jnp.where(lane >= m - step, 0.0, pltpu.roll(x, m - step, axis=1))
    return (left + right) + (pltpu.roll(x, step, axis=0) + pltpu.roll(x, n - step, axis=0))


def sides(g):
    return (jnp.bitwise_and(g, 1) == 0), jnp.logical_and(g > 0, g < 15)


def pack_grp(pos, disp, trac, heat, main, cross, clear, touch, clip, me, mo, kinv, obst):
    par = jnp.bitwise_and(pos[0], 1)
    obst[...] = jnp.where(touch[...] == 1, clear[...], FREE)
    for p in range(4):
        inv = inverse(main[0, p], main[1, p], main[2, p], cross[0, p], cross[1, p], cross[2, p])
        for k in range(6):
            kinv[k, p] = inv[k]
    for msg, at in ((me, 1 - par), (mo, par)):
        for c in range(3):
            msg[3 * c : 3 * c + 3] = disp[c, pl.ds(at, 3)]
        msg[9:12] = heat[pl.ds(at, 3)]
        msg[12:15] = clip[pl.ds(at, 3)].astype(F32)
        for c in range(3):
            msg[15 + 2 * c : 17 + 2 * c] = trac[c, pl.ds(2 * at, 2)]
        for k in range(6):
            msg[21 + 2 * k : 23 + 2 * k] = kinv[k, pl.ds(2 * at, 2)]
        msg[33:35] = obst[pl.ds(2 * at, 2)]


def wide_plane(own, re, ro, even, inside, base, width, p):
    if p < width:
        return jnp.where(even, jnp.where(inside, ro[base + p], 0.0), re[base + p])
    if p < width + 4:
        return own(p - width)
    q = base + p - width - 4
    return jnp.where(even, re[q], jnp.where(inside, ro[q], 0.0))


def fields(disp, heat, clip, trac, kinv, obst):
    wide = [lambda p, c=c: disp[c, p] for c in range(3)]
    wide += [lambda p: heat[p], lambda p: clip[p].astype(F32)]
    near = [lambda p, c=c: trac[c, p] for c in range(3)]
    near += [lambda p, k=k: kinv[k, p] for k in range(6)]
    near += [lambda p: obst[p]]
    return wide, near


def put(msg, t, r, x):
    n = x.shape[0]
    msg[t, r : r + n, :] = x[:, :128]
    msg[t, r + 4 : r + 4 + n, :] = x[:, 128:]


def pack_brick(pos, disp, heat, clip, trac, kinv, obst, re, ro, be, bo):
    even, inside = sides(pos[0])
    up = jnp.bitwise_and(pos[1], 1) == 0
    wide, near = fields(disp, heat, clip, trac, kinv, obst)
    for f in range(5):
        for p in range(10):
            x = wide_plane(wide[f], re, ro, even, inside, 3 * f, 3, p)
            low, high = x[0:3], x[13:16]
            put(be, f * 10 + p, 0, jnp.where(up, high, low))
            put(bo, f * 10 + p, 0, jnp.where(up, low, high))
    for f in range(10):
        for p in range(8):
            x = wide_plane(near[f], re, ro, even, inside, 15 + 2 * f, 2, p)
            low, high = x[0:2], x[14:16]
            put(be, 50 + f * 4 + p // 2, 2 * (p % 2), jnp.where(up, high, low))
            put(bo, 50 + f * 4 + p // 2, 2 * (p % 2), jnp.where(up, low, high))


def brick_rows(be, bo, up, inside, t, r, n):
    e = jnp.concatenate([be[t, r : r + n, :], be[t, r + 4 : r + 4 + n, :]], 1)
    o = jnp.concatenate([bo[t, r : r + n, :], bo[t, r + 4 : r + 4 + n, :]], 1)
    o = jnp.where(inside, o, 0.0)
    return jnp.where(up, o, e), jnp.where(up, e, o)


def smooth(v0, force, kinv, obst, v1, v2):
    def one(src, dst, shift, planes):
        def body(p, carry):
            rest = []
            for c in range(3):
                near = src[c, p] + src[c, p + 2] + beside(src[c, p + 1])
                rest.append(force[c, p + shift] + near)
            inv = [kinv[k, p + shift] for k in range(6)]
            step = symmetric_times(inv, rest)
            new = [KEEP * src[c, p + 1] + OMEGA * step[c] for c in range(3)]
            dst[0, p] = jnp.minimum(new[0], obst[p + shift])
            dst[1, p] = new[1]
            dst[2, p] = new[2]
            return carry

        lax.fori_loop(0, planes, body, 0)

    one(v0, v1, 0, 8)
    one(v1, v2, 1, 6)


def residual_plane(v2, force, main, cross, p):
    own = [v2[c, p + 1][8:24] for c in range(3)]
    mat = [main[c, p] for c in range(3)] + [cross[c, p] for c in range(3)]
    kv = symmetric_times(mat, own)
    out = []
    for c in range(3):
        near = v2[c, p, 8:24, :] + v2[c, p + 2, 8:24, :] + beside(v2[c, p + 1])[8:24]
        out.append(force[c, p + 2, 8:24, :] - (kv[c] - near))
    return out


def presmooth(
    pos, disp, heat, clip, trac, kinv, obst, main, cross, clear, touch, re, ro, be, bo,
    force_x, kinv_x, obst_x, clip_x, pre, em, om,
    v0, heat_x, v1, v2, rest, gath,
):
    even, inside = sides(pos[0])
    up, inner = sides(pos[1])
    par = jnp.bitwise_and(pos[0], 1)
    wide, near = fields(disp, heat, clip, trac, kinv, obst)
    wide_to = [lambda p, c=c: v0.at[c, p] for c in range(3)]
    wide_to += [lambda p: heat_x.at[p], lambda p: clip_x.at[p]]
    near_to = [lambda p, c=c: force_x.at[c, p] for c in range(3)]
    near_to += [lambda p, k=k: kinv_x.at[k, p] for k in range(6)]
    near_to += [lambda p: obst_x.at[p]]
    for f in range(5):
        for p in range(10):
            to = wide_to[f](p)
            to[8:24, :] = wide_plane(wide[f], re, ro, even, inside, 3 * f, 3, p)
            low, high = brick_rows(be, bo, up, inner, f * 10 + p, 0, 3)
            to[5:8, :] = low
            to[24:27, :] = high
    for f in range(10):
        for p in range(8):
            to = near_to[f](p)
            to[8:24, :] = wide_plane(near[f], re, ro, even, inside, 15 + 2 * f, 2, p)
            low, high = brick_rows(be, bo, up, inner, 50 + f * 4 + p // 2, 2 * (p % 2), 2)
            to[6:8, :] = low
            to[24:26, :] = high

    def drift(p, carry):
        h = heat_x[p + 1]
        lane = lanes(h.shape)
        right = jnp.where(lane == 255, 0.0, pltpu.roll(h, 255, axis=1))
        left = jnp.where(lane == 0, 0.0, pltpu.roll(h, 1, axis=1))
        force_x[0, p] = force_x[0, p] - (heat_x[p + 2] - heat_x[p])
        force_x[1, p] = force_x[1, p] - (pltpu.roll(h, 31, axis=0) - pltpu.roll(h, 1, axis=0))
        force_x[2, p] = force_x[2, p] - (right - left)
        return carry

    lax.fori_loop(0, 8, drift, 0)
    smooth(v0, force_x, kinv_x, obst_x, v1, v2)

    shape = (16, 256)
    first = jnp.bitwise_and(lanes(shape), 1) == 0
    for q in range(2):
        low = None
        for p in (2 * q, 2 * q + 1):
            out = residual_plane(v2, force_x, main, cross, p)
            cut = clip[p] == 1
            out[0] = jnp.where(cut, 0.0, out[0])
            gap = jnp.logical_and(touch[p] == 1, clip[p] != 1)
            room = jnp.where(gap, clear[p] - v2[0, p + 1, 8:24, :], FREE)
            part = out + [room] + [main[c, p] for c in range(3)] + [cross[c, p] for c in range(3)]
            if low is None:
                low = part
            else:
                low = [jnp.minimum(x, y) if i == 3 else x + y for i, (x, y) in enumerate(zip(low, part))]
        for i in range(10):
            x = low[i]
            if i < 3:
                x = 0.25 * x
            elif i > 3:
                x = 0.125 * x
            for h in range(2):
                rest[i, h] = x[:, 128 * h : 128 * h + 128]
            halves = []
            for h in range(2):
                a, b = rest[i, h, pl.ds(0, 8, 2), :], rest[i, h, pl.ds(1, 8, 2), :]
                halves.append(jnp.minimum(a, b) if i == 3 else a + b)
            x = jnp.concatenate(halves, 1)
            if i == 3:
                x = jnp.minimum(x, pltpu.roll(x, 255, axis=1))
                x = jnp.where(first[0:8], x, 0.0)
            gath[(2 * i + q) * 8 : (2 * i + q) * 8 + 8, :] = x
    i, j = rows((256, 128)), lanes((256, 128))
    pick = jnp.where(lax.shift_right_logical(i, 1) == j, 1.0, 0.0)
    small = jnp.dot(gath[...], pick, precision=HIGH, preferred_element_type=F32)
    small = small.reshape(20, 8, 128)
    em[0:20] = small
    om[0:20] = small
    for p in range(4):
        for c in range(3):
            pre[c, p] = v2[c, p + 1, 8:24, :]
    for msg, at in ((em, 1 - par), (om, par)):
        for c in range(3):
            for k in range(3):
                t = 20 + (c * 3 + k) * 4
                x = v2[c, at + k + 1, 8:24, :]
                msg[t] = x[:8, :128]
                msg[t + 1] = x[:8, 128:]
                msg[t + 2] = x[8:, :128]
                msg[t + 3] = x[8:, 128:]


def pre_plane(pre, e, o, even, inside, c, p):
    def tile(msg, base, k):
        t = base + (c * 3 + k) * 4
        left = jnp.concatenate([msg[t], msg[t + 2]], 0)
        right = jnp.concatenate([msg[t + 1], msg[t + 3]], 0)
        return jnp.concatenate([left, right], 1)

    if p < 3:
        return jnp.where(even, jnp.where(inside, tile(o, 40, p), 0.0), tile(e, 20, p))
    if p < 7:
        return pre[c, p - 3]
    return jnp.where(even, tile(e, 20, p - 7), jnp.where(inside, tile(o, 40, p - 7), 0.0))


def pack_coarse(pos, pre, em, e, o, e2, o2, be, bo):
    even, inside = sides(pos[0])
    up = jnp.bitwise_and(pos[1], 1) == 0
    for msg in (be, bo):
        msg[0:20] = em[0:20]
        msg[20:40] = e[0:20]
        msg[40:80] = o[0:40]
        msg[80:120] = e2[...]
        msg[120:160] = o2[...]
    for c in range(3):
        for p in range(10):
            x = pre_plane(pre, e, o, even, inside, c, p)
            low, high = x[0:3], x[13:16]
            put(be, 160 + c * 10 + p, 0, jnp.where(up, high, low))
            put(bo, 160 + c * 10 + p, 0, jnp.where(up, low, high))


def pair_spread(x, op):
    n, m = x.shape
    even = jnp.bitwise_and(lanes(x.shape), 1) == 0
    x = op(x, jnp.where(even, pltpu.roll(x, m - 1, axis=1), pltpu.roll(x, 1, axis=1)))
    even = jnp.bitwise_and(rows(x.shape), 1) == 0
    return op(x, jnp.where(even, pltpu.roll(x, n - 1, axis=0), pltpu.roll(x, 1, axis=0)))


def coarse(pos, sent, be, bo, mid2, own, g, ki, va, vb, f3, k3, o3, l3):
    par = jnp.bitwise_and(pos[0], 1)
    up, inner = sides(pos[1])
    grp = pos[0]
    for s in range(8):
        place = jnp.where(par == 0, EVEN_SLOTS[s], 7 - EVEN_SLOTS[s])
        where = grp + place - jnp.where(par == 0, 4, 3)
        real = jnp.logical_and(where >= 0, where < 16)
        for f in range(10):
            for q in range(2):
                t = s * 20 + f * 2 + q
                a = jnp.where(real, be[t], 0.0)
                b = jnp.where(jnp.logical_and(real, inner), bo[t], 0.0)
                to = g.at[f, 2 * place + q]
                to[0:8, :] = jnp.where(up, b, a)
                to[8:16, :] = jnp.where(real, sent[t], 0.0)
                to[16:24, :] = jnp.where(up, a, b)

    def start(p, carry):
        inv = inverse(*[g[4 + k, p] for k in range(6)])
        for k in range(6):
            ki[k, p] = inv[k]
        v = symmetric_times(inv, [OMEGA * g[c, p] for c in range(3)])
        va[0, p] = jnp.minimum(v[0], g[3, p])
        va[1, p] = v[1]
        va[2, p] = v[2]
        return carry

    lax.fori_loop(0, 16, start, 0)

    def sweep(src, dst):
        def body(p, carry):
            rest = []
            for c in range(3):
                near = src[c, p - 1] + src[c, p + 1] + beside(src[c, p])
                rest.append(g[c, p] + near)
            step = symmetric_times([ki[k, p] for k in range(6)], rest)
            new = [KEEP * src[c, p] + OMEGA * step[c] for c in range(3)]
            dst[0, p] = jnp.minimum(new[0], g[3, p])
            dst[1, p] = new[1]
            dst[2, p] = new[2]
            return carry

        return body

    lax.fori_loop(1, 15, sweep(va, vb), 0)

    def third(q, carry):
        total = None
        for p in (2 * q, 2 * q + 1):
            mat = [g[4 + k, p] for k in range(6)]
            kv = symmetric_times(mat, [vb[c, p] for c in range(3)])
            part = []
            for c in range(3):
                near = vb[c, p - 1] + vb[c, p + 1] + beside(vb[c, p])
                part.append(g[c, p] - (kv[c] - near))
            part += mat + [g[3, p] - vb[0, p]]
            if total is None:
                total = part
            else:
                total = [jnp.minimum(x, y) if i == 9 else x + y for i, (x, y) in enumerate(zip(total, part))]
        force = [0.25 * pair_spread(total[c], jnp.add) for c in range(3)]
        mat = [0.125 * pair_spread(total[3 + k], jnp.add) for k in range(6)]
        room = pair_spread(total[9], jnp.minimum)
        inv = inverse(*mat)
        v = symmetric_times(inv, [OMEGA * x for x in force])
        v[0] = jnp.minimum(v[0], room)
        for c in range(3):
            f3[c, q] = force[c]
            l3[c, q] = v[c]
        for k in range(6):
            k3[k, q] = inv[k]
        o3[q] = room
        return carry

    lax.fori_loop(1, 7, third, 0)

    def lowest(q, carry):
        rest = []
        for c in range(3):
            near = l3[c, q - 1] + l3[c, q + 1] + beside(l3[c, q], 2)
            rest.append(f3[c, q] + near)
        step = symmetric_times([k3[k, q] for k in range(6)], rest)
        new = [KEEP * l3[c, q] + OMEGA * step[c] for c in range(3)]
        new[0] = jnp.minimum(new[0], o3[q])
        for c in range(3):
            for p in (2 * q, 2 * q + 1):
                va[c, p] = vb[c, p] + new[c]
        return carry

    lax.fori_loop(2, 6, lowest, 0)
    lax.fori_loop(5, 11, sweep(va, vb), 0)
    lax.fori_loop(6, 10, sweep(vb, va), 0)
    for c in range(3):
        for k in range(4):
            mid2[c, k] = va[c, 6 + k][4:20]
        for k in range(2):
            own[c, k] = va[c, 8 - 2 * par + k][4:20]


def finish(
    pos, pre, e, o, be, bo, mid2, other, force_x, kinv_x, obst_x, clip_x, main, cross,
    moved, residual, v0, v1, v2, mid_x, fine,
):
    par = jnp.bitwise_and(pos[0], 1)
    even, inside = sides(pos[0])
    up, inner = sides(pos[1])
    for c in range(3):
        for p in range(10):
            to = v0.at[c, p]
            to[8:24, :] = pre_plane(pre, e, o, even, inside, c, p)
            low, high = brick_rows(be, bo, up, inner, 160 + c * 10 + p, 0, 3)
            to[5:8, :] = low
            to[24:27, :] = high
    i, j = rows((128, 256)), lanes((128, 256))
    copy = jnp.where(lax.shift_right_logical(j, 1) == i, 1.0, 0.0)
    for c in range(3):
        mid_x[c, pl.ds(2 * par, 4)] = mid2[c]
        mid_x[c, pl.ds(4 * (1 - par), 2)] = other[c]
    wide = jnp.dot(
        mid_x[...].reshape(3 * 6 * 16, 128), copy, precision=HIGH, preferred_element_type=F32
    )
    for c in range(3):
        for k in range(6):
            x = wide[(c * 6 + k) * 16 : (c * 6 + k) * 16 + 16]
            for h in range(2):
                y = x[:, 128 * h : 128 * h + 128]
                fine[h, pl.ds(0, 16, 2), :] = y
                fine[h, pl.ds(1, 16, 2), :] = y
            up2 = jnp.concatenate([fine[0], fine[1]], 1)
            for p in range(10):
                if (p + 1) // 2 == k:
                    add = jnp.where(clip_x[p] == 1.0, 0.0, up2) if c == 0 else up2
                    v0[c, p] = v0[c, p] + add
    smooth(v0, force_x, kinv_x, obst_x, v1, v2)
    for p in range(4):
        out = residual_plane(v2, force_x, main, cross, p)
        for c in range(3):
            residual[c, p] = out[c]
            moved[c, p] = v2[c, p + 1, 8:24, :]


def call(kernel, outs, scratch, *args):
    vm = pl.BlockSpec(memory_space=pltpu.VMEM)
    return pl.pallas_call(
        kernel,
        out_shape=[jax.ShapeDtypeStruct(s, F32) for s in outs],
        in_specs=[pl.BlockSpec(memory_space=pltpu.SMEM)] + [vm] * (len(args) - 1),
        out_specs=[vm] * len(outs),
        scratch_shapes=[pltpu.VMEM(s, F32) for s in scratch],
        compiler_params=pltpu.CompilerParams(vmem_limit_bytes=32 * 1024 * 1024),
    )(*args)


EVEN = [(i, i ^ 1) for i in range(16)]
ODD = [(i, (((i + 1) ^ 1) - 1) % 16) for i in range(16)]


def swap_even(x, axis):
    return lax.ppermute(x, axis, EVEN)


def swap_odd(x, axis):
    return lax.ppermute(x, axis, ODD)


def local(disp, trac, heat, main, cross, clear, touch, clip):
    pos = jnp.stack([lax.axis_index("grp"), lax.axis_index("brick")]).astype(jnp.int32)
    own = (4, 16, 256)
    me, mo, kinv, obst = call(
        pack_grp, [(35, 16, 256), (35, 16, 256), (6,) + own, own], [],
        pos, disp, trac, heat, main, cross, clear, touch, clip,
    )
    re, ro = swap_even(me, "grp"), swap_odd(mo, "grp")
    be, bo = call(
        pack_brick, [(90, 8, 128)] * 2, [],
        pos, disp, heat, clip, trac, kinv, obst, re, ro,
    )
    re_b, ro_b = swap_even(be, "brick"), swap_odd(bo, "brick")
    force_x, kinv_x, obst_x, clip_x, pre, em, om = call(
        presmooth,
        [(3, 8, 32, 256), (6, 8, 32, 256), (8, 32, 256), (10, 32, 256), (3,) + own,
         (56, 8, 128), (56, 8, 128)],
        [(3, 10, 32, 256), (10, 32, 256), (3, 8, 32, 256), (3, 6, 32, 256),
         (10, 2, 16, 128), (160, 256)],
        pos, disp, heat, clip, trac, kinv, obst, main, cross, clear, touch, re, ro, re_b, ro_b,
    )
    e = swap_even(em, "grp")
    o = swap_odd(jnp.concatenate([om[:20], e[:20], om[20:]], 0), "grp")
    e2 = swap_even(o[:40], "grp")
    o2 = swap_odd(e2, "grp")
    ce, co = call(pack_coarse, [(190, 8, 128)] * 2, [], pos, pre, em, e, o, e2, o2)
    re_c, ro_c = swap_even(ce, "brick"), swap_odd(co, "brick")
    field = (3, 16, 24, 128)
    third = (3, 8, 24, 128)
    mid2, mine = call(
        coarse,
        [(3, 4, 16, 128), (3, 2, 16, 128)],
        [(10, 16, 24, 128), (6, 16, 24, 128), field, field, third, (6, 8, 24, 128),
         (8, 24, 128), third],
        pos, ce, re_c, ro_c,
    )
    other = swap_even(mine, "grp")
    return tuple(
        call(
            finish,
            [(3,) + own, (3,) + own],
            [(3, 10, 32, 256), (3, 8, 32, 256), (3, 6, 32, 256), (3, 6, 16, 128), (2, 32, 128)],
            pos, pre, e, o, re_c, ro_c, mid2, other, force_x, kinv_x, obst_x, clip_x, main, cross,
        )
    )


def solution(mesh):
    vector, scalar = P(None, "grp", "brick", None), P("grp", "brick", None)
    return jax.shard_map(
        local,
        mesh=mesh,
        in_specs=(vector, vector, scalar, vector, vector, scalar, scalar, scalar),
        out_specs=(vector, vector),
        check_vma=False,
    )
```

```python
import jax
import jax.numpy as jnp
from jax import lax
from jax.experimental import pallas as pl
from jax.experimental.pallas import tpu as pltpu
from jax.sharding import PartitionSpec as P

OMEGA = 0.6
KEEP = 0.4
FREE = 1000.0
F32 = jnp.float32
HIGH = lax.Precision.HIGHEST
EVEN_SLOTS = (4, 5, 3, 2, 6, 7, 1, 0)


def inverse(a, b, c, d, e, f):
    i00 = b * c - e * e
    i11 = a * c - f * f
    i22 = a * b - d * d
    i01 = f * e - d * c
    i12 = d * f - a * e
    i02 = d * e - b * f
    det = a * i00 + d * i01 + f * i02
    scale = jnp.where(det == 0.0, 0.0, 1.0 / jnp.where(det == 0.0, 1.0, det))
    return [i00 * scale, i11 * scale, i22 * scale, i01 * scale, i12 * scale, i02 * scale]


def symmetric_times(m, r):
    return [
        m[0] * r[0] + m[3] * r[1] + m[5] * r[2],
        m[3] * r[0] + m[1] * r[1] + m[4] * r[2],
        m[5] * r[0] + m[4] * r[1] + m[2] * r[2],
    ]


def lanes(shape):
    return lax.broadcasted_iota(jnp.int32, shape, 1)


def rows(shape):
    return lax.broadcasted_iota(jnp.int32, shape, 0)


def beside(x, step=1):
    n, m = x.shape
    lane = lanes(x.shape)
    left = jnp.where(lane < step, 0.0, pltpu.roll(x, step, axis=1))
    right = jnp.where(lane >= m - step, 0.0, pltpu.roll(x, m - step, axis=1))
    return (left + right) + (pltpu.roll(x, step, axis=0) + pltpu.roll(x, n - step, axis=0))


def sides(g):
    return (jnp.bitwise_and(g, 1) == 0), jnp.logical_and(g > 0, g < 15)


def put(msg, t, r, x):
    n = x.shape[0]
    msg[t, r : r + n, :] = x[:, :128]
    msg[t, r + 4 : r + 4 + n, :] = x[:, 128:]


def put_rows(be, bo, up, t, r, x, n, skip=0):
    low, high = x[skip : skip + n], x[16 - skip - n : 16 - skip]
    put(be, t, r, jnp.where(up, high, low))
    put(bo, t, r, jnp.where(up, low, high))


def get_rows(be, bo, up, inside, t, r, n):
    e = jnp.concatenate([be[t, r : r + n, :], be[t, r + 4 : r + 4 + n, :]], 1)
    o = jnp.concatenate([bo[t, r : r + n, :], bo[t, r + 4 : r + 4 + n, :]], 1)
    o = jnp.where(inside, o, 0.0)
    return jnp.where(up, o, e), jnp.where(up, e, o)


def fields(disp, heat, trac, kinv, obst):
    wide = [lambda p, c=c: disp[c, p] for c in range(3)]
    wide += [lambda p: heat[p]]
    near = [lambda p, c=c: trac[c, p] for c in range(3)]
    near += [lambda p, k=k: kinv[k, p] for k in range(6)]
    near += [lambda p: obst[p]]
    return wide, near


def load_pack(
    pos, disp_h, trac_h, heat_h, main_h, cross_h, clear_h, touch_h,
    kinv, obst, me, mo, be, bo,
    disp, trac, heat, main, cross, clear, touch, sem,
):
    pairs = [
        (main_h, main), (cross_h, cross), (clear_h, clear), (touch_h, touch),
        (disp_h, disp), (trac_h, trac), (heat_h, heat),
    ]
    copies = [pltpu.make_async_copy(x, y, sem.at[i]) for i, (x, y) in enumerate(pairs)]
    for c in copies:
        c.start()
    par = jnp.bitwise_and(pos[0], 1)
    up = jnp.bitwise_and(pos[1], 1) == 0
    copies[0].wait()
    copies[1].wait()

    def invert(p, carry):
        inv = inverse(main[0, p], main[1, p], main[2, p], cross[0, p], cross[1, p], cross[2, p])
        for k in range(6):
            kinv[k, p] = inv[k]
        return carry

    lax.fori_loop(0, 4, invert, 0)
    copies[2].wait()
    copies[3].wait()
    obst[...] = jnp.where(touch[...] == 1, clear[...], FREE)
    for c in copies[4:]:
        c.wait()
    for msg, at in ((me, 1 - par), (mo, par)):
        for c in range(3):
            msg[3 * c : 3 * c + 3] = disp[c, pl.ds(at, 3)]
        msg[9:12] = heat[pl.ds(at, 3)]
        for c in range(3):
            msg[12 + 2 * c : 14 + 2 * c] = trac[c, pl.ds(2 * at, 2)]
        for k in range(6):
            msg[18 + 2 * k : 20 + 2 * k] = kinv[k, pl.ds(2 * at, 2)]
        msg[30:32] = obst[pl.ds(2 * at, 2)]
    wide, near = fields(disp, heat, trac, kinv, obst)
    for f in range(4):
        for p in range(4):
            put_rows(be, bo, up, f * 4 + p, 0, wide[f](p), 3)
    for f in range(10):
        for p in range(4):
            put_rows(be, bo, up, 16 + f * 2 + p // 2, 2 * (p % 2), near[f](p), 2)


def halo_plane(re, ro, even, inside, low, k):
    e, o = re[k], jnp.where(inside, ro[k], 0.0)
    return jnp.where(even, o, e) if low else jnp.where(even, e, o)


def pack_corner(pos, re, ro, be, bo):
    even, inside = sides(pos[0])
    up = jnp.bitwise_and(pos[1], 1) == 0
    for f in range(4):
        for side in range(2):
            low = side == 0
            x = halo_plane(re, ro, even, inside, low, 3 * f + (2 if low else 0))
            put_rows(be, bo, up, f * 2 + side, 0, x, 2)
            x = halo_plane(re, ro, even, inside, low, 3 * f + 1)
            put_rows(be, bo, up, f * 2 + side, 2, x, 1)
    for f in range(10):
        for side in range(2):
            low = side == 0
            n = f * 2 + side
            x = halo_plane(re, ro, even, inside, low, 12 + 2 * f + (1 if low else 0))
            put_rows(be, bo, up, 8 + n // 4, n % 4, x, 1)


def smooth(v0, force, kinv, obst, v1, v2):
    def one(src, dst, shift, planes):
        def body(p, carry):
            rest = []
            for c in range(3):
                near = src[c, p] + src[c, p + 2] + beside(src[c, p + 1])
                rest.append(force[c, p + shift] + near)
            inv = [kinv[k, p + shift] for k in range(6)]
            step = symmetric_times(inv, rest)
            new = [KEEP * src[c, p + 1] + OMEGA * step[c] for c in range(3)]
            dst[0, p] = jnp.minimum(new[0], obst[p + shift])
            dst[1, p] = new[1]
            dst[2, p] = new[2]
            return carry

        lax.fori_loop(0, planes, body, 0)

    one(v0, v1, 0, 8)
    one(v1, v2, 1, 6)


def residual_plane(v2, force, main, cross, p):
    own = [v2[c, p + 1][8:24] for c in range(3)]
    mat = [main[c, p] for c in range(3)] + [cross[c, p] for c in range(3)]
    kv = symmetric_times(mat, own)
    out = []
    for c in range(3):
        near = v2[c, p, 8:24, :] + v2[c, p + 2, 8:24, :] + beside(v2[c, p + 1])[8:24]
        out.append(force[c, p + 2, 8:24, :] - (kv[c] - near))
    return out


def presmooth(
    pos, disp, heat, clip, trac, kinv, obst, main, cross, clear, touch,
    re, ro, be, bo, ce, co,
    force_x, kinv_x, obst_x, v2, small_out, planes_out, pe, po,
    v0, heat_x, v1, rest, gath,
):
    even, inside = sides(pos[0])
    up, inner = sides(pos[1])
    wide, near = fields(disp, heat, trac, kinv, obst)
    wide_to = [lambda p, c=c: v0.at[c, p] for c in range(3)]
    wide_to += [lambda p: heat_x.at[p]]
    near_to = [lambda p, c=c: force_x.at[c, p] for c in range(3)]
    near_to += [lambda p, k=k: kinv_x.at[k, p] for k in range(6)]
    near_to += [lambda p: obst_x.at[p]]
    for f in range(4):
        for p in range(4):
            to = wide_to[f](p + 3)
            to[8:24, :] = wide[f](p)
            to[5:8, :], to[24:27, :] = get_rows(be, bo, up, inner, f * 4 + p, 0, 3)
        for side in range(2):
            low = side == 0
            for k in range(3):
                to = wide_to[f](k if low else 7 + k)
                to[8:24, :] = halo_plane(re, ro, even, inside, low, 3 * f + k)
            to = wide_to[f](2 if low else 7)
            to[6:8, :], to[24:26, :] = get_rows(ce, co, up, inner, f * 2 + side, 0, 2)
            to = wide_to[f](1 if low else 8)
            to[7:8, :], to[24:25, :] = get_rows(ce, co, up, inner, f * 2 + side, 2, 1)
    for f in range(10):
        for p in range(4):
            to = near_to[f](p + 2)
            to[8:24, :] = near[f](p)
            to[6:8, :], to[24:26, :] = get_rows(be, bo, up, inner, 16 + f * 2 + p // 2, 2 * (p % 2), 2)
        for side in range(2):
            low = side == 0
            for k in range(2):
                to = near_to[f](k if low else 6 + k)
                to[8:24, :] = halo_plane(re, ro, even, inside, low, 12 + 2 * f + k)
            n = f * 2 + side
            to = near_to[f](1 if low else 6)
            to[7:8, :], to[24:25, :] = get_rows(ce, co, up, inner, 8 + n // 4, n % 4, 1)

    def drift(p, carry):
        h = heat_x[p + 1]
        lane = lanes(h.shape)
        right = jnp.where(lane == 255, 0.0, pltpu.roll(h, 255, axis=1))
        left = jnp.where(lane == 0, 0.0, pltpu.roll(h, 1, axis=1))
        force_x[0, p] = force_x[0, p] - (heat_x[p + 2] - heat_x[p])
        force_x[1, p] = force_x[1, p] - (pltpu.roll(h, 31, axis=0) - pltpu.roll(h, 1, axis=0))
        force_x[2, p] = force_x[2, p] - (right - left)
        return carry

    lax.fori_loop(0, 8, drift, 0)
    smooth(v0, force_x, kinv_x, obst_x, v1, v2)

    shape = (16, 256)
    first = jnp.bitwise_and(lanes(shape), 1) == 0
    for q in range(2):
        low = None
        for p in (2 * q, 2 * q + 1):
            out = residual_plane(v2, force_x, main, cross, p)
            cut = clip[p] == 1
            out[0] = jnp.where(cut, 0.0, out[0])
            gap = jnp.logical_and(touch[p] == 1, clip[p] != 1)
            room = jnp.where(gap, clear[p] - v2[0, p + 1, 8:24, :], FREE)
            part = out + [room] + [main[c, p] for c in range(3)] + [cross[c, p] for c in range(3)]
            if low is None:
                low = part
            else:
                low = [jnp.minimum(x, y) if i == 3 else x + y for i, (x, y) in enumerate(zip(low, part))]
        for i in range(10):
            x = low[i]
            if i < 3:
                x = 0.25 * x
            elif i > 3:
                x = 0.125 * x
            for h in range(2):
                rest[i, h] = x[:, 128 * h : 128 * h + 128]
            halves = []
            for h in range(2):
                a, b = rest[i, h, pl.ds(0, 8, 2), :], rest[i, h, pl.ds(1, 8, 2), :]
                halves.append(jnp.minimum(a, b) if i == 3 else a + b)
            x = jnp.concatenate(halves, 1)
            if i == 3:
                x = jnp.minimum(x, pltpu.roll(x, 255, axis=1))
                x = jnp.where(first[0:8], x, 0.0)
            gath[(2 * i + q) * 8 : (2 * i + q) * 8 + 8, :] = x
    i, j = rows((256, 128)), lanes((256, 128))
    pick = jnp.where(lax.shift_right_logical(i, 1) == j, 1.0, 0.0)
    small = jnp.dot(gath[...], pick, precision=HIGH, preferred_element_type=F32)
    small_out[...] = small.reshape(20, 8, 128)
    for c in range(3):
        for k in range(2):
            planes_out[2 * c + k] = v2[c, k + 2, 8:24, :]
    for p in range(4):
        planes_out[6 + p] = clip[p].astype(F32)
    for c in range(3):
        for p in range(4):
            put_rows(pe, po, up, c * 2 + p // 2, 2 * (p % 2), v2[c, p + 1, 8:24, :], 2, 1)
        for side in range(2):
            n = 2 * c + side
            put_rows(pe, po, up, 10 + n // 2, 2 * (n % 2), v2[c, 5 * side, 8:24, :], 2)
    for p in range(4):
        put_rows(pe, po, up, 6 + p, 0, clip[p].astype(F32), 3)


def pack_late(pos, ge, go, be, bo):
    even, inside = sides(pos[0])
    up = jnp.bitwise_and(pos[1], 1) == 0
    for side in range(2):
        low = side == 0
        for c in range(3):
            x = halo_plane(ge, go, even, inside, low, 2 * c + (1 if low else 0))
            put_rows(be, bo, up, side, c, x, 1)
        x = halo_plane(ge, go, even, inside, low, 6 + (3 if low else 0))
        put_rows(be, bo, up, 2 + side, 0, x, 2)
        x = halo_plane(ge, go, even, inside, low, 6 + (2 if low else 1))
        put_rows(be, bo, up, 2 + side, 2, x, 1)


def pair_spread(x, op):
    n, m = x.shape
    even = jnp.bitwise_and(lanes(x.shape), 1) == 0
    x = op(x, jnp.where(even, pltpu.roll(x, m - 1, axis=1), pltpu.roll(x, 1, axis=1)))
    even = jnp.bitwise_and(rows(x.shape), 1) == 0
    return op(x, jnp.where(even, pltpu.roll(x, n - 1, axis=0), pltpu.roll(x, 1, axis=0)))


def coarse(
    pos, b0, b1, b2, b3, b4, r1e, r1o, r2e, r2o, r3e, r3o,
    mid2, own, g, ki, va, vb, f3, k3, o3, l3,
):
    par = jnp.bitwise_and(pos[0], 1)
    up, inner = sides(pos[1])
    grp = pos[0]
    slots = [
        (b0, 0, r1e, r1o, 0), (b1, 0, r1e, r1o, 20), (b2, 0, r2e, r2o, 0), (b2, 20, r2e, r2o, 20),
        (b3, 0, r2e, r2o, 40), (b3, 20, r2e, r2o, 60), (b4, 0, r3e, r3o, 0), (b4, 20, r3e, r3o, 20),
    ]
    for s, (mine, m, re, ro, r) in enumerate(slots):
        place = jnp.where(par == 0, EVEN_SLOTS[s], 7 - EVEN_SLOTS[s])
        where = grp + place - jnp.where(par == 0, 4, 3)
        real = jnp.logical_and(where >= 0, where < 16)

        def fill(f, carry):
            for q in range(2):
                t = f * 2 + q
                a = jnp.where(real, re[r + t], 0.0)
                b = jnp.where(jnp.logical_and(real, inner), ro[r + t], 0.0)
                to = g.at[f, 2 * place + q]
                to[0:8, :] = jnp.where(up, b, a)
                to[8:16, :] = jnp.where(real, mine[m + t], 0.0)
                to[16:24, :] = jnp.where(up, a, b)
            return carry

        lax.fori_loop(0, 10, fill, 0)

    def start(p, carry):
        inv = inverse(*[g[4 + k, p] for k in range(6)])
        for k in range(6):
            ki[k, p] = inv[k]
        v = symmetric_times(inv, [OMEGA * g[c, p] for c in range(3)])
        va[0, p] = jnp.minimum(v[0], g[3, p])
        va[1, p] = v[1]
        va[2, p] = v[2]
        return carry

    lax.fori_loop(0, 16, start, 0)

    def sweep(src, dst):
        def body(p, carry):
            rest = []
            for c in range(3):
                near = src[c, p - 1] + src[c, p + 1] + beside(src[c, p])
                rest.append(g[c, p] + near)
            step = symmetric_times([ki[k, p] for k in range(6)], rest)
            new = [KEEP * src[c, p] + OMEGA * step[c] for c in range(3)]
            dst[0, p] = jnp.minimum(new[0], g[3, p])
            dst[1, p] = new[1]
            dst[2, p] = new[2]
            return carry

        return body

    lax.fori_loop(1, 15, sweep(va, vb), 0)

    def third(q, carry):
        total = None
        for p in (2 * q, 2 * q + 1):
            mat = [g[4 + k, p] for k in range(6)]
            kv = symmetric_times(mat, [vb[c, p] for c in range(3)])
            part = []
            for c in range(3):
                near = vb[c, p - 1] + vb[c, p + 1] + beside(vb[c, p])
                part.append(g[c, p] - (kv[c] - near))
            part += mat + [g[3, p] - vb[0, p]]
            if total is None:
                total = part
            else:
                total = [jnp.minimum(x, y) if i == 9 else x + y for i, (x, y) in enumerate(zip(total, part))]
        force = [0.25 * pair_spread(total[c], jnp.add) for c in range(3)]
        mat = [0.125 * pair_spread(total[3 + k], jnp.add) for k in range(6)]
        room = pair_spread(total[9], jnp.minimum)
        inv = inverse(*mat)
        v = symmetric_times(inv, [OMEGA * x for x in force])
        v[0] = jnp.minimum(v[0], room)
        for c in range(3):
            f3[c, q] = force[c]
            l3[c, q] = v[c]
        for k in range(6):
            k3[k, q] = inv[k]
        o3[q] = room
        return carry

    lax.fori_loop(1, 7, third, 0)

    def lowest(q, carry):
        rest = []
        for c in range(3):
            near = l3[c, q - 1] + l3[c, q + 1] + beside(l3[c, q], 2)
            rest.append(f3[c, q] + near)
        step = symmetric_times([k3[k, q] for k in range(6)], rest)
        new = [KEEP * l3[c, q] + OMEGA * step[c] for c in range(3)]
        new[0] = jnp.minimum(new[0], o3[q])
        for c in range(3):
            for p in (2 * q, 2 * q + 1):
                va[c, p] = vb[c, p] + new[c]
        return carry

    lax.fori_loop(2, 6, lowest, 0)
    lax.fori_loop(5, 11, sweep(va, vb), 0)
    lax.fori_loop(6, 10, sweep(vb, va), 0)
    for c in range(3):
        for k in range(4):
            mid2[c, k] = va[c, 6 + k][4:20]
        for k in range(2):
            own[c, k] = va[c, 8 - 2 * par + k][4:20]


def finish(
    pos, pre, ge, go, r1e, r1o, r3e, r3o, mid2, other, force_x, kinv_x, obst_x, clip, main, cross,
    moved, residual, v0, v1, v2, clip_x, mid_x, fine,
):
    par = jnp.bitwise_and(pos[0], 1)
    even, inside = sides(pos[0])
    up, inner = sides(pos[1])
    for c in range(3):
        for p in range(6):
            v0[c, p + 2] = pre[c, p]
        for p in range(4):
            to = v0.at[c, p + 3]
            to[5:7, :], to[25:27, :] = get_rows(r1e, r1o, up, inner, 40 + c * 2 + p // 2, 2 * (p % 2), 2)
        for side in range(2):
            low = side == 0
            n = 2 * c + side
            to = v0.at[c, 2 if low else 7]
            to[6:8, :], to[24:26, :] = get_rows(r1e, r1o, up, inner, 50 + n // 2, 2 * (n % 2), 2)
            for k in range(2):
                to = v0.at[c, k if low else 8 + k]
                to[8:24, :] = halo_plane(ge, go, even, inside, low, 2 * c + k)
            to = v0.at[c, 1 if low else 8]
            to[7:8, :], to[24:25, :] = get_rows(r3e, r3o, up, inner, 40 + side, c, 1)
    for p in range(4):
        to = clip_x.at[p + 3]
        to[8:24, :] = clip[p].astype(F32)
        to[5:8, :], to[24:27, :] = get_rows(r1e, r1o, up, inner, 46 + p, 0, 3)
    for side in range(2):
        low = side == 0
        for k in range(3):
            to = clip_x.at[k if low else 7 + k]
            to[8:24, :] = halo_plane(ge, go, even, inside, low, 6 + k + (1 if low else 0))
        to = clip_x.at[2 if low else 7]
        to[6:8, :], to[24:26, :] = get_rows(r3e, r3o, up, inner, 42 + side, 0, 2)
        to = clip_x.at[1 if low else 8]
        to[7:8, :], to[24:25, :] = get_rows(r3e, r3o, up, inner, 42 + side, 2, 1)
    i, j = rows((128, 256)), lanes((128, 256))
    copy = jnp.where(lax.shift_right_logical(j, 1) == i, 1.0, 0.0)
    for c in range(3):
        mid_x[c, pl.ds(2 * par, 4)] = mid2[c]
        mid_x[c, pl.ds(4 * (1 - par), 2)] = other[c]
    wide = jnp.dot(
        mid_x[...].reshape(3 * 6 * 16, 128), copy, precision=HIGH, preferred_element_type=F32
    )
    for c in range(3):
        for k in range(6):
            x = wide[(c * 6 + k) * 16 : (c * 6 + k) * 16 + 16]
            for h in range(2):
                y = x[:, 128 * h : 128 * h + 128]
                fine[h, pl.ds(0, 16, 2), :] = y
                fine[h, pl.ds(1, 16, 2), :] = y
            up2 = jnp.concatenate([fine[0], fine[1]], 1)
            for p in range(10):
                if (p + 1) // 2 == k:
                    add = jnp.where(clip_x[p] == 1.0, 0.0, up2) if c == 0 else up2
                    v0[c, p] = v0[c, p] + add
    smooth(v0, force_x, kinv_x, obst_x, v1, v2)
    for p in range(4):
        out = residual_plane(v2, force_x, main, cross, p)
        for c in range(3):
            residual[c, p] = out[c]
            moved[c, p] = v2[c, p + 1, 8:24, :]


def call(kernel, outs, scratch, *args, limit=0):
    vm = pl.BlockSpec(memory_space=pltpu.VMEM)
    source = pl.BlockSpec(memory_space=pltpu.HBM) if limit else vm
    return pl.pallas_call(
        kernel,
        out_shape=[jax.ShapeDtypeStruct(x, F32) for x in outs],
        in_specs=[pl.BlockSpec(memory_space=pltpu.SMEM)] + [source] * (len(args) - 1),
        out_specs=[vm] * len(outs),
        scratch_shapes=[pltpu.VMEM(x, F32) if isinstance(x, tuple) else x for x in scratch],
        compiler_params=pltpu.CompilerParams(vmem_limit_bytes=limit or 32 * 1024 * 1024),
    )(*args)


EVEN = [(i, i ^ 1) for i in range(16)]
ODD = [(i, (((i + 1) ^ 1) - 1) % 16) for i in range(16)]


def swap_even(x, axis):
    return lax.ppermute(x, axis, EVEN)


def swap_odd(x, axis):
    return lax.ppermute(x, axis, ODD)


def local(disp, trac, heat, main, cross, clear, touch, clip):
    pos = jnp.stack([lax.axis_index("grp"), lax.axis_index("brick")]).astype(jnp.int32)
    own, vec, six = (4, 16, 256), (3, 4, 16, 256), (6, 4, 16, 256)
    kinv, obst, me, mo, be, bo = call(
        load_pack,
        [six, own] + [(32, 16, 256)] * 2 + [(36, 8, 128)] * 2,
        [vec, vec, own, vec, vec, own, pltpu.VMEM(own, jnp.int32), pltpu.SemaphoreType.DMA((7,))],
        pos, disp, trac, heat, main, cross, clear, touch, limit=58 * 1024 * 1024,
    )
    re, ro = swap_even(me, "grp"), swap_odd(mo, "grp")
    re_b, ro_b = swap_even(be, "brick"), swap_odd(bo, "brick")
    ce, co = call(pack_corner, [(13, 8, 128)] * 2, [], pos, re, ro)
    re_c, ro_c = swap_even(ce, "brick"), swap_odd(co, "brick")
    force_x, kinv_x, obst_x, pre, b0, planes, pe, po = call(
        presmooth,
        [(3, 8, 32, 256), (6, 8, 32, 256), (8, 32, 256), (3, 6, 32, 256), (20, 8, 128),
         (10, 16, 256), (13, 8, 128), (13, 8, 128)],
        [(3, 10, 32, 256), (10, 32, 256), (3, 8, 32, 256), (10, 2, 16, 128), (160, 256)],
        pos, disp, heat, clip, trac, kinv, obst, main, cross, clear, touch,
        re, ro, re_b, ro_b, re_c, ro_c,
    )
    b1 = swap_even(b0, "grp")
    b2 = swap_odd(jnp.concatenate([b0, b1], 0), "grp")
    ge, go = swap_even(planes, "grp"), swap_odd(planes, "grp")
    r1e = swap_even(jnp.concatenate([b0, b1, pe], 0), "brick")
    r1o = swap_odd(jnp.concatenate([b0, b1, po], 0), "brick")
    b3 = swap_even(b2, "grp")
    second = jnp.concatenate([b2, b3], 0)
    r2e, r2o = swap_even(second, "brick"), swap_odd(second, "brick")
    b4 = swap_odd(b3, "grp")
    qe, qo = call(pack_late, [(4, 8, 128)] * 2, [], pos, ge, go)
    r3e = swap_even(jnp.concatenate([b4, qe], 0), "brick")
    r3o = swap_odd(jnp.concatenate([b4, qo], 0), "brick")
    field, third = (3, 16, 24, 128), (3, 8, 24, 128)
    mid2, mine = call(
        coarse,
        [(3, 4, 16, 128), (3, 2, 16, 128)],
        [(10, 16, 24, 128), (6, 16, 24, 128), field, field, third, (6, 8, 24, 128),
         (8, 24, 128), third],
        pos, b0, b1, b2, b3, b4, r1e, r1o, r2e, r2o, r3e, r3o,
    )
    other = swap_even(mine, "grp")
    return tuple(
        call(
            finish,
            [vec, vec],
            [(3, 10, 32, 256), (3, 8, 32, 256), (3, 6, 32, 256), (10, 32, 256), (3, 6, 16, 128),
             (2, 32, 128)],
            pos, pre, ge, go, r1e, r1o, r3e, r3o, mid2, other, force_x, kinv_x, obst_x, clip,
            main, cross,
        )
    )


def solution(mesh):
    vector, scalar = P(None, "grp", "brick", None), P("grp", "brick", None)
    return jax.shard_map(
        local,
        mesh=mesh,
        in_specs=(vector, vector, scalar, vector, vector, scalar, scalar, scalar),
        out_specs=(vector, vector),
        check_vma=False,
    )
```

```python
import jax
import jax.numpy as jnp
from jax import lax
from jax.experimental import pallas as pl
from jax.experimental.pallas import tpu as pltpu
from jax.sharding import PartitionSpec as P

OMEGA = 0.6
KEEP = 0.4
FREE = 1000.0
F32 = jnp.float32
HIGH = lax.Precision.HIGHEST
EVEN_SLOTS = (4, 5, 3, 2, 6, 7, 1, 0)


def inverse(a, b, c, d, e, f):
    i00 = b * c - e * e
    i11 = a * c - f * f
    i22 = a * b - d * d
    i01 = f * e - d * c
    i12 = d * f - a * e
    i02 = d * e - b * f
    det = a * i00 + d * i01 + f * i02
    scale = jnp.where(det == 0.0, 0.0, 1.0 / jnp.where(det == 0.0, 1.0, det))
    return [i00 * scale, i11 * scale, i22 * scale, i01 * scale, i12 * scale, i02 * scale]


def symmetric_times(m, r):
    return [
        m[0] * r[0] + m[3] * r[1] + m[5] * r[2],
        m[3] * r[0] + m[1] * r[1] + m[4] * r[2],
        m[5] * r[0] + m[4] * r[1] + m[2] * r[2],
    ]


def lanes(shape):
    return lax.broadcasted_iota(jnp.int32, shape, 1)


def rows(shape):
    return lax.broadcasted_iota(jnp.int32, shape, 0)


def beside(x, step=1):
    n, m = x.shape
    lane = lanes(x.shape)
    left = jnp.where(lane < step, 0.0, pltpu.roll(x, step, axis=1))
    right = jnp.where(lane >= m - step, 0.0, pltpu.roll(x, m - step, axis=1))
    return (left + right) + (pltpu.roll(x, step, axis=0) + pltpu.roll(x, n - step, axis=0))


def sides(g):
    return (jnp.bitwise_and(g, 1) == 0), jnp.logical_and(g > 0, g < 15)


def put(msg, t, r, x):
    n = x.shape[0]
    msg[t, r : r + n, :] = x[:, :128]
    msg[t, r + 4 : r + 4 + n, :] = x[:, 128:]


def put_rows(be, bo, up, t, r, x, n, skip=0):
    low, high = x[skip : skip + n], x[16 - skip - n : 16 - skip]
    put(be, t, r, jnp.where(up, high, low))
    put(bo, t, r, jnp.where(up, low, high))


def get_rows(be, bo, up, inside, t, r, n):
    e = jnp.concatenate([be[t, r : r + n, :], be[t, r + 4 : r + 4 + n, :]], 1)
    o = jnp.concatenate([bo[t, r : r + n, :], bo[t, r + 4 : r + 4 + n, :]], 1)
    o = jnp.where(inside, o, 0.0)
    return jnp.where(up, o, e), jnp.where(up, e, o)


def fields(disp, heat, trac, kinv, obst):
    wide = [lambda p, c=c: disp[c, p] for c in range(3)]
    wide += [lambda p: heat[p]]
    near = [lambda p, c=c: trac[c, p] for c in range(3)]
    near += [lambda p, k=k: kinv[k, p] for k in range(6)]
    near += [lambda p: obst[p]]
    return wide, near


def load_pack(
    pos, disp_h, trac_h, heat_h, main_h, cross_h, clear_h, touch_h,
    kinv, obst, me, mo, be, bo,
    disp, trac, heat, main, cross, clear, touch, sem,
):
    pairs = [
        (main_h, main), (cross_h, cross), (clear_h, clear), (touch_h, touch),
        (disp_h, disp), (trac_h, trac), (heat_h, heat),
    ]
    copies = [pltpu.make_async_copy(x, y, sem.at[i]) for i, (x, y) in enumerate(pairs)]
    for c in copies:
        c.start()
    par = jnp.bitwise_and(pos[0], 1)
    up = jnp.bitwise_and(pos[1], 1) == 0
    copies[0].wait()
    copies[1].wait()

    def invert(p, carry):
        inv = inverse(main[0, p], main[1, p], main[2, p], cross[0, p], cross[1, p], cross[2, p])
        for k in range(6):
            kinv[k, p] = inv[k]
        return carry

    lax.fori_loop(0, 4, invert, 0)
    copies[2].wait()
    copies[3].wait()
    obst[...] = jnp.where(touch[...] == 1, clear[...], FREE)
    for c in copies[4:]:
        c.wait()
    for msg, at in ((me, 1 - par), (mo, par)):
        for c in range(3):
            msg[3 * c : 3 * c + 3] = disp[c, pl.ds(at, 3)]
        msg[9:12] = heat[pl.ds(at, 3)]
        for c in range(3):
            msg[12 + 2 * c : 14 + 2 * c] = trac[c, pl.ds(2 * at, 2)]
        for k in range(6):
            msg[18 + 2 * k : 20 + 2 * k] = kinv[k, pl.ds(2 * at, 2)]
        msg[30:32] = obst[pl.ds(2 * at, 2)]
    wide, near = fields(disp, heat, trac, kinv, obst)
    for f in range(4):
        for p in range(4):
            put_rows(be, bo, up, f * 4 + p, 0, wide[f](p), 3)
    for f in range(10):
        for p in range(4):
            put_rows(be, bo, up, 16 + f * 2 + p // 2, 2 * (p % 2), near[f](p), 2)


def halo_plane(re, ro, even, inside, low, k):
    e, o = re[k], jnp.where(inside, ro[k], 0.0)
    return jnp.where(even, o, e) if low else jnp.where(even, e, o)


def pack_corner(pos, re, ro, be, bo):
    even, inside = sides(pos[0])
    up = jnp.bitwise_and(pos[1], 1) == 0
    for f in range(4):
        for side in range(2):
            low = side == 0
            x = halo_plane(re, ro, even, inside, low, 3 * f + (2 if low else 0))
            put_rows(be, bo, up, f * 2 + side, 0, x, 2)
            x = halo_plane(re, ro, even, inside, low, 3 * f + 1)
            put_rows(be, bo, up, f * 2 + side, 2, x, 1)
    for f in range(10):
        for side in range(2):
            low = side == 0
            n = f * 2 + side
            x = halo_plane(re, ro, even, inside, low, 12 + 2 * f + (1 if low else 0))
            put_rows(be, bo, up, 8 + n // 4, n % 4, x, 1)


def smooth(v0, force, kinv, obst, v1, v2):
    def one(src, dst, shift, planes):
        def body(p, carry):
            rest = []
            for c in range(3):
                near = src[c, p] + src[c, p + 2] + beside(src[c, p + 1])
                rest.append(force[c, p + shift] + near)
            inv = [kinv[k, p + shift] for k in range(6)]
            step = symmetric_times(inv, rest)
            new = [KEEP * src[c, p + 1] + OMEGA * step[c] for c in range(3)]
            dst[0, p] = jnp.minimum(new[0], obst[p + shift])
            dst[1, p] = new[1]
            dst[2, p] = new[2]
            return carry

        lax.fori_loop(0, planes, body, 0, unroll=4)

    one(v0, v1, 0, 8)
    one(v1, v2, 1, 6)


def residual_plane(v2, force, main, cross, p):
    own = [v2[c, p + 1][0:16] for c in range(3)]
    mat = [main[c, p] for c in range(3)] + [cross[c, p] for c in range(3)]
    kv = symmetric_times(mat, own)
    out = []
    for c in range(3):
        near = v2[c, p, 0:16, :] + v2[c, p + 2, 0:16, :] + beside(v2[c, p + 1])[0:16]
        out.append(force[c, p + 2, 0:16, :] - (kv[c] - near))
    return out


def presmooth(
    pos, disp, heat, clip, trac, kinv, obst, main, cross, clear, touch,
    re, ro, be, bo, ce, co,
    force_x, kinv_x, obst_x, v2, small_out, planes_out, pe, po,
    v0, heat_x, v1, rest, gath,
):
    even, inside = sides(pos[0])
    up, inner = sides(pos[1])
    wide, near = fields(disp, heat, trac, kinv, obst)
    wide_to = [lambda p, c=c: v0.at[c, p] for c in range(3)]
    wide_to += [lambda p: heat_x.at[p]]
    near_to = [lambda p, c=c: force_x.at[c, p] for c in range(3)]
    near_to += [lambda p, k=k: kinv_x.at[k, p] for k in range(6)]
    near_to += [lambda p: obst_x.at[p]]
    for f in range(4):
        for p in range(4):
            to = wide_to[f](p + 3)
            to[0:16, :] = wide[f](p)
            to[21:24, :], to[16:19, :] = get_rows(be, bo, up, inner, f * 4 + p, 0, 3)
        for side in range(2):
            low = side == 0
            for k in range(3):
                to = wide_to[f](k if low else 7 + k)
                to[0:16, :] = halo_plane(re, ro, even, inside, low, 3 * f + k)
            to = wide_to[f](2 if low else 7)
            to[22:24, :], to[16:18, :] = get_rows(ce, co, up, inner, f * 2 + side, 0, 2)
            to = wide_to[f](1 if low else 8)
            to[23:24, :], to[16:17, :] = get_rows(ce, co, up, inner, f * 2 + side, 2, 1)
    for f in range(10):
        for p in range(4):
            to = near_to[f](p + 2)
            to[0:16, :] = near[f](p)
            to[22:24, :], to[16:18, :] = get_rows(be, bo, up, inner, 16 + f * 2 + p // 2, 2 * (p % 2), 2)
        for side in range(2):
            low = side == 0
            for k in range(2):
                to = near_to[f](k if low else 6 + k)
                to[0:16, :] = halo_plane(re, ro, even, inside, low, 12 + 2 * f + k)
            n = f * 2 + side
            to = near_to[f](1 if low else 6)
            to[23:24, :], to[16:17, :] = get_rows(ce, co, up, inner, 8 + n // 4, n % 4, 1)

    def drift(p, carry):
        h = heat_x[p + 1]
        lane = lanes(h.shape)
        right = jnp.where(lane == 255, 0.0, pltpu.roll(h, 255, axis=1))
        left = jnp.where(lane == 0, 0.0, pltpu.roll(h, 1, axis=1))
        force_x[0, p] = force_x[0, p] - (heat_x[p + 2] - heat_x[p])
        force_x[1, p] = force_x[1, p] - (pltpu.roll(h, 23, axis=0) - pltpu.roll(h, 1, axis=0))
        force_x[2, p] = force_x[2, p] - (right - left)
        return carry

    lax.fori_loop(0, 8, drift, 0)
    smooth(v0, force_x, kinv_x, obst_x, v1, v2)

    shape = (16, 256)
    first = jnp.bitwise_and(lanes(shape), 1) == 0
    for q in range(2):
        low = None
        for p in (2 * q, 2 * q + 1):
            out = residual_plane(v2, force_x, main, cross, p)
            cut = clip[p] == 1
            out[0] = jnp.where(cut, 0.0, out[0])
            gap = jnp.logical_and(touch[p] == 1, clip[p] != 1)
            room = jnp.where(gap, clear[p] - v2[0, p + 1, 0:16, :], FREE)
            part = out + [room] + [main[c, p] for c in range(3)] + [cross[c, p] for c in range(3)]
            if low is None:
                low = part
            else:
                low = [jnp.minimum(x, y) if i == 3 else x + y for i, (x, y) in enumerate(zip(low, part))]
        for i in range(10):
            x = low[i]
            if i < 3:
                x = 0.25 * x
            elif i > 3:
                x = 0.125 * x
            for h in range(2):
                rest[i, h] = x[:, 128 * h : 128 * h + 128]
            halves = []
            for h in range(2):
                a, b = rest[i, h, pl.ds(0, 8, 2), :], rest[i, h, pl.ds(1, 8, 2), :]
                halves.append(jnp.minimum(a, b) if i == 3 else a + b)
            x = jnp.concatenate(halves, 1)
            if i == 3:
                x = jnp.minimum(x, pltpu.roll(x, 255, axis=1))
                x = jnp.where(first[0:8], x, 0.0)
            gath[(2 * i + q) * 8 : (2 * i + q) * 8 + 8, :] = x
    i, j = rows((256, 128)), lanes((256, 128))
    pick = jnp.where(lax.shift_right_logical(i, 1) == j, 1.0, 0.0)
    small = jnp.dot(gath[...], pick, precision=HIGH, preferred_element_type=F32)
    small_out[...] = small.reshape(20, 8, 128)
    for c in range(3):
        for k in range(2):
            planes_out[2 * c + k] = v2[c, k + 2, 0:16, :]
    for p in range(4):
        planes_out[6 + p] = clip[p].astype(F32)
    for c in range(3):
        for p in range(4):
            put_rows(pe, po, up, c * 2 + p // 2, 2 * (p % 2), v2[c, p + 1, 0:16, :], 2, 1)
        for side in range(2):
            n = 2 * c + side
            put_rows(pe, po, up, 10 + n // 2, 2 * (n % 2), v2[c, 5 * side, 0:16, :], 2)
    for p in range(4):
        put_rows(pe, po, up, 6 + p, 0, clip[p].astype(F32), 3)


def pack_late(pos, ge, go, be, bo):
    even, inside = sides(pos[0])
    up = jnp.bitwise_and(pos[1], 1) == 0
    for side in range(2):
        low = side == 0
        for c in range(3):
            x = halo_plane(ge, go, even, inside, low, 2 * c + (1 if low else 0))
            put_rows(be, bo, up, side, c, x, 1)
        x = halo_plane(ge, go, even, inside, low, 6 + (3 if low else 0))
        put_rows(be, bo, up, 2 + side, 0, x, 2)
        x = halo_plane(ge, go, even, inside, low, 6 + (2 if low else 1))
        put_rows(be, bo, up, 2 + side, 2, x, 1)


def pair_spread(x, op):
    n, m = x.shape
    even = jnp.bitwise_and(lanes(x.shape), 1) == 0
    x = op(x, jnp.where(even, pltpu.roll(x, m - 1, axis=1), pltpu.roll(x, 1, axis=1)))
    even = jnp.bitwise_and(rows(x.shape), 1) == 0
    return op(x, jnp.where(even, pltpu.roll(x, n - 1, axis=0), pltpu.roll(x, 1, axis=0)))


def coarse(
    pos, b0, b1, b2, b3, b4, r1e, r1o, r2e, r2o, r3e, r3o,
    mid2, own, g, ki, va, vb, f3, k3, o3, l3,
):
    par = jnp.bitwise_and(pos[0], 1)
    up, inner = sides(pos[1])
    grp = pos[0]
    slots = [
        (b0, 0, r1e, r1o, 0), (b1, 0, r1e, r1o, 20), (b2, 0, r2e, r2o, 0), (b2, 20, r2e, r2o, 20),
        (b3, 0, r2e, r2o, 40), (b3, 20, r2e, r2o, 60), (b4, 0, r3e, r3o, 0), (b4, 20, r3e, r3o, 20),
    ]
    for s, (mine, m, re, ro, r) in enumerate(slots):
        place = jnp.where(par == 0, EVEN_SLOTS[s], 7 - EVEN_SLOTS[s])
        where = grp + place - jnp.where(par == 0, 4, 3)
        real = jnp.logical_and(where >= 0, where < 16)

        def fill(f, carry):
            for q in range(2):
                t = f * 2 + q
                a = jnp.where(real, re[r + t], 0.0)
                b = jnp.where(jnp.logical_and(real, inner), ro[r + t], 0.0)
                to = g.at[f, 2 * place + q]
                to[0:8, :] = jnp.where(real, mine[m + t], 0.0)
                to[8:16, :] = jnp.where(up, a, b)
                to[16:24, :] = jnp.where(up, b, a)
            return carry

        lax.fori_loop(0, 10, fill, 0, unroll=2)

    def start(p, carry):
        inv = inverse(*[g[4 + k, p] for k in range(6)])
        for k in range(6):
            ki[k, p] = inv[k]
        v = symmetric_times(inv, [OMEGA * g[c, p] for c in range(3)])
        va[0, p] = jnp.minimum(v[0], g[3, p])
        va[1, p] = v[1]
        va[2, p] = v[2]
        return carry

    lax.fori_loop(0, 16, start, 0, unroll=4)

    def sweep(src, dst):
        def body(p, carry):
            rest = []
            for c in range(3):
                near = src[c, p - 1] + src[c, p + 1] + beside(src[c, p])
                rest.append(g[c, p] + near)
            step = symmetric_times([ki[k, p] for k in range(6)], rest)
            new = [KEEP * src[c, p] + OMEGA * step[c] for c in range(3)]
            dst[0, p] = jnp.minimum(new[0], g[3, p])
            dst[1, p] = new[1]
            dst[2, p] = new[2]
            return carry

        return body

    lax.fori_loop(1, 15, sweep(va, vb), 0, unroll=4)

    def third(q, carry):
        total = None
        for p in (2 * q, 2 * q + 1):
            mat = [g[4 + k, p] for k in range(6)]
            kv = symmetric_times(mat, [vb[c, p] for c in range(3)])
            part = []
            for c in range(3):
                near = vb[c, p - 1] + vb[c, p + 1] + beside(vb[c, p])
                part.append(g[c, p] - (kv[c] - near))
            part += mat + [g[3, p] - vb[0, p]]
            if total is None:
                total = part
            else:
                total = [jnp.minimum(x, y) if i == 9 else x + y for i, (x, y) in enumerate(zip(total, part))]
        force = [0.25 * pair_spread(total[c], jnp.add) for c in range(3)]
        mat = [0.125 * pair_spread(total[3 + k], jnp.add) for k in range(6)]
        room = pair_spread(total[9], jnp.minimum)
        inv = inverse(*mat)
        v = symmetric_times(inv, [OMEGA * x for x in force])
        v[0] = jnp.minimum(v[0], room)
        for c in range(3):
            f3[c, q] = force[c]
            l3[c, q] = v[c]
        for k in range(6):
            k3[k, q] = inv[k]
        o3[q] = room
        return carry

    lax.fori_loop(1, 7, third, 0, unroll=4)

    def lowest(q, carry):
        rest = []
        for c in range(3):
            near = l3[c, q - 1] + l3[c, q + 1] + beside(l3[c, q], 2)
            rest.append(f3[c, q] + near)
        step = symmetric_times([k3[k, q] for k in range(6)], rest)
        new = [KEEP * l3[c, q] + OMEGA * step[c] for c in range(3)]
        new[0] = jnp.minimum(new[0], o3[q])
        for c in range(3):
            for p in (2 * q, 2 * q + 1):
                va[c, p] = vb[c, p] + new[c]
        return carry

    lax.fori_loop(2, 6, lowest, 0, unroll=4)
    lax.fori_loop(5, 11, sweep(va, vb), 0, unroll=4)
    lax.fori_loop(6, 10, sweep(vb, va), 0, unroll=4)
    for c in range(3):
        for k in range(4):
            mid2[c, k, 0:10, :] = va[c, 6 + k, 0:10, :]
            mid2[c, k, 10:12, :] = va[c, 6 + k, 22:24, :]
        for k in range(2):
            own[c, k, 0:10, :] = va[c, 8 - 2 * par + k, 0:10, :]
            own[c, k, 10:12, :] = va[c, 8 - 2 * par + k, 22:24, :]


def finish(
    pos, pre, ge, go, r1e, r1o, r3e, r3o, mid2, other, force_x, kinv_x, obst_x, clip, main, cross,
    moved, residual, v0, v1, v2, clip_x, mid_x, fine,
):
    par = jnp.bitwise_and(pos[0], 1)
    even, inside = sides(pos[0])
    up, inner = sides(pos[1])
    for c in range(3):
        for p in range(6):
            v0[c, p + 2] = pre[c, p]
        for p in range(4):
            to = v0.at[c, p + 3]
            to[21:23, :], to[17:19, :] = get_rows(r1e, r1o, up, inner, 40 + c * 2 + p // 2, 2 * (p % 2), 2)
        for side in range(2):
            low = side == 0
            n = 2 * c + side
            to = v0.at[c, 2 if low else 7]
            to[22:24, :], to[16:18, :] = get_rows(r1e, r1o, up, inner, 50 + n // 2, 2 * (n % 2), 2)
            for k in range(2):
                to = v0.at[c, k if low else 8 + k]
                to[0:16, :] = halo_plane(ge, go, even, inside, low, 2 * c + k)
            to = v0.at[c, 1 if low else 8]
            to[23:24, :], to[16:17, :] = get_rows(r3e, r3o, up, inner, 40 + side, c, 1)
    for p in range(4):
        to = clip_x.at[p + 3]
        to[0:16, :] = clip[p].astype(F32)
        to[21:24, :], to[16:19, :] = get_rows(r1e, r1o, up, inner, 46 + p, 0, 3)
    for side in range(2):
        low = side == 0
        for k in range(3):
            to = clip_x.at[k if low else 7 + k]
            to[0:16, :] = halo_plane(ge, go, even, inside, low, 6 + k + (1 if low else 0))
        to = clip_x.at[2 if low else 7]
        to[22:24, :], to[16:18, :] = get_rows(r3e, r3o, up, inner, 42 + side, 0, 2)
        to = clip_x.at[1 if low else 8]
        to[23:24, :], to[16:17, :] = get_rows(r3e, r3o, up, inner, 42 + side, 2, 1)
    i, j = rows((128, 256)), lanes((128, 256))
    copy = jnp.where(lax.shift_right_logical(j, 1) == i, 1.0, 0.0)
    for c in range(3):
        mid_x[c, pl.ds(2 * par, 4)] = mid2[c]
        mid_x[c, pl.ds(4 * (1 - par), 2)] = other[c]
    wide = jnp.dot(
        mid_x[...].reshape(3 * 6 * 16, 128), copy, precision=HIGH, preferred_element_type=F32
    )
    for c in range(3):
        for k in range(6):
            x = wide[(c * 6 + k) * 16 : (c * 6 + k) * 16 + 16]
            for h in range(2):
                y = x[:, 128 * h : 128 * h + 128]
                fine[h, pl.ds(0, 16, 2), :] = y
                fine[h, pl.ds(1, 16, 2), :] = y
            up2 = jnp.concatenate([fine[0, 0:24, :], fine[1, 0:24, :]], 1)
            for p in range(10):
                if (p + 1) // 2 == k:
                    add = jnp.where(clip_x[p] == 1.0, 0.0, up2) if c == 0 else up2
                    v0[c, p] = v0[c, p] + add
    smooth(v0, force_x, kinv_x, obst_x, v1, v2)
    for p in range(4):
        out = residual_plane(v2, force_x, main, cross, p)
        for c in range(3):
            residual[c, p] = out[c]
            moved[c, p] = v2[c, p + 1, 0:16, :]


def call(kernel, outs, scratch, *args, limit=0):
    vm = pl.BlockSpec(memory_space=pltpu.VMEM)
    source = pl.BlockSpec(memory_space=pltpu.HBM) if limit else vm
    return pl.pallas_call(
        kernel,
        out_shape=[jax.ShapeDtypeStruct(x, F32) for x in outs],
        in_specs=[pl.BlockSpec(memory_space=pltpu.SMEM)] + [source] * (len(args) - 1),
        out_specs=[vm] * len(outs),
        scratch_shapes=[pltpu.VMEM(x, F32) if isinstance(x, tuple) else x for x in scratch],
        compiler_params=pltpu.CompilerParams(vmem_limit_bytes=limit or 32 * 1024 * 1024),
    )(*args)


EVEN = [(i, i ^ 1) for i in range(16)]
ODD = [(i, (((i + 1) ^ 1) - 1) % 16) for i in range(16)]


def swap_even(x, axis):
    return lax.ppermute(x, axis, EVEN)


def swap_odd(x, axis):
    return lax.ppermute(x, axis, ODD)


def local(disp, trac, heat, main, cross, clear, touch, clip):
    pos = jnp.stack([lax.axis_index("grp"), lax.axis_index("brick")]).astype(jnp.int32)
    own, vec, six = (4, 16, 256), (3, 4, 16, 256), (6, 4, 16, 256)
    kinv, obst, me, mo, be, bo = call(
        load_pack,
        [six, own] + [(32, 16, 256)] * 2 + [(36, 8, 128)] * 2,
        [vec, vec, own, vec, vec, own, pltpu.VMEM(own, jnp.int32), pltpu.SemaphoreType.DMA((7,))],
        pos, *[pltpu.with_memory_space_constraint(z, pltpu.HBM) for z in (disp, trac, heat, main, cross, clear, touch)], limit=32 * 1024 * 1024,
    )
    re, ro = swap_even(me, "grp"), swap_odd(mo, "grp")
    re_b, ro_b = swap_even(be, "brick"), swap_odd(bo, "brick")
    ce, co = call(pack_corner, [(13, 8, 128)] * 2, [], pos, re, ro)
    re_c, ro_c = swap_even(ce, "brick"), swap_odd(co, "brick")
    force_x, kinv_x, obst_x, pre, b0, planes, pe, po = call(
        presmooth,
        [(3, 8, 24, 256), (6, 8, 24, 256), (8, 24, 256), (3, 6, 24, 256), (20, 8, 128),
         (10, 16, 256), (13, 8, 128), (13, 8, 128)],
        [(3, 10, 24, 256), (10, 24, 256), (3, 8, 24, 256), (10, 2, 16, 128), (160, 256)],
        pos, disp, heat, clip, trac, kinv, obst, main, cross, clear, touch,
        re, ro, re_b, ro_b, re_c, ro_c,
    )
    b1 = swap_even(b0, "grp")
    b2 = swap_odd(jnp.concatenate([b0, b1], 0), "grp")
    ge, go = swap_even(planes, "grp"), swap_odd(planes, "grp")
    r1e = swap_even(jnp.concatenate([b0, b1, pe], 0), "brick")
    r1o = swap_odd(jnp.concatenate([b0, b1, po], 0), "brick")
    b3 = swap_even(b2, "grp")
    second = jnp.concatenate([b2, b3], 0)
    r2e, r2o = swap_even(second, "brick"), swap_odd(second, "brick")
    b4 = swap_odd(b3, "grp")
    qe, qo = call(pack_late, [(4, 8, 128)] * 2, [], pos, ge, go)
    r3e = swap_even(jnp.concatenate([b4, qe], 0), "brick")
    r3o = swap_odd(jnp.concatenate([b4, qo], 0), "brick")
    field, third = (3, 16, 24, 128), (3, 8, 24, 128)
    mid2, mine = call(
        coarse,
        [(3, 4, 16, 128), (3, 2, 16, 128)],
        [(10, 16, 24, 128), (6, 16, 24, 128), field, field, third, (6, 8, 24, 128),
         (8, 24, 128), third],
        pos, b0, b1, b2, b3, b4, r1e, r1o, r2e, r2o, r3e, r3o,
    )
    other = swap_even(mine, "grp")
    return tuple(
        call(
            finish,
            [vec, vec],
            [(3, 10, 24, 256), (3, 8, 24, 256), (3, 6, 24, 256), (10, 24, 256), (3, 6, 16, 128),
             (2, 32, 128)],
            pos, pre, ge, go, r1e, r1o, r3e, r3o, mid2, other, force_x, kinv_x, obst_x, clip,
            main, cross,
        )
    )


def solution(mesh):
    vector, scalar = P(None, "grp", "brick", None), P("grp", "brick", None)
    return jax.shard_map(
        local,
        mesh=mesh,
        in_specs=(vector, vector, scalar, vector, vector, scalar, scalar, scalar),
        out_specs=(vector, vector),
        check_vma=False,
    )
```

```python
import jax
import jax.numpy as jnp
from jax import lax
from jax.experimental import pallas as pl
from jax.experimental.pallas import tpu as pltpu
from jax.sharding import PartitionSpec as P

OMEGA = 0.6
KEEP = 0.4
FREE = 1000.0
F32 = jnp.float32
HIGH = lax.Precision.HIGHEST
EVEN_SLOTS = (4, 5, 3, 2, 6, 7, 1, 0)


def inverse(a, b, c, d, e, f):
    i00 = b * c - e * e
    i11 = a * c - f * f
    i22 = a * b - d * d
    i01 = f * e - d * c
    i12 = d * f - a * e
    i02 = d * e - b * f
    det = a * i00 + d * i01 + f * i02
    scale = jnp.where(det == 0.0, 0.0, 1.0 / jnp.where(det == 0.0, 1.0, det))
    return [i00 * scale, i11 * scale, i22 * scale, i01 * scale, i12 * scale, i02 * scale]


def symmetric_times(m, r):
    return [
        m[0] * r[0] + m[3] * r[1] + m[5] * r[2],
        m[3] * r[0] + m[1] * r[1] + m[4] * r[2],
        m[5] * r[0] + m[4] * r[1] + m[2] * r[2],
    ]


def lanes(shape):
    return lax.broadcasted_iota(jnp.int32, shape, 1)


def rows(shape):
    return lax.broadcasted_iota(jnp.int32, shape, 0)


def beside(x, step=1):
    n, m = x.shape
    lane = lanes(x.shape)
    left = jnp.where(lane < step, 0.0, pltpu.roll(x, step, axis=1))
    right = jnp.where(lane >= m - step, 0.0, pltpu.roll(x, m - step, axis=1))
    return (left + right) + (pltpu.roll(x, step, axis=0) + pltpu.roll(x, n - step, axis=0))


def sides(g):
    return (jnp.bitwise_and(g, 1) == 0), jnp.logical_and(g > 0, g < 15)


def put(msg, t, r, x):
    n = x.shape[0]
    msg[t, r : r + n, :] = x[:, :128]
    msg[t, r + 4 : r + 4 + n, :] = x[:, 128:]


def put_rows(be, bo, up, t, r, x, n, skip=0):
    low, high = x[skip : skip + n], x[16 - skip - n : 16 - skip]
    put(be, t, r, jnp.where(up, high, low))
    put(bo, t, r, jnp.where(up, low, high))


def get_rows(be, bo, up, inside, t, r, n):
    e = jnp.concatenate([be[t, r : r + n, :], be[t, r + 4 : r + 4 + n, :]], 1)
    o = jnp.concatenate([bo[t, r : r + n, :], bo[t, r + 4 : r + 4 + n, :]], 1)
    o = jnp.where(inside, o, 0.0)
    return jnp.where(up, o, e), jnp.where(up, e, o)


def fields(disp, heat, trac, kinv, obst):
    wide = [lambda p, c=c: disp[c, p] for c in range(3)]
    wide += [lambda p: heat[p]]
    near = [lambda p, c=c: trac[c, p] for c in range(3)]
    near += [lambda p, k=k: kinv[k, p] for k in range(6)]
    near += [lambda p: obst[p]]
    return wide, near


def load_pack(
    pos, disp_h, trac_h, heat_h, main_h, cross_h, clear_h, touch_h, clip_h,
    kinv, obst, me, mo, be, bo, k0,
    disp, trac, heat, main, cross, clear, touch, clip, rest, gath, sem,
):
    pairs = [
        (main_h, main), (cross_h, cross), (clear_h, clear), (touch_h, touch),
        (disp_h, disp), (trac_h, trac), (heat_h, heat), (clip_h, clip),
    ]
    copies = [pltpu.make_async_copy(x, y, sem.at[i]) for i, (x, y) in enumerate(pairs)]
    for c in copies:
        c.start()
    par = jnp.bitwise_and(pos[0], 1)
    up = jnp.bitwise_and(pos[1], 1) == 0
    copies[0].wait()
    copies[1].wait()

    def invert(p, carry):
        inv = inverse(main[0, p], main[1, p], main[2, p], cross[0, p], cross[1, p], cross[2, p])
        for k in range(6):
            kinv[k, p] = inv[k]
        return carry

    lax.fori_loop(0, 4, invert, 0)
    for k in range(6):
        src, c = (main, k) if k < 3 else (cross, k - 3)
        for q in range(2):
            x = 0.125 * (src[c, 2 * q] + src[c, 2 * q + 1])
            gath[(2 * k + q) * 8 : (2 * k + q) * 8 + 8, :] = pair_rows(rest.at[2 * k + q], x, jnp.add)
    k0[...] = pair_lanes(gath[...]).reshape(12, 8, 128)
    copies[2].wait()
    copies[3].wait()
    obst[...] = jnp.where(touch[...] == 1, clear[...], FREE)
    for c in copies[4:]:
        c.wait()
    for msg, at in ((me, 1 - par), (mo, par)):
        for c in range(3):
            msg[3 * c : 3 * c + 3] = disp[c, pl.ds(at, 3)]
        msg[9:12] = heat[pl.ds(at, 3)]
        for c in range(3):
            msg[12 + 2 * c : 14 + 2 * c] = trac[c, pl.ds(2 * at, 2)]
        for k in range(6):
            msg[18 + 2 * k : 20 + 2 * k] = kinv[k, pl.ds(2 * at, 2)]
        msg[30:32] = obst[pl.ds(2 * at, 2)]
    for t in range(12):
        r, h = 8 * (t % 4 // 2), 128 * (t % 2)
        me[32 + t // 4, r : r + 8, h : h + 128] = k0[t]
    wide, near = fields(disp, heat, trac, kinv, obst)
    for f in range(4):
        for p in range(4):
            put_rows(be, bo, up, f * 4 + p, 0, wide[f](p), 3)
    for f in range(10):
        for p in range(4):
            put_rows(be, bo, up, 16 + f * 2 + p // 2, 2 * (p % 2), near[f](p), 2)
    for p in range(4):
        put_rows(be, bo, up, 36 + p, 0, clip[p].astype(F32), 3)


def halo_plane(re, ro, even, inside, low, k):
    e, o = re[k], jnp.where(inside, ro[k], 0.0)
    return jnp.where(even, o, e) if low else jnp.where(even, e, o)


def pack_corner(pos, re, ro, k0, be, bo, k01):
    k01[0:12] = k0[...]
    for t in range(12):
        r, h = 8 * (t % 4 // 2), 128 * (t % 2)
        k01[12 + t] = re[32 + t // 4, r : r + 8, h : h + 128]
    even, inside = sides(pos[0])
    up = jnp.bitwise_and(pos[1], 1) == 0
    for f in range(4):
        for side in range(2):
            low = side == 0
            x = halo_plane(re, ro, even, inside, low, 3 * f + (2 if low else 0))
            put_rows(be, bo, up, f * 2 + side, 0, x, 2)
            x = halo_plane(re, ro, even, inside, low, 3 * f + 1)
            put_rows(be, bo, up, f * 2 + side, 2, x, 1)
    for f in range(10):
        for side in range(2):
            low = side == 0
            n = f * 2 + side
            x = halo_plane(re, ro, even, inside, low, 12 + 2 * f + (1 if low else 0))
            put_rows(be, bo, up, 8 + n // 4, n % 4, x, 1)


def smooth(v0, force, kinv, obst, v1, v2):
    def one(src, dst, shift, planes):
        def body(p, carry):
            rest = []
            for c in range(3):
                near = src[c, p] + src[c, p + 2] + beside(src[c, p + 1])
                rest.append(force[c, p + shift] + near)
            inv = [kinv[k, p + shift] for k in range(6)]
            step = symmetric_times(inv, rest)
            new = [KEEP * src[c, p + 1] + OMEGA * step[c] for c in range(3)]
            dst[0, p] = jnp.minimum(new[0], obst[p + shift])
            dst[1, p] = new[1]
            dst[2, p] = new[2]
            return carry

        lax.fori_loop(0, planes, body, 0, unroll=4)

    one(v0, v1, 0, 8)
    one(v1, v2, 1, 6)


def residual_plane(v2, force, main, cross, p):
    own = [v2[c, p + 1][0:16] for c in range(3)]
    mat = [main[c, p] for c in range(3)] + [cross[c, p] for c in range(3)]
    kv = symmetric_times(mat, own)
    out = []
    for c in range(3):
        near = v2[c, p, 0:16, :] + v2[c, p + 2, 0:16, :] + beside(v2[c, p + 1])[0:16]
        out.append(force[c, p + 2, 0:16, :] - (kv[c] - near))
    return out


def pair_rows(room, x, op):
    for h in range(2):
        room[h] = x[:, 128 * h : 128 * h + 128]
    return jnp.concatenate(
        [op(room[h, pl.ds(0, 8, 2), :], room[h, pl.ds(1, 8, 2), :]) for h in range(2)], 1
    )


def pair_lanes(x):
    i, j = rows((256, 128)), lanes((256, 128))
    pick = jnp.where(lax.shift_right_logical(i, 1) == j, 1.0, 0.0)
    return jnp.dot(x, pick, precision=HIGH, preferred_element_type=F32)


def put_extra(planes, n, x):
    planes[10 + n // 16, n % 16 : n % 16 + x.shape[0], :] = x


def get_extra(ge, go, even, inside, low, n, m):
    e = ge[10 + n // 16, n % 16 : n % 16 + m, :]
    o = jnp.where(inside, go[10 + n // 16, n % 16 : n % 16 + m, :], 0.0)
    return jnp.where(even, o, e) if low else jnp.where(even, e, o)


def presmooth(
    pos, disp, heat, clip, trac, kinv, obst, main, cross, clear, touch,
    re, ro, be, bo, ce, co,
    force_x, kinv_x, obst_x, v2, small_out, planes_out, pe, po,
    v0, heat_x, v1, rest, gath,
):
    even, inside = sides(pos[0])
    up, inner = sides(pos[1])
    wide, near = fields(disp, heat, trac, kinv, obst)
    wide_to = [lambda p, c=c: v0.at[c, p] for c in range(3)]
    wide_to += [lambda p: heat_x.at[p]]
    near_to = [lambda p, c=c: force_x.at[c, p] for c in range(3)]
    near_to += [lambda p, k=k: kinv_x.at[k, p] for k in range(6)]
    near_to += [lambda p: obst_x.at[p]]
    for f in range(4):
        for p in range(4):
            to = wide_to[f](p + 3)
            to[0:16, :] = wide[f](p)
            to[21:24, :], to[16:19, :] = get_rows(be, bo, up, inner, f * 4 + p, 0, 3)
        for side in range(2):
            low = side == 0
            for k in range(3):
                to = wide_to[f](k if low else 7 + k)
                to[0:16, :] = halo_plane(re, ro, even, inside, low, 3 * f + k)
            to = wide_to[f](2 if low else 7)
            to[22:24, :], to[16:18, :] = get_rows(ce, co, up, inner, f * 2 + side, 0, 2)
            to = wide_to[f](1 if low else 8)
            to[23:24, :], to[16:17, :] = get_rows(ce, co, up, inner, f * 2 + side, 2, 1)
    for f in range(10):
        for p in range(4):
            to = near_to[f](p + 2)
            to[0:16, :] = near[f](p)
            to[22:24, :], to[16:18, :] = get_rows(be, bo, up, inner, 16 + f * 2 + p // 2, 2 * (p % 2), 2)
        for side in range(2):
            low = side == 0
            for k in range(2):
                to = near_to[f](k if low else 6 + k)
                to[0:16, :] = halo_plane(re, ro, even, inside, low, 12 + 2 * f + k)
            n = f * 2 + side
            to = near_to[f](1 if low else 6)
            to[23:24, :], to[16:17, :] = get_rows(ce, co, up, inner, 8 + n // 4, n % 4, 1)

    def drift(p, carry):
        h = heat_x[p + 1]
        lane = lanes(h.shape)
        right = jnp.where(lane == 255, 0.0, pltpu.roll(h, 255, axis=1))
        left = jnp.where(lane == 0, 0.0, pltpu.roll(h, 1, axis=1))
        force_x[0, p] = force_x[0, p] - (heat_x[p + 2] - heat_x[p])
        force_x[1, p] = force_x[1, p] - (pltpu.roll(h, 23, axis=0) - pltpu.roll(h, 1, axis=0))
        force_x[2, p] = force_x[2, p] - (right - left)
        return carry

    lax.fori_loop(0, 8, drift, 0)
    smooth(v0, force_x, kinv_x, obst_x, v1, v2)

    shape = (16, 256)
    first = jnp.bitwise_and(lanes(shape), 1) == 0
    for q in range(2):
        low = None
        for p in (2 * q, 2 * q + 1):
            out = residual_plane(v2, force_x, main, cross, p)
            cut = clip[p] == 1
            out[0] = jnp.where(cut, 0.0, out[0])
            gap = jnp.logical_and(touch[p] == 1, clip[p] != 1)
            room = jnp.where(gap, clear[p] - v2[0, p + 1, 0:16, :], FREE)
            part = out + [room]
            if low is None:
                low = part
            else:
                low = [jnp.minimum(x, y) if i == 3 else x + y for i, (x, y) in enumerate(zip(low, part))]
        for i in range(4):
            x = pair_rows(rest.at[i], low[i] if i == 3 else 0.25 * low[i], jnp.minimum if i == 3 else jnp.add)
            if i == 3:
                x = jnp.minimum(x, pltpu.roll(x, 255, axis=1))
                x = jnp.where(first[0:8], x, 0.0)
            gath[(2 * i + q) * 8 : (2 * i + q) * 8 + 8, :] = x
    small_out[...] = pair_lanes(gath[...]).reshape(8, 8, 128)
    for c in range(3):
        for k in range(2):
            planes_out[2 * c + k] = v2[c, k + 2, 0:16, :]
            for side in range(2):
                put_extra(planes_out, (c * 2 + k) * 2 + side, v2[c, k + 2, 16 if side else 23 : 17 if side else 24, :])
    for p in range(4):
        planes_out[6 + p] = clip[p].astype(F32)
        low, high = get_rows(be, bo, up, inner, 36 + p, 0, 3)
        put_extra(planes_out, 12 + 4 * p, low[1:3])
        put_extra(planes_out, 14 + 4 * p, high[0:2])
    for c in range(3):
        for p in range(4):
            put_rows(pe, po, up, c * 2 + p // 2, 2 * (p % 2), v2[c, p + 1, 0:16, :], 2, 1)
        for side in range(2):
            n = 2 * c + side
            put_rows(pe, po, up, 6 + n // 2, 2 * (n % 2), v2[c, 5 * side, 0:16, :], 2)


def pair_spread(x, op):
    n, m = x.shape
    even = jnp.bitwise_and(lanes(x.shape), 1) == 0
    x = op(x, jnp.where(even, pltpu.roll(x, m - 1, axis=1), pltpu.roll(x, 1, axis=1)))
    even = jnp.bitwise_and(rows(x.shape), 1) == 0
    return op(x, jnp.where(even, pltpu.roll(x, n - 1, axis=0), pltpu.roll(x, 1, axis=0)))


def coarse(
    pos, b0, eb, ob, b3, b4, k01, k23, r1e, r1o, rme, rmo, r2e, r2o,
    mid2, own, g, ki, va, vb, f3, k3, o3, l3,
):
    par = jnp.bitwise_and(pos[0], 1)
    up, inner = sides(pos[1])
    grp = pos[0]
    one, mid, two = (r1e, r1o), (rme, rmo), (r2e, r2o)
    slots = [
        (b0, 0, one, 0, k01, 0, one, 8), (eb, 0, mid, 0, k01, 12, one, 20),
        (ob, 0, mid, 32, k23, 0, one, 32), (ob, 8, mid, 40, k23, 12, one, 44),
        (b3, 0, two, 0, eb, 8, mid, 8), (b3, 8, two, 8, eb, 20, mid, 20),
        (b4, 0, two, 16, ob, 16, mid, 48), (b4, 8, two, 24, ob, 28, mid, 60),
    ]
    for s, (mine, m, (re, ro), r, mat, k, (ke, ko), kr) in enumerate(slots):
        place = jnp.where(par == 0, EVEN_SLOTS[s], 7 - EVEN_SLOTS[s])
        where = grp + place - jnp.where(par == 0, 4, 3)
        real = jnp.logical_and(where >= 0, where < 16)
        real_o = jnp.logical_and(real, inner)

        def lay(f, q, x, e, o):
            a = jnp.where(real, e, 0.0)
            b = jnp.where(real_o, o, 0.0)
            to = g.at[f, 2 * place + q]
            to[0:8, :] = jnp.where(real, x, 0.0)
            to[8:16, :] = jnp.where(up, a, b)
            to[16:24, :] = jnp.where(up, b, a)

        def fill(f, carry):
            for q in range(2):
                t = 2 * f + q
                lay(f, q, mine[m + t], re[r + t], ro[r + t])
            return carry

        def fill_k(f, carry):
            for q in range(2):
                t = 2 * f + q
                lay(4 + f, q, mat[k + t], ke[kr + t], ko[kr + t])
            return carry

        lax.fori_loop(0, 4, fill, 0, unroll=2)
        lax.fori_loop(0, 6, fill_k, 0, unroll=2)

    def start(p, carry):
        inv = inverse(*[g[4 + k, p] for k in range(6)])
        for k in range(6):
            ki[k, p] = inv[k]
        v = symmetric_times(inv, [OMEGA * g[c, p] for c in range(3)])
        va[0, p] = jnp.minimum(v[0], g[3, p])
        va[1, p] = v[1]
        va[2, p] = v[2]
        return carry

    lax.fori_loop(0, 16, start, 0, unroll=4)

    def sweep(src, dst):
        def body(p, carry):
            rest = []
            for c in range(3):
                near = src[c, p - 1] + src[c, p + 1] + beside(src[c, p])
                rest.append(g[c, p] + near)
            step = symmetric_times([ki[k, p] for k in range(6)], rest)
            new = [KEEP * src[c, p] + OMEGA * step[c] for c in range(3)]
            dst[0, p] = jnp.minimum(new[0], g[3, p])
            dst[1, p] = new[1]
            dst[2, p] = new[2]
            return carry

        return body

    lax.fori_loop(1, 15, sweep(va, vb), 0, unroll=4)

    def third(q, carry):
        total = None
        for p in (2 * q, 2 * q + 1):
            mat = [g[4 + k, p] for k in range(6)]
            kv = symmetric_times(mat, [vb[c, p] for c in range(3)])
            part = []
            for c in range(3):
                near = vb[c, p - 1] + vb[c, p + 1] + beside(vb[c, p])
                part.append(g[c, p] - (kv[c] - near))
            part += mat + [g[3, p] - vb[0, p]]
            if total is None:
                total = part
            else:
                total = [jnp.minimum(x, y) if i == 9 else x + y for i, (x, y) in enumerate(zip(total, part))]
        force = [0.25 * pair_spread(total[c], jnp.add) for c in range(3)]
        mat = [0.125 * pair_spread(total[3 + k], jnp.add) for k in range(6)]
        room = pair_spread(total[9], jnp.minimum)
        inv = inverse(*mat)
        v = symmetric_times(inv, [OMEGA * x for x in force])
        v[0] = jnp.minimum(v[0], room)
        for c in range(3):
            f3[c, q] = force[c]
            l3[c, q] = v[c]
        for k in range(6):
            k3[k, q] = inv[k]
        o3[q] = room
        return carry

    lax.fori_loop(1, 7, third, 0, unroll=4)

    def lowest(q, carry):
        rest = []
        for c in range(3):
            near = l3[c, q - 1] + l3[c, q + 1] + beside(l3[c, q], 2)
            rest.append(f3[c, q] + near)
        step = symmetric_times([k3[k, q] for k in range(6)], rest)
        new = [KEEP * l3[c, q] + OMEGA * step[c] for c in range(3)]
        new[0] = jnp.minimum(new[0], o3[q])
        for c in range(3):
            for p in (2 * q, 2 * q + 1):
                va[c, p] = vb[c, p] + new[c]
        return carry

    lax.fori_loop(2, 6, lowest, 0, unroll=4)
    lax.fori_loop(5, 11, sweep(va, vb), 0, unroll=4)
    lax.fori_loop(6, 10, sweep(vb, va), 0, unroll=4)
    for c in range(3):
        for k in range(4):
            mid2[c, k, 0:10, :] = va[c, 6 + k, 0:10, :]
            mid2[c, k, 10:12, :] = va[c, 6 + k, 22:24, :]
        for k in range(2):
            own[c, k, 0:10, :] = va[c, 8 - 2 * par + k, 0:10, :]
            own[c, k, 10:12, :] = va[c, 8 - 2 * par + k, 22:24, :]


def finish(
    pos, pre, ge, go, r1e, r1o, be, bo, mid2, other, force_x, kinv_x, obst_x, clip, main, cross,
    moved, residual, v0, v1, v2, clip_x, mid_x, fine,
):
    par = jnp.bitwise_and(pos[0], 1)
    even, inside = sides(pos[0])
    up, inner = sides(pos[1])
    for c in range(3):
        for p in range(6):
            v0[c, p + 2] = pre[c, p]
        for p in range(4):
            to = v0.at[c, p + 3]
            to[21:23, :], to[17:19, :] = get_rows(r1e, r1o, up, inner, 56 + c * 2 + p // 2, 2 * (p % 2), 2)
        for side in range(2):
            low = side == 0
            n = 2 * c + side
            to = v0.at[c, 2 if low else 7]
            to[22:24, :], to[16:18, :] = get_rows(r1e, r1o, up, inner, 56 + 6 + n // 2, 2 * (n % 2), 2)
            for k in range(2):
                to = v0.at[c, k if low else 8 + k]
                to[0:16, :] = halo_plane(ge, go, even, inside, low, 2 * c + k)
            k = 1 if low else 0
            to = v0.at[c, 1 if low else 8]
            to[23:24, :] = get_extra(ge, go, even, inside, low, (c * 2 + k) * 2, 1)
            to[16:17, :] = get_extra(ge, go, even, inside, low, (c * 2 + k) * 2 + 1, 1)
    for p in range(4):
        to = clip_x.at[p + 3]
        to[0:16, :] = clip[p].astype(F32)
        to[21:24, :], to[16:19, :] = get_rows(be, bo, up, inner, 36 + p, 0, 3)
    for side in range(2):
        low = side == 0
        for k in range(3):
            to = clip_x.at[k if low else 7 + k]
            to[0:16, :] = halo_plane(ge, go, even, inside, low, 6 + k + (1 if low else 0))
        to = clip_x.at[2 if low else 7]
        n = 12 + 4 * (3 if low else 0)
        to[22:24, :] = get_extra(ge, go, even, inside, low, n, 2)
        to[16:18, :] = get_extra(ge, go, even, inside, low, n + 2, 2)
        n = 12 + 4 * (2 if low else 1)
        to = clip_x.at[1 if low else 8]
        to[23:24, :] = get_extra(ge, go, even, inside, low, n + 1, 1)
        to[16:17, :] = get_extra(ge, go, even, inside, low, n + 2, 1)
    i, j = rows((128, 256)), lanes((128, 256))
    copy = jnp.where(lax.shift_right_logical(j, 1) == i, 1.0, 0.0)
    for c in range(3):
        mid_x[c, pl.ds(2 * par, 4)] = mid2[c]
        mid_x[c, pl.ds(4 * (1 - par), 2)] = other[c]
    wide = jnp.dot(
        mid_x[...].reshape(3 * 6 * 16, 128), copy, precision=HIGH, preferred_element_type=F32
    )
    for c in range(3):
        for k in range(6):
            x = wide[(c * 6 + k) * 16 : (c * 6 + k) * 16 + 16]
            for h in range(2):
                y = x[:, 128 * h : 128 * h + 128]
                fine[h, pl.ds(0, 16, 2), :] = y
                fine[h, pl.ds(1, 16, 2), :] = y
            up2 = jnp.concatenate([fine[0, 0:24, :], fine[1, 0:24, :]], 1)
            for p in range(10):
                if (p + 1) // 2 == k:
                    add = jnp.where(clip_x[p] == 1.0, 0.0, up2) if c == 0 else up2
                    v0[c, p] = v0[c, p] + add
    smooth(v0, force_x, kinv_x, obst_x, v1, v2)
    for p in range(4):
        out = residual_plane(v2, force_x, main, cross, p)
        for c in range(3):
            residual[c, p] = out[c]
            moved[c, p] = v2[c, p + 1, 0:16, :]


def call(kernel, outs, scratch, *args, limit=0):
    vm = pl.BlockSpec(memory_space=pltpu.VMEM)
    source = pl.BlockSpec(memory_space=pltpu.HBM) if limit else vm
    return pl.pallas_call(
        kernel,
        out_shape=[jax.ShapeDtypeStruct(x, F32) for x in outs],
        in_specs=[pl.BlockSpec(memory_space=pltpu.SMEM)] + [source] * (len(args) - 1),
        out_specs=[vm] * len(outs),
        scratch_shapes=[pltpu.VMEM(x, F32) if isinstance(x, tuple) else x for x in scratch],
        compiler_params=pltpu.CompilerParams(vmem_limit_bytes=limit or 32 * 1024 * 1024),
    )(*args)


EVEN = [(i, i ^ 1) for i in range(16)]
ODD = [(i, (((i + 1) ^ 1) - 1) % 16) for i in range(16)]


def swap_even(x, axis):
    return lax.ppermute(x, axis, EVEN)


def swap_odd(x, axis):
    return lax.ppermute(x, axis, ODD)


def local(disp, trac, heat, main, cross, clear, touch, clip):
    pos = jnp.stack([lax.axis_index("grp"), lax.axis_index("brick")]).astype(jnp.int32)
    own, vec, six = (4, 16, 256), (3, 4, 16, 256), (6, 4, 16, 256)
    kinv, obst, me, mo, be, bo, k0 = call(
        load_pack,
        [six, own, (35, 16, 256), (32, 16, 256), (40, 8, 128), (40, 8, 128), (12, 8, 128)],
        [vec, vec, own, vec, vec, own, pltpu.VMEM(own, jnp.int32), pltpu.VMEM(own, jnp.int32),
         (12, 2, 16, 128), (96, 256), pltpu.SemaphoreType.DMA((8,))],
        pos, *[pltpu.with_memory_space_constraint(z, pltpu.HBM) for z in (disp, trac, heat, main, cross, clear, touch, clip)], limit=32 * 1024 * 1024,
    )
    re, ro = swap_even(me, "grp"), swap_odd(mo, "grp")
    re_b, ro_b = swap_even(be, "brick"), swap_odd(bo, "brick")
    ce, co, k01 = call(pack_corner, [(13, 8, 128)] * 2 + [(24, 8, 128)], [], pos, re, ro, k0)
    re_c, ro_c = swap_even(ce, "brick"), swap_odd(co, "brick")
    k23 = swap_odd(k01, "grp")
    force_x, kinv_x, obst_x, pre, b0, planes, pe, po = call(
        presmooth,
        [(3, 8, 24, 256), (6, 8, 24, 256), (8, 24, 256), (3, 6, 24, 256), (8, 8, 128),
         (12, 16, 256), (9, 8, 128), (9, 8, 128)],
        [(3, 10, 24, 256), (10, 24, 256), (3, 8, 24, 256), (4, 2, 16, 128), (64, 256)],
        pos, disp, heat, clip, trac, kinv, obst, main, cross, clear, touch,
        re, ro, re_b, ro_b, re_c, ro_c,
    )
    eb = swap_even(jnp.concatenate([b0, k23], 0), "grp")
    ob = swap_odd(jnp.concatenate([b0, eb], 0), "grp")
    ge, go = swap_even(planes, "grp"), swap_odd(planes, "grp")
    after, go = lax.optimization_barrier((b0, go))
    r1e = swap_even(jnp.concatenate([after, k01, k23, pe], 0), "brick")
    r1o = swap_odd(jnp.concatenate([after, k01, k23, po], 0), "brick")
    after, ge = lax.optimization_barrier((eb, ge))
    middle = jnp.concatenate([after, ob], 0)
    rme, rmo = swap_even(middle, "brick"), swap_odd(middle, "brick")
    b3 = swap_even(ob[:16], "grp")
    b4 = swap_odd(b3, "grp")
    last = jnp.concatenate([b3, b4], 0)
    r2e, r2o = swap_even(last, "brick"), swap_odd(last, "brick")
    field, third = (3, 16, 24, 128), (3, 8, 24, 128)
    mid2, mine = call(
        coarse,
        [(3, 4, 16, 128), (3, 2, 16, 128)],
        [(10, 16, 24, 128), (6, 16, 24, 128), field, field, third, (6, 8, 24, 128),
         (8, 24, 128), third],
        pos, b0, eb, ob, b3, b4, k01, k23, r1e, r1o, rme, rmo, r2e, r2o,
    )
    other = swap_even(mine, "grp")
    return tuple(
        call(
            finish,
            [vec, vec],
            [(3, 10, 24, 256), (3, 8, 24, 256), (3, 6, 24, 256), (10, 24, 256), (3, 6, 16, 128),
             (2, 32, 128)],
            pos, pre, ge, go, r1e, r1o, re_b, ro_b, mid2, other, force_x, kinv_x, obst_x, clip,
            main, cross,
        )
    )


def solution(mesh):
    vector, scalar = P(None, "grp", "brick", None), P("grp", "brick", None)
    return jax.shard_map(
        local,
        mesh=mesh,
        in_specs=(vector, vector, scalar, vector, vector, scalar, scalar, scalar),
        out_specs=(vector, vector),
        check_vma=False,
    )
```

```python
import jax
import jax.numpy as jnp
from jax import lax
from jax.experimental import pallas as pl
from jax.experimental.pallas import tpu as pltpu
from jax.sharding import PartitionSpec as P

OMEGA = 0.6
KEEP = 0.4
FREE = 1000.0
F32 = jnp.float32
HIGH = lax.Precision.HIGHEST
EVEN_SLOTS = (4, 5, 3, 2, 6, 7, 1, 0)


def inverse(a, b, c, d, e, f):
    i00 = b * c - e * e
    i11 = a * c - f * f
    i22 = a * b - d * d
    i01 = f * e - d * c
    i12 = d * f - a * e
    i02 = d * e - b * f
    det = a * i00 + d * i01 + f * i02
    scale = jnp.where(det == 0.0, 0.0, 1.0 / jnp.where(det == 0.0, 1.0, det))
    return [i00 * scale, i11 * scale, i22 * scale, i01 * scale, i12 * scale, i02 * scale]


def symmetric_times(m, r):
    return [
        m[0] * r[0] + m[3] * r[1] + m[5] * r[2],
        m[3] * r[0] + m[1] * r[1] + m[4] * r[2],
        m[5] * r[0] + m[4] * r[1] + m[2] * r[2],
    ]


def lanes(shape):
    return lax.broadcasted_iota(jnp.int32, shape, 1)


def rows(shape):
    return lax.broadcasted_iota(jnp.int32, shape, 0)


def beside(x, step=1):
    n, m = x.shape
    lane = lanes(x.shape)
    left = jnp.where(lane < step, 0.0, pltpu.roll(x, step, axis=1))
    right = jnp.where(lane >= m - step, 0.0, pltpu.roll(x, m - step, axis=1))
    return (left + right) + (pltpu.roll(x, step, axis=0) + pltpu.roll(x, n - step, axis=0))


def sides(g):
    return (jnp.bitwise_and(g, 1) == 0), jnp.logical_and(g > 0, g < 15)


def put(msg, t, r, x):
    n = x.shape[0]
    msg[t, r : r + n, :] = x[:, :128]
    msg[t, r + 4 : r + 4 + n, :] = x[:, 128:]


def put_rows(be, bo, up, t, r, x, n, skip=0):
    low, high = x[skip : skip + n], x[16 - skip - n : 16 - skip]
    put(be, t, r, jnp.where(up, high, low))
    put(bo, t, r, jnp.where(up, low, high))


def get_rows(be, bo, up, inside, t, r, n):
    e = jnp.concatenate([be[t, r : r + n, :], be[t, r + 4 : r + 4 + n, :]], 1)
    o = jnp.concatenate([bo[t, r : r + n, :], bo[t, r + 4 : r + 4 + n, :]], 1)
    o = jnp.where(inside, o, 0.0)
    return jnp.where(up, o, e), jnp.where(up, e, o)


def fields(disp, heat, trac, kinv, obst):
    wide = [lambda p, c=c: disp[c, p] for c in range(3)]
    wide += [lambda p: heat[p]]
    near = [lambda p, c=c: trac[c, p] for c in range(3)]
    near += [lambda p, k=k: kinv[k, p] for k in range(6)]
    near += [lambda p: obst[p]]
    return wide, near


def load_pack(
    pos, disp_h, trac_h, heat_h, main_h, cross_h, clear_h, touch_h, clip_h,
    kinv, obst, me, mo, be, bo, k0,
    disp, trac, heat, main, cross, clear, touch, clip, rest, gath, sem,
):
    pairs = [
        (main_h, main), (cross_h, cross), (clear_h, clear), (touch_h, touch),
        (disp_h, disp), (trac_h, trac), (heat_h, heat), (clip_h, clip),
    ]
    copies = [pltpu.make_async_copy(x, y, sem.at[i]) for i, (x, y) in enumerate(pairs)]
    for c in copies:
        c.start()
    par = jnp.bitwise_and(pos[0], 1)
    up = jnp.bitwise_and(pos[1], 1) == 0
    copies[0].wait()
    copies[1].wait()

    def invert(p, carry):
        inv = inverse(main[0, p], main[1, p], main[2, p], cross[0, p], cross[1, p], cross[2, p])
        for k in range(6):
            kinv[k, p] = inv[k]
        return carry

    lax.fori_loop(0, 4, invert, 0)
    for k in range(6):
        src, c = (main, k) if k < 3 else (cross, k - 3)
        for q in range(2):
            x = 0.125 * (src[c, 2 * q] + src[c, 2 * q + 1])
            gath[(2 * k + q) * 8 : (2 * k + q) * 8 + 8, :] = pair_rows(rest.at[2 * k + q], x, jnp.add)
    k0[...] = pair_lanes(gath[...]).reshape(12, 8, 128)
    copies[2].wait()
    copies[3].wait()
    obst[...] = jnp.where(touch[...] == 1, clear[...], FREE)
    for c in copies[4:]:
        c.wait()
    for msg, at in ((me, 1 - par), (mo, par)):
        for c in range(3):
            msg[3 * c : 3 * c + 3] = disp[c, pl.ds(at, 3)]
        msg[9:12] = heat[pl.ds(at, 3)]
        for c in range(3):
            msg[12 + 2 * c : 14 + 2 * c] = trac[c, pl.ds(2 * at, 2)]
        for k in range(6):
            msg[18 + 2 * k : 20 + 2 * k] = kinv[k, pl.ds(2 * at, 2)]
        msg[30:32] = obst[pl.ds(2 * at, 2)]
    for t in range(12):
        r, h = 8 * (t % 4 // 2), 128 * (t % 2)
        me[32 + t // 4, r : r + 8, h : h + 128] = k0[t]
    wide, near = fields(disp, heat, trac, kinv, obst)
    for f in range(4):
        for p in range(4):
            put_rows(be, bo, up, f * 4 + p, 0, wide[f](p), 3)
    for f in range(10):
        for p in range(4):
            put_rows(be, bo, up, 16 + f * 2 + p // 2, 2 * (p % 2), near[f](p), 2)
    for p in range(4):
        put_rows(be, bo, up, 36 + p, 0, clip[p].astype(F32), 3)


def halo_plane(re, ro, even, inside, low, k):
    e, o = re[k], jnp.where(inside, ro[k], 0.0)
    return jnp.where(even, o, e) if low else jnp.where(even, e, o)


def pack_corner(pos, re, ro, k0, be, bo, k01):
    k01[0:12] = k0[...]
    for t in range(12):
        r, h = 8 * (t % 4 // 2), 128 * (t % 2)
        k01[12 + t] = re[32 + t // 4, r : r + 8, h : h + 128]
    even, inside = sides(pos[0])
    up = jnp.bitwise_and(pos[1], 1) == 0
    for f in range(4):
        for side in range(2):
            low = side == 0
            x = halo_plane(re, ro, even, inside, low, 3 * f + (2 if low else 0))
            put_rows(be, bo, up, f * 2 + side, 0, x, 2)
            x = halo_plane(re, ro, even, inside, low, 3 * f + 1)
            put_rows(be, bo, up, f * 2 + side, 2, x, 1)
    for f in range(10):
        for side in range(2):
            low = side == 0
            n = f * 2 + side
            x = halo_plane(re, ro, even, inside, low, 12 + 2 * f + (1 if low else 0))
            put_rows(be, bo, up, 8 + n // 4, n % 4, x, 1)


def smooth(v0, force, kinv, obst, v1, v2):
    def one(src, dst, shift, planes):
        def body(p, carry):
            rest = []
            for c in range(3):
                near = src[c, p] + src[c, p + 2] + beside(src[c, p + 1])
                rest.append(force[c, p + shift] + near)
            inv = [kinv[k, p + shift] for k in range(6)]
            step = symmetric_times(inv, rest)
            new = [KEEP * src[c, p + 1] + OMEGA * step[c] for c in range(3)]
            dst[0, p] = jnp.minimum(new[0], obst[p + shift])
            dst[1, p] = new[1]
            dst[2, p] = new[2]
            return carry

        lax.fori_loop(0, planes, body, 0, unroll=4)

    one(v0, v1, 0, 8)
    one(v1, v2, 1, 6)


def residual_plane(v2, force, main, cross, p):
    own = [v2[c, p + 1][0:16] for c in range(3)]
    mat = [main[c, p] for c in range(3)] + [cross[c, p] for c in range(3)]
    kv = symmetric_times(mat, own)
    out = []
    for c in range(3):
        near = v2[c, p, 0:16, :] + v2[c, p + 2, 0:16, :] + beside(v2[c, p + 1])[0:16]
        out.append(force[c, p + 2, 0:16, :] - (kv[c] - near))
    return out


def pair_rows(room, x, op):
    for h in range(2):
        room[h] = x[:, 128 * h : 128 * h + 128]
    return jnp.concatenate(
        [op(room[h, pl.ds(0, 8, 2), :], room[h, pl.ds(1, 8, 2), :]) for h in range(2)], 1
    )


def pair_lanes(x):
    i, j = rows((256, 128)), lanes((256, 128))
    pick = jnp.where(lax.shift_right_logical(i, 1) == j, 1.0, 0.0)
    return jnp.dot(x, pick, precision=HIGH, preferred_element_type=F32)


def put_extra(planes, n, x):
    planes[10 + n // 16, n % 16 : n % 16 + x.shape[0], :] = x


def get_extra(ge, go, even, inside, low, n, m):
    e = ge[10 + n // 16, n % 16 : n % 16 + m, :]
    o = jnp.where(inside, go[10 + n // 16, n % 16 : n % 16 + m, :], 0.0)
    return jnp.where(even, o, e) if low else jnp.where(even, e, o)


def presmooth(
    pos, disp, heat, clip, trac, kinv, obst, main, cross, clear, touch,
    re, ro, be, bo, ce, co,
    force_x, kinv_x, obst_x, v2, small_out, planes_out, pe, po,
    v0, heat_x, v1, rest, gath,
):
    even, inside = sides(pos[0])
    up, inner = sides(pos[1])
    wide, near = fields(disp, heat, trac, kinv, obst)
    wide_to = [lambda p, c=c: v0.at[c, p] for c in range(3)]
    wide_to += [lambda p: heat_x.at[p]]
    near_to = [lambda p, c=c: force_x.at[c, p] for c in range(3)]
    near_to += [lambda p, k=k: kinv_x.at[k, p] for k in range(6)]
    near_to += [lambda p: obst_x.at[p]]
    for f in range(4):
        for p in range(4):
            to = wide_to[f](p + 3)
            to[0:16, :] = wide[f](p)
            to[21:24, :], to[16:19, :] = get_rows(be, bo, up, inner, f * 4 + p, 0, 3)
        for side in range(2):
            low = side == 0
            for k in range(3):
                to = wide_to[f](k if low else 7 + k)
                to[0:16, :] = halo_plane(re, ro, even, inside, low, 3 * f + k)
            to = wide_to[f](2 if low else 7)
            to[22:24, :], to[16:18, :] = get_rows(ce, co, up, inner, f * 2 + side, 0, 2)
            to = wide_to[f](1 if low else 8)
            to[23:24, :], to[16:17, :] = get_rows(ce, co, up, inner, f * 2 + side, 2, 1)
    for f in range(10):
        for p in range(4):
            to = near_to[f](p + 2)
            to[0:16, :] = near[f](p)
            to[22:24, :], to[16:18, :] = get_rows(be, bo, up, inner, 16 + f * 2 + p // 2, 2 * (p % 2), 2)
        for side in range(2):
            low = side == 0
            for k in range(2):
                to = near_to[f](k if low else 6 + k)
                to[0:16, :] = halo_plane(re, ro, even, inside, low, 12 + 2 * f + k)
            n = f * 2 + side
            to = near_to[f](1 if low else 6)
            to[23:24, :], to[16:17, :] = get_rows(ce, co, up, inner, 8 + n // 4, n % 4, 1)

    def drift(p, carry):
        h = heat_x[p + 1]
        lane = lanes(h.shape)
        right = jnp.where(lane == 255, 0.0, pltpu.roll(h, 255, axis=1))
        left = jnp.where(lane == 0, 0.0, pltpu.roll(h, 1, axis=1))
        force_x[0, p] = force_x[0, p] - (heat_x[p + 2] - heat_x[p])
        force_x[1, p] = force_x[1, p] - (pltpu.roll(h, 23, axis=0) - pltpu.roll(h, 1, axis=0))
        force_x[2, p] = force_x[2, p] - (right - left)
        return carry

    lax.fori_loop(0, 8, drift, 0)
    smooth(v0, force_x, kinv_x, obst_x, v1, v2)

    shape = (16, 256)
    first = jnp.bitwise_and(lanes(shape), 1) == 0
    for q in range(2):
        low = None
        for p in (2 * q, 2 * q + 1):
            out = residual_plane(v2, force_x, main, cross, p)
            cut = clip[p] == 1
            out[0] = jnp.where(cut, 0.0, out[0])
            gap = jnp.logical_and(touch[p] == 1, clip[p] != 1)
            room = jnp.where(gap, clear[p] - v2[0, p + 1, 0:16, :], FREE)
            part = out + [room]
            if low is None:
                low = part
            else:
                low = [jnp.minimum(x, y) if i == 3 else x + y for i, (x, y) in enumerate(zip(low, part))]
        for i in range(4):
            x = pair_rows(rest.at[i], low[i] if i == 3 else 0.25 * low[i], jnp.minimum if i == 3 else jnp.add)
            if i == 3:
                x = jnp.minimum(x, pltpu.roll(x, 255, axis=1))
                x = jnp.where(first[0:8], x, 0.0)
            gath[(2 * i + q) * 8 : (2 * i + q) * 8 + 8, :] = x
    small_out[...] = pair_lanes(gath[...]).reshape(8, 8, 128)
    for c in range(3):
        for k in range(2):
            planes_out[2 * c + k] = v2[c, k + 2, 0:16, :]
            for side in range(2):
                put_extra(planes_out, (c * 2 + k) * 2 + side, v2[c, k + 2, 16 if side else 23 : 17 if side else 24, :])
    for p in range(4):
        planes_out[6 + p] = clip[p].astype(F32)
        low, high = get_rows(be, bo, up, inner, 36 + p, 0, 3)
        put_extra(planes_out, 12 + 4 * p, low[1:3])
        put_extra(planes_out, 14 + 4 * p, high[0:2])
    for c in range(3):
        for p in range(4):
            put_rows(pe, po, up, c * 2 + p // 2, 2 * (p % 2), v2[c, p + 1, 0:16, :], 2, 1)
        for side in range(2):
            n = 2 * c + side
            put_rows(pe, po, up, 6 + n // 2, 2 * (n % 2), v2[c, 5 * side, 0:16, :], 2)


def pair_spread(x, op):
    n, m = x.shape
    even = jnp.bitwise_and(lanes(x.shape), 1) == 0
    x = op(x, jnp.where(even, pltpu.roll(x, m - 1, axis=1), pltpu.roll(x, 1, axis=1)))
    even = jnp.bitwise_and(rows(x.shape), 1) == 0
    return op(x, jnp.where(even, pltpu.roll(x, n - 1, axis=0), pltpu.roll(x, 1, axis=0)))


SLOTS = (
    ("b0", 0, "one", 0, "k01", 0, "one", 8), ("eb", 0, "mid", 0, "k01", 12, "one", 20),
    ("ob", 0, "mid", 32, "k23", 0, "one", 32), ("ob", 8, "mid", 40, "k23", 12, "one", 44),
    ("b3", 0, "two", 0, "eb", 8, "mid", 8), ("b3", 8, "two", 8, "eb", 20, "mid", 20),
    ("b4", 0, "two", 16, "ob", 16, "mid", 48), ("b4", 8, "two", 24, "ob", 28, "mid", 60),
)


def lay_window(pos, refs, g, force):
    par = jnp.bitwise_and(pos[0], 1)
    up, inner = sides(pos[1])
    grp = pos[0]
    for s, (mine, m, row, r, mat, k, krow, kr) in enumerate(SLOTS):
        if not force:
            mine, m, row, r = mat, k, krow, kr
        mine, (re, ro) = refs[mine], refs[row]
        place = jnp.where(par == 0, EVEN_SLOTS[s], 7 - EVEN_SLOTS[s])
        where = grp + place - jnp.where(par == 0, 4, 3)
        real = jnp.logical_and(where >= 0, where < 16)
        real_o = jnp.logical_and(real, inner)

        def fill(f, carry):
            for q in range(2):
                t = 2 * f + q
                a = jnp.where(real, re[r + t], 0.0)
                b = jnp.where(real_o, ro[r + t], 0.0)
                to = g.at[f, 2 * place + q]
                to[0:8, :] = jnp.where(real, mine[m + t], 0.0)
                to[8:16, :] = jnp.where(up, a, b)
                to[16:24, :] = jnp.where(up, b, a)
            return carry

        lax.fori_loop(0, 4 if force else 6, fill, 0, unroll=2)


def coarse_blocks(pos, eb, ob, k01, k23, r1e, r1o, rme, rmo, gk, ki, k3):
    refs = dict(eb=eb, ob=ob, k01=k01, k23=k23, one=(r1e, r1o), mid=(rme, rmo))
    lay_window(pos, refs, gk, False)

    def invert(p, carry):
        inv = inverse(*[gk[k, p] for k in range(6)])
        for k in range(6):
            ki[k, p] = inv[k]
        return carry

    lax.fori_loop(0, 16, invert, 0, unroll=4)

    def third(q, carry):
        mat = [0.125 * pair_spread(gk[k, 2 * q] + gk[k, 2 * q + 1], jnp.add) for k in range(6)]
        inv = inverse(*mat)
        for k in range(6):
            k3[k, q] = inv[k]
        return carry

    lax.fori_loop(1, 7, third, 0, unroll=2)


def coarse(
    pos, b0, eb, ob, b3, b4, r1e, r1o, rme, rmo, r2e, r2o, gk, ki, k3,
    mid2, own, g, va, vb, f3, o3, l3,
):
    par = jnp.bitwise_and(pos[0], 1)
    refs = dict(b0=b0, eb=eb, ob=ob, b3=b3, b4=b4, one=(r1e, r1o), mid=(rme, rmo), two=(r2e, r2o))
    lay_window(pos, refs, g, True)

    def start(p, carry):
        v = symmetric_times([ki[k, p] for k in range(6)], [OMEGA * g[c, p] for c in range(3)])
        va[0, p] = jnp.minimum(v[0], g[3, p])
        va[1, p] = v[1]
        va[2, p] = v[2]
        return carry

    lax.fori_loop(0, 16, start, 0, unroll=4)

    def sweep(src, dst):
        def body(p, carry):
            rest = []
            for c in range(3):
                near = src[c, p - 1] + src[c, p + 1] + beside(src[c, p])
                rest.append(g[c, p] + near)
            step = symmetric_times([ki[k, p] for k in range(6)], rest)
            new = [KEEP * src[c, p] + OMEGA * step[c] for c in range(3)]
            dst[0, p] = jnp.minimum(new[0], g[3, p])
            dst[1, p] = new[1]
            dst[2, p] = new[2]
            return carry

        return body

    lax.fori_loop(1, 15, sweep(va, vb), 0, unroll=4)

    def third(q, carry):
        total = None
        for p in (2 * q, 2 * q + 1):
            mat = [gk[k, p] for k in range(6)]
            kv = symmetric_times(mat, [vb[c, p] for c in range(3)])
            part = []
            for c in range(3):
                near = vb[c, p - 1] + vb[c, p + 1] + beside(vb[c, p])
                part.append(g[c, p] - (kv[c] - near))
            part.append(g[3, p] - vb[0, p])
            if total is None:
                total = part
            else:
                total = [jnp.minimum(x, y) if i == 3 else x + y for i, (x, y) in enumerate(zip(total, part))]
        force = [0.25 * pair_spread(total[c], jnp.add) for c in range(3)]
        room = pair_spread(total[3], jnp.minimum)
        v = symmetric_times([k3[k, q] for k in range(6)], [OMEGA * x for x in force])
        v[0] = jnp.minimum(v[0], room)
        for c in range(3):
            f3[c, q] = force[c]
            l3[c, q] = v[c]
        o3[q] = room
        return carry

    lax.fori_loop(1, 7, third, 0, unroll=4)

    def lowest(q, carry):
        rest = []
        for c in range(3):
            near = l3[c, q - 1] + l3[c, q + 1] + beside(l3[c, q], 2)
            rest.append(f3[c, q] + near)
        step = symmetric_times([k3[k, q] for k in range(6)], rest)
        new = [KEEP * l3[c, q] + OMEGA * step[c] for c in range(3)]
        new[0] = jnp.minimum(new[0], o3[q])
        for c in range(3):
            for p in (2 * q, 2 * q + 1):
                va[c, p] = vb[c, p] + new[c]
        return carry

    lax.fori_loop(2, 6, lowest, 0, unroll=4)
    lax.fori_loop(5, 11, sweep(va, vb), 0, unroll=4)
    lax.fori_loop(6, 10, sweep(vb, va), 0, unroll=4)
    for c in range(3):
        for k in range(4):
            mid2[c, k, 0:10, :] = va[c, 6 + k, 0:10, :]
            mid2[c, k, 10:12, :] = va[c, 6 + k, 22:24, :]
        for k in range(2):
            own[c, k, 0:10, :] = va[c, 8 - 2 * par + k, 0:10, :]
            own[c, k, 10:12, :] = va[c, 8 - 2 * par + k, 22:24, :]


def gather_pre(pos, pre, ge, go, r1e, r1o, be, bo, clip, v0, clip_x):
    even, inside = sides(pos[0])
    up, inner = sides(pos[1])
    for c in range(3):
        for p in range(6):
            v0[c, p + 2] = pre[c, p]
        for p in range(4):
            to = v0.at[c, p + 3]
            to[21:23, :], to[17:19, :] = get_rows(r1e, r1o, up, inner, 56 + c * 2 + p // 2, 2 * (p % 2), 2)
        for side in range(2):
            low = side == 0
            n = 2 * c + side
            to = v0.at[c, 2 if low else 7]
            to[22:24, :], to[16:18, :] = get_rows(r1e, r1o, up, inner, 56 + 6 + n // 2, 2 * (n % 2), 2)
            for k in range(2):
                to = v0.at[c, k if low else 8 + k]
                to[0:16, :] = halo_plane(ge, go, even, inside, low, 2 * c + k)
            k = 1 if low else 0
            to = v0.at[c, 1 if low else 8]
            to[23:24, :] = get_extra(ge, go, even, inside, low, (c * 2 + k) * 2, 1)
            to[16:17, :] = get_extra(ge, go, even, inside, low, (c * 2 + k) * 2 + 1, 1)
    for p in range(4):
        to = clip_x.at[p + 3]
        to[0:16, :] = clip[p].astype(F32)
        to[21:24, :], to[16:19, :] = get_rows(be, bo, up, inner, 36 + p, 0, 3)
    for side in range(2):
        low = side == 0
        for k in range(3):
            to = clip_x.at[k if low else 7 + k]
            to[0:16, :] = halo_plane(ge, go, even, inside, low, 6 + k + (1 if low else 0))
        to = clip_x.at[2 if low else 7]
        n = 12 + 4 * (3 if low else 0)
        to[22:24, :] = get_extra(ge, go, even, inside, low, n, 2)
        to[16:18, :] = get_extra(ge, go, even, inside, low, n + 2, 2)
        n = 12 + 4 * (2 if low else 1)
        to = clip_x.at[1 if low else 8]
        to[23:24, :] = get_extra(ge, go, even, inside, low, n + 1, 1)
        to[16:17, :] = get_extra(ge, go, even, inside, low, n + 2, 1)


def finish(
    pos, held, mid2, other, force_x, kinv_x, obst_x, clip_x, main, cross,
    moved, residual, v0, v1, v2, mid_x, fine,
):
    par = jnp.bitwise_and(pos[0], 1)
    i, j = rows((128, 256)), lanes((128, 256))
    copy = jnp.where(lax.shift_right_logical(j, 1) == i, 1.0, 0.0)
    for c in range(3):
        mid_x[c, pl.ds(2 * par, 4)] = mid2[c]
        mid_x[c, pl.ds(4 * (1 - par), 2)] = other[c]
    wide = jnp.dot(
        mid_x[...].reshape(3 * 6 * 16, 128), copy, precision=HIGH, preferred_element_type=F32
    )
    for c in range(3):
        for k in range(6):
            x = wide[(c * 6 + k) * 16 : (c * 6 + k) * 16 + 16]
            for h in range(2):
                y = x[:, 128 * h : 128 * h + 128]
                fine[h, pl.ds(0, 16, 2), :] = y
                fine[h, pl.ds(1, 16, 2), :] = y
            up2 = jnp.concatenate([fine[0, 0:24, :], fine[1, 0:24, :]], 1)
            for p in range(10):
                if (p + 1) // 2 == k:
                    add = jnp.where(clip_x[p] == 1.0, 0.0, up2) if c == 0 else up2
                    v0[c, p] = held[c, p] + add
    smooth(v0, force_x, kinv_x, obst_x, v1, v2)
    for p in range(4):
        out = residual_plane(v2, force_x, main, cross, p)
        for c in range(3):
            residual[c, p] = out[c]
            moved[c, p] = v2[c, p + 1, 0:16, :]


def call(kernel, outs, scratch, *args, limit=0):
    vm = pl.BlockSpec(memory_space=pltpu.VMEM)
    source = pl.BlockSpec(memory_space=pltpu.HBM) if limit else vm
    return pl.pallas_call(
        kernel,
        out_shape=[jax.ShapeDtypeStruct(x, F32) for x in outs],
        in_specs=[pl.BlockSpec(memory_space=pltpu.SMEM)] + [source] * (len(args) - 1),
        out_specs=[vm] * len(outs),
        scratch_shapes=[pltpu.VMEM(x, F32) if isinstance(x, tuple) else x for x in scratch],
        compiler_params=pltpu.CompilerParams(vmem_limit_bytes=limit or 32 * 1024 * 1024),
    )(*args)


EVEN = [(i, i ^ 1) for i in range(16)]
ODD = [(i, (((i + 1) ^ 1) - 1) % 16) for i in range(16)]


def swap_even(x, axis):
    return lax.ppermute(x, axis, EVEN)


def swap_odd(x, axis):
    return lax.ppermute(x, axis, ODD)


def local(disp, trac, heat, main, cross, clear, touch, clip):
    pos = jnp.stack([lax.axis_index("grp"), lax.axis_index("brick")]).astype(jnp.int32)
    own, vec, six = (4, 16, 256), (3, 4, 16, 256), (6, 4, 16, 256)
    kinv, obst, me, mo, be, bo, k0 = call(
        load_pack,
        [six, own, (35, 16, 256), (32, 16, 256), (40, 8, 128), (40, 8, 128), (12, 8, 128)],
        [vec, vec, own, vec, vec, own, pltpu.VMEM(own, jnp.int32), pltpu.VMEM(own, jnp.int32),
         (12, 2, 16, 128), (96, 256), pltpu.SemaphoreType.DMA((8,))],
        pos, *[pltpu.with_memory_space_constraint(z, pltpu.HBM) for z in (disp, trac, heat, main, cross, clear, touch, clip)], limit=32 * 1024 * 1024,
    )
    re, ro = swap_even(me, "grp"), swap_odd(mo, "grp")
    re_b, ro_b = swap_even(be, "brick"), swap_odd(bo, "brick")
    ce, co, k01 = call(pack_corner, [(13, 8, 128)] * 2 + [(24, 8, 128)], [], pos, re, ro, k0)
    re_c, ro_c = swap_even(ce, "brick"), swap_odd(co, "brick")
    k23 = swap_odd(k01, "grp")
    force_x, kinv_x, obst_x, pre, b0, planes, pe, po = call(
        presmooth,
        [(3, 8, 24, 256), (6, 8, 24, 256), (8, 24, 256), (3, 6, 24, 256), (8, 8, 128),
         (12, 16, 256), (9, 8, 128), (9, 8, 128)],
        [(3, 10, 24, 256), (10, 24, 256), (3, 8, 24, 256), (4, 2, 16, 128), (64, 256)],
        pos, disp, heat, clip, trac, kinv, obst, main, cross, clear, touch,
        re, ro, re_b, ro_b, re_c, ro_c,
    )
    eb = swap_even(jnp.concatenate([b0, k23], 0), "grp")
    ob = swap_odd(jnp.concatenate([b0, eb], 0), "grp")
    ge, go = swap_even(planes, "grp"), swap_odd(planes, "grp")
    after, go = lax.optimization_barrier((b0, go))
    r1e = swap_even(jnp.concatenate([after, k01, k23, pe], 0), "brick")
    r1o = swap_odd(jnp.concatenate([after, k01, k23, po], 0), "brick")
    after, ge = lax.optimization_barrier((eb, ge))
    middle = jnp.concatenate([after, ob], 0)
    rme, rmo = swap_even(middle, "brick"), swap_odd(middle, "brick")
    b3 = swap_even(ob[:16], "grp")
    b4 = swap_odd(b3, "grp")
    last = jnp.concatenate([b3, b4], 0)
    r2e, r2o = swap_even(last, "brick"), swap_odd(last, "brick")
    field, third = (3, 16, 24, 128), (3, 8, 24, 128)
    gk, ki, k3 = call(
        coarse_blocks,
        [(6, 16, 24, 128), (6, 16, 24, 128), (6, 8, 24, 128)],
        [],
        pos, eb, ob, k01, k23, r1e, r1o, rme, rmo,
    )
    mid2, mine = call(
        coarse,
        [(3, 4, 16, 128), (3, 2, 16, 128)],
        [(4, 16, 24, 128), field, field, third, (8, 24, 128), third],
        pos, b0, eb, ob, b3, b4, r1e, r1o, rme, rmo, r2e, r2o, gk, ki, k3,
    )
    other = swap_even(mine, "grp")
    held, clip_x = call(
        gather_pre, [(3, 10, 24, 256), (10, 24, 256)], [],
        pos, pre, ge, go, r1e, r1o, re_b, ro_b, clip,
    )
    return tuple(
        call(
            finish,
            [vec, vec],
            [(3, 10, 24, 256), (3, 8, 24, 256), (3, 6, 24, 256), (3, 6, 16, 128), (2, 32, 128)],
            pos, held, mid2, other, force_x, kinv_x, obst_x, clip_x, main, cross,
        )
    )


def solution(mesh):
    vector, scalar = P(None, "grp", "brick", None), P("grp", "brick", None)
    return jax.shard_map(
        local,
        mesh=mesh,
        in_specs=(vector, vector, scalar, vector, vector, scalar, scalar, scalar),
        out_specs=(vector, vector),
        check_vma=False,
    )
```

```python
import jax
import jax.numpy as jnp
from jax import lax
from jax.experimental import pallas as pl
from jax.experimental.pallas import tpu as pltpu
from jax.sharding import PartitionSpec as P

OMEGA = 0.6
KEEP = 0.4
FREE = 1000.0
F32 = jnp.float32
HIGH = lax.Precision.HIGHEST
EVEN_SLOTS = (4, 5, 3, 2, 6, 7, 1, 0)


def inverse(a, b, c, d, e, f):
    i00 = b * c - e * e
    i11 = a * c - f * f
    i22 = a * b - d * d
    i01 = f * e - d * c
    i12 = d * f - a * e
    i02 = d * e - b * f
    det = a * i00 + d * i01 + f * i02
    scale = jnp.where(det == 0.0, 0.0, 1.0 / jnp.where(det == 0.0, 1.0, det))
    return [i00 * scale, i11 * scale, i22 * scale, i01 * scale, i12 * scale, i02 * scale]


def symmetric_times(m, r):
    return [
        m[0] * r[0] + m[3] * r[1] + m[5] * r[2],
        m[3] * r[0] + m[1] * r[1] + m[4] * r[2],
        m[5] * r[0] + m[4] * r[1] + m[2] * r[2],
    ]


def lanes(shape):
    return lax.broadcasted_iota(jnp.int32, shape, 1)


def rows(shape):
    return lax.broadcasted_iota(jnp.int32, shape, 0)


def beside(x, step=1):
    n, m = x.shape
    lane = lanes(x.shape)
    left = jnp.where(lane < step, 0.0, pltpu.roll(x, step, axis=1))
    right = jnp.where(lane >= m - step, 0.0, pltpu.roll(x, m - step, axis=1))
    return (left + right) + (pltpu.roll(x, step, axis=0) + pltpu.roll(x, n - step, axis=0))


def sides(g):
    return (jnp.bitwise_and(g, 1) == 0), jnp.logical_and(g > 0, g < 15)


def put(msg, t, r, x):
    n = x.shape[0]
    msg[t, r : r + n, :] = x[:, :128]
    msg[t, r + 4 : r + 4 + n, :] = x[:, 128:]


def put_rows(be, bo, up, t, r, x, n, skip=0):
    low, high = x[skip : skip + n], x[16 - skip - n : 16 - skip]
    put(be, t, r, jnp.where(up, high, low))
    put(bo, t, r, jnp.where(up, low, high))


def get_rows(be, bo, up, inside, t, r, n):
    e = jnp.concatenate([be[t, r : r + n, :], be[t, r + 4 : r + 4 + n, :]], 1)
    o = jnp.concatenate([bo[t, r : r + n, :], bo[t, r + 4 : r + 4 + n, :]], 1)
    o = jnp.where(inside, o, 0.0)
    return jnp.where(up, o, e), jnp.where(up, e, o)


def fields(disp, heat, trac, kinv, obst):
    wide = [lambda p, c=c: disp[c, p] for c in range(3)]
    wide += [lambda p: heat[p]]
    near = [lambda p, c=c: trac[c, p] for c in range(3)]
    near += [lambda p, k=k: kinv[k, p] for k in range(6)]
    near += [lambda p: obst[p]]
    return wide, near


def load_pack(
    pos, disp_h, trac_h, heat_h, main_h, cross_h, clear_h, touch_h, clip_h,
    kinv, obst, me, mo, be, bo, k0,
    disp, trac, heat, main, cross, clear, touch, clip, rest, gath, sem,
):
    pairs = [
        (main_h, main), (cross_h, cross), (clear_h, clear), (touch_h, touch),
        (disp_h, disp), (trac_h, trac), (heat_h, heat), (clip_h, clip),
    ]
    copies = [pltpu.make_async_copy(x, y, sem.at[i]) for i, (x, y) in enumerate(pairs)]
    for c in copies:
        c.start()
    par = jnp.bitwise_and(pos[0], 1)
    up = jnp.bitwise_and(pos[1], 1) == 0
    copies[0].wait()
    copies[1].wait()

    def invert(p, carry):
        inv = inverse(main[0, p], main[1, p], main[2, p], cross[0, p], cross[1, p], cross[2, p])
        for k in range(6):
            kinv[k, p] = inv[k]
        return carry

    lax.fori_loop(0, 4, invert, 0)
    for k in range(6):
        src, c = (main, k) if k < 3 else (cross, k - 3)
        for q in range(2):
            x = 0.125 * (src[c, 2 * q] + src[c, 2 * q + 1])
            gath[(2 * k + q) * 8 : (2 * k + q) * 8 + 8, :] = pair_rows(rest.at[2 * k + q], x, jnp.add)
    k0[...] = pair_lanes(gath[...]).reshape(12, 8, 128)
    copies[2].wait()
    copies[3].wait()
    obst[...] = jnp.where(touch[...] == 1, clear[...], FREE)
    for c in copies[4:]:
        c.wait()
    for msg, at in ((me, 1 - par), (mo, par)):
        for c in range(3):
            msg[3 * c : 3 * c + 3] = disp[c, pl.ds(at, 3)]
        msg[9:12] = heat[pl.ds(at, 3)]
        for c in range(3):
            msg[12 + 2 * c : 14 + 2 * c] = trac[c, pl.ds(2 * at, 2)]
        for k in range(6):
            msg[18 + 2 * k : 20 + 2 * k] = kinv[k, pl.ds(2 * at, 2)]
        msg[30:32] = obst[pl.ds(2 * at, 2)]
    for t in range(12):
        r, h = 8 * (t % 4 // 2), 128 * (t % 2)
        me[32 + t // 4, r : r + 8, h : h + 128] = k0[t]
    wide, near = fields(disp, heat, trac, kinv, obst)
    for f in range(4):
        for p in range(4):
            put_rows(be, bo, up, f * 4 + p, 0, wide[f](p), 3)
    for f in range(10):
        for p in range(4):
            put_rows(be, bo, up, 16 + f * 2 + p // 2, 2 * (p % 2), near[f](p), 2)
    for p in range(4):
        put_rows(be, bo, up, 36 + p, 0, clip[p].astype(F32), 3)


def halo_plane(re, ro, even, inside, low, k):
    e, o = re[k], jnp.where(inside, ro[k], 0.0)
    return jnp.where(even, o, e) if low else jnp.where(even, e, o)


def pack_corner(pos, re, ro, k0, be, bo, k01):
    k01[0:12] = k0[...]
    for t in range(12):
        r, h = 8 * (t % 4 // 2), 128 * (t % 2)
        k01[12 + t] = re[32 + t // 4, r : r + 8, h : h + 128]
    even, inside = sides(pos[0])
    up = jnp.bitwise_and(pos[1], 1) == 0
    for f in range(4):
        for side in range(2):
            low = side == 0
            x = halo_plane(re, ro, even, inside, low, 3 * f + (2 if low else 0))
            put_rows(be, bo, up, f * 2 + side, 0, x, 2)
            x = halo_plane(re, ro, even, inside, low, 3 * f + 1)
            put_rows(be, bo, up, f * 2 + side, 2, x, 1)
    for f in range(10):
        for side in range(2):
            low = side == 0
            n = f * 2 + side
            x = halo_plane(re, ro, even, inside, low, 12 + 2 * f + (1 if low else 0))
            put_rows(be, bo, up, 8 + n // 4, n % 4, x, 1)


def smooth(v0, force, kinv, obst, v1, v2):
    def one(src, dst, shift, planes):
        def body(p, carry):
            rest = []
            for c in range(3):
                near = src[c, p] + src[c, p + 2] + beside(src[c, p + 1])
                rest.append(force[c, p + shift] + near)
            inv = [kinv[k, p + shift] for k in range(6)]
            step = symmetric_times(inv, rest)
            new = [KEEP * src[c, p + 1] + OMEGA * step[c] for c in range(3)]
            dst[0, p] = jnp.minimum(new[0], obst[p + shift])
            dst[1, p] = new[1]
            dst[2, p] = new[2]
            return carry

        lax.fori_loop(0, planes, body, 0, unroll=4)

    one(v0, v1, 0, 8)
    one(v1, v2, 1, 6)


def residual_plane(v2, force, main, cross, p):
    own = [v2[c, p + 1][0:16] for c in range(3)]
    mat = [main[c, p] for c in range(3)] + [cross[c, p] for c in range(3)]
    kv = symmetric_times(mat, own)
    out = []
    for c in range(3):
        near = v2[c, p, 0:16, :] + v2[c, p + 2, 0:16, :] + beside(v2[c, p + 1])[0:16]
        out.append(force[c, p + 2, 0:16, :] - (kv[c] - near))
    return out


def pair_rows(room, x, op):
    for h in range(2):
        room[h] = x[:, 128 * h : 128 * h + 128]
    return jnp.concatenate(
        [op(room[h, pl.ds(0, 8, 2), :], room[h, pl.ds(1, 8, 2), :]) for h in range(2)], 1
    )


def pair_lanes(x):
    i, j = rows((256, 128)), lanes((256, 128))
    pick = jnp.where(lax.shift_right_logical(i, 1) == j, 1.0, 0.0)
    return jnp.dot(x, pick, precision=HIGH, preferred_element_type=F32)


def put_extra(planes, n, x):
    planes[10 + n // 16, n % 16 : n % 16 + x.shape[0], :] = x


def get_extra(ge, go, even, inside, low, n, m):
    e = ge[10 + n // 16, n % 16 : n % 16 + m, :]
    o = jnp.where(inside, go[10 + n // 16, n % 16 : n % 16 + m, :], 0.0)
    return jnp.where(even, o, e) if low else jnp.where(even, e, o)


def presmooth(
    pos, disp, heat, clip, trac, kinv, obst, main, cross, clear, touch,
    re, ro, be, bo, ce, co,
    force_x, kinv_x, obst_x, v2, small_out, planes_out, pe, po,
    v0, heat_x, v1, rest, gath,
):
    even, inside = sides(pos[0])
    up, inner = sides(pos[1])
    wide, near = fields(disp, heat, trac, kinv, obst)
    wide_to = [lambda p, c=c: v0.at[c, p] for c in range(3)]
    wide_to += [lambda p: heat_x.at[p]]
    near_to = [lambda p, c=c: force_x.at[c, p] for c in range(3)]
    near_to += [lambda p, k=k: kinv_x.at[k, p] for k in range(6)]
    near_to += [lambda p: obst_x.at[p]]
    for f in range(4):
        for p in range(4):
            to = wide_to[f](p + 3)
            to[0:16, :] = wide[f](p)
            to[21:24, :], to[16:19, :] = get_rows(be, bo, up, inner, f * 4 + p, 0, 3)
        for side in range(2):
            low = side == 0
            for k in range(3):
                to = wide_to[f](k if low else 7 + k)
                to[0:16, :] = halo_plane(re, ro, even, inside, low, 3 * f + k)
            to = wide_to[f](2 if low else 7)
            to[22:24, :], to[16:18, :] = get_rows(ce, co, up, inner, f * 2 + side, 0, 2)
            to = wide_to[f](1 if low else 8)
            to[23:24, :], to[16:17, :] = get_rows(ce, co, up, inner, f * 2 + side, 2, 1)
    for f in range(10):
        for p in range(4):
            to = near_to[f](p + 2)
            to[0:16, :] = near[f](p)
            to[22:24, :], to[16:18, :] = get_rows(be, bo, up, inner, 16 + f * 2 + p // 2, 2 * (p % 2), 2)
        for side in range(2):
            low = side == 0
            for k in range(2):
                to = near_to[f](k if low else 6 + k)
                to[0:16, :] = halo_plane(re, ro, even, inside, low, 12 + 2 * f + k)
            n = f * 2 + side
            to = near_to[f](1 if low else 6)
            to[23:24, :], to[16:17, :] = get_rows(ce, co, up, inner, 8 + n // 4, n % 4, 1)

    def drift(p, carry):
        h = heat_x[p + 1]
        lane = lanes(h.shape)
        right = jnp.where(lane == 255, 0.0, pltpu.roll(h, 255, axis=1))
        left = jnp.where(lane == 0, 0.0, pltpu.roll(h, 1, axis=1))
        force_x[0, p] = force_x[0, p] - (heat_x[p + 2] - heat_x[p])
        force_x[1, p] = force_x[1, p] - (pltpu.roll(h, 23, axis=0) - pltpu.roll(h, 1, axis=0))
        force_x[2, p] = force_x[2, p] - (right - left)
        return carry

    lax.fori_loop(0, 8, drift, 0, unroll=4)
    smooth(v0, force_x, kinv_x, obst_x, v1, v2)

    shape = (16, 256)
    first = jnp.bitwise_and(lanes(shape), 1) == 0
    for q in range(2):
        low = None
        for p in (2 * q, 2 * q + 1):
            out = residual_plane(v2, force_x, main, cross, p)
            cut = clip[p] == 1
            out[0] = jnp.where(cut, 0.0, out[0])
            gap = jnp.logical_and(touch[p] == 1, clip[p] != 1)
            room = jnp.where(gap, clear[p] - v2[0, p + 1, 0:16, :], FREE)
            part = out + [room]
            if low is None:
                low = part
            else:
                low = [jnp.minimum(x, y) if i == 3 else x + y for i, (x, y) in enumerate(zip(low, part))]
        for i in range(4):
            x = pair_rows(rest.at[i], low[i] if i == 3 else 0.25 * low[i], jnp.minimum if i == 3 else jnp.add)
            if i == 3:
                x = jnp.minimum(x, pltpu.roll(x, 255, axis=1))
                x = jnp.where(first[0:8], x, 0.0)
            gath[(2 * i + q) * 8 : (2 * i + q) * 8 + 8, :] = x
    small_out[...] = pair_lanes(gath[...]).reshape(8, 8, 128)
    for c in range(3):
        for k in range(2):
            planes_out[2 * c + k] = v2[c, k + 2, 0:16, :]
            for side in range(2):
                put_extra(planes_out, (c * 2 + k) * 2 + side, v2[c, k + 2, 16 if side else 23 : 17 if side else 24, :])
    for p in range(4):
        planes_out[6 + p] = clip[p].astype(F32)
        low, high = get_rows(be, bo, up, inner, 36 + p, 0, 3)
        put_extra(planes_out, 12 + 4 * p, low[1:3])
        put_extra(planes_out, 14 + 4 * p, high[0:2])
    for c in range(3):
        for p in range(4):
            put_rows(pe, po, up, c * 2 + p // 2, 2 * (p % 2), v2[c, p + 1, 0:16, :], 2, 1)
        for side in range(2):
            n = 2 * c + side
            put_rows(pe, po, up, 6 + n // 2, 2 * (n % 2), v2[c, 5 * side, 0:16, :], 2)


def pair_spread(x, op):
    n, m = x.shape
    even = jnp.bitwise_and(lanes(x.shape), 1) == 0
    x = op(x, jnp.where(even, pltpu.roll(x, m - 1, axis=1), pltpu.roll(x, 1, axis=1)))
    even = jnp.bitwise_and(rows(x.shape), 1) == 0
    return op(x, jnp.where(even, pltpu.roll(x, n - 1, axis=0), pltpu.roll(x, 1, axis=0)))


SLOTS = (
    ("b0", 0, "one", 0, "k01", 0, "one", 8), ("eb", 0, "mid", 0, "k01", 12, "one", 20),
    ("ob", 0, "mid", 32, "k23", 0, "one", 32), ("ob", 8, "mid", 40, "k23", 12, "one", 44),
    ("b3", 0, "two", 0, "eb", 8, "mid", 8), ("b3", 8, "two", 8, "eb", 20, "mid", 20),
    ("b4", 0, "two", 16, "ob", 16, "mid", 48), ("b4", 8, "two", 24, "ob", 28, "mid", 60),
)


def lay_window(pos, refs, g, force):
    par = jnp.bitwise_and(pos[0], 1)
    up, inner = sides(pos[1])
    grp = pos[0]
    for s, (mine, m, row, r, mat, k, krow, kr) in enumerate(SLOTS):
        if not force:
            mine, m, row, r = mat, k, krow, kr
        mine, (re, ro) = refs[mine], refs[row]
        place = jnp.where(par == 0, EVEN_SLOTS[s], 7 - EVEN_SLOTS[s])
        where = grp + place - jnp.where(par == 0, 4, 3)
        real = jnp.logical_and(where >= 0, where < 16)
        real_o = jnp.logical_and(real, inner)

        def fill(f, carry):
            for q in range(2):
                t = 2 * f + q
                a = jnp.where(real, re[r + t], 0.0)
                b = jnp.where(real_o, ro[r + t], 0.0)
                to = g.at[f, 2 * place + q]
                to[0:8, :] = jnp.where(real, mine[m + t], 0.0)
                to[8:16, :] = jnp.where(up, a, b)
                to[16:24, :] = jnp.where(up, b, a)
            return carry

        lax.fori_loop(0, 4 if force else 6, fill, 0, unroll=2)


def coarse_blocks(pos, eb, ob, k01, k23, r1e, r1o, rme, rmo, gk, ki, k3):
    refs = dict(eb=eb, ob=ob, k01=k01, k23=k23, one=(r1e, r1o), mid=(rme, rmo))
    lay_window(pos, refs, gk, False)

    def invert(p, carry):
        inv = inverse(*[gk[k, p] for k in range(6)])
        for k in range(6):
            ki[k, p] = inv[k]
        return carry

    lax.fori_loop(0, 16, invert, 0, unroll=4)

    def third(q, carry):
        mat = [0.125 * pair_spread(gk[k, 2 * q] + gk[k, 2 * q + 1], jnp.add) for k in range(6)]
        inv = inverse(*mat)
        for k in range(6):
            k3[k, q] = inv[k]
        return carry

    lax.fori_loop(1, 7, third, 0, unroll=2)


def coarse(
    pos, b0, eb, ob, b3, b4, r1e, r1o, rme, rmo, r2e, r2o, gk, ki, k3,
    mid2, own, g, va, vb, f3, o3, l3,
):
    par = jnp.bitwise_and(pos[0], 1)
    refs = dict(b0=b0, eb=eb, ob=ob, b3=b3, b4=b4, one=(r1e, r1o), mid=(rme, rmo), two=(r2e, r2o))
    lay_window(pos, refs, g, True)

    def start(p, carry):
        v = symmetric_times([ki[k, p] for k in range(6)], [OMEGA * g[c, p] for c in range(3)])
        va[0, p] = jnp.minimum(v[0], g[3, p])
        va[1, p] = v[1]
        va[2, p] = v[2]
        return carry

    lax.fori_loop(0, 16, start, 0, unroll=4)

    def sweep(src, dst):
        def body(p, carry):
            rest = []
            for c in range(3):
                near = src[c, p - 1] + src[c, p + 1] + beside(src[c, p])
                rest.append(g[c, p] + near)
            step = symmetric_times([ki[k, p] for k in range(6)], rest)
            new = [KEEP * src[c, p] + OMEGA * step[c] for c in range(3)]
            dst[0, p] = jnp.minimum(new[0], g[3, p])
            dst[1, p] = new[1]
            dst[2, p] = new[2]
            return carry

        return body

    lax.fori_loop(1, 15, sweep(va, vb), 0, unroll=4)

    def third(q, carry):
        total = None
        for p in (2 * q, 2 * q + 1):
            mat = [gk[k, p] for k in range(6)]
            kv = symmetric_times(mat, [vb[c, p] for c in range(3)])
            part = []
            for c in range(3):
                near = vb[c, p - 1] + vb[c, p + 1] + beside(vb[c, p])
                part.append(g[c, p] - (kv[c] - near))
            part.append(g[3, p] - vb[0, p])
            if total is None:
                total = part
            else:
                total = [jnp.minimum(x, y) if i == 3 else x + y for i, (x, y) in enumerate(zip(total, part))]
        force = [0.25 * pair_spread(total[c], jnp.add) for c in range(3)]
        room = pair_spread(total[3], jnp.minimum)
        v = symmetric_times([k3[k, q] for k in range(6)], [OMEGA * x for x in force])
        v[0] = jnp.minimum(v[0], room)
        for c in range(3):
            f3[c, q] = force[c]
            l3[c, q] = v[c]
        o3[q] = room
        return carry

    lax.fori_loop(1, 7, third, 0, unroll=4)

    def lowest(q, carry):
        rest = []
        for c in range(3):
            near = l3[c, q - 1] + l3[c, q + 1] + beside(l3[c, q], 2)
            rest.append(f3[c, q] + near)
        step = symmetric_times([k3[k, q] for k in range(6)], rest)
        new = [KEEP * l3[c, q] + OMEGA * step[c] for c in range(3)]
        new[0] = jnp.minimum(new[0], o3[q])
        for c in range(3):
            for p in (2 * q, 2 * q + 1):
                va[c, p] = vb[c, p] + new[c]
        return carry

    lax.fori_loop(2, 6, lowest, 0, unroll=4)
    lax.fori_loop(5, 11, sweep(va, vb), 0, unroll=4)
    lax.fori_loop(6, 10, sweep(vb, va), 0, unroll=4)
    for c in range(3):
        for k in range(4):
            mid2[c, k, 0:10, :] = va[c, 6 + k, 0:10, :]
            mid2[c, k, 10:12, :] = va[c, 6 + k, 22:24, :]
        for k in range(2):
            own[c, k, 0:10, :] = va[c, 8 - 2 * par + k, 0:10, :]
            own[c, k, 10:12, :] = va[c, 8 - 2 * par + k, 22:24, :]


def gather_pre(pos, pre, ge, go, r1e, r1o, be, bo, clip, v0, clip_x):
    even, inside = sides(pos[0])
    up, inner = sides(pos[1])
    for c in range(3):
        for p in range(6):
            v0[c, p + 2] = pre[c, p]
        for p in range(4):
            to = v0.at[c, p + 3]
            to[21:23, :], to[17:19, :] = get_rows(r1e, r1o, up, inner, 56 + c * 2 + p // 2, 2 * (p % 2), 2)
        for side in range(2):
            low = side == 0
            n = 2 * c + side
            to = v0.at[c, 2 if low else 7]
            to[22:24, :], to[16:18, :] = get_rows(r1e, r1o, up, inner, 56 + 6 + n // 2, 2 * (n % 2), 2)
            for k in range(2):
                to = v0.at[c, k if low else 8 + k]
                to[0:16, :] = halo_plane(ge, go, even, inside, low, 2 * c + k)
            k = 1 if low else 0
            to = v0.at[c, 1 if low else 8]
            to[23:24, :] = get_extra(ge, go, even, inside, low, (c * 2 + k) * 2, 1)
            to[16:17, :] = get_extra(ge, go, even, inside, low, (c * 2 + k) * 2 + 1, 1)
    for p in range(4):
        to = clip_x.at[p + 3]
        to[0:16, :] = clip[p].astype(F32)
        to[21:24, :], to[16:19, :] = get_rows(be, bo, up, inner, 36 + p, 0, 3)
    for side in range(2):
        low = side == 0
        for k in range(3):
            to = clip_x.at[k if low else 7 + k]
            to[0:16, :] = halo_plane(ge, go, even, inside, low, 6 + k + (1 if low else 0))
        to = clip_x.at[2 if low else 7]
        n = 12 + 4 * (3 if low else 0)
        to[22:24, :] = get_extra(ge, go, even, inside, low, n, 2)
        to[16:18, :] = get_extra(ge, go, even, inside, low, n + 2, 2)
        n = 12 + 4 * (2 if low else 1)
        to = clip_x.at[1 if low else 8]
        to[23:24, :] = get_extra(ge, go, even, inside, low, n + 1, 1)
        to[16:17, :] = get_extra(ge, go, even, inside, low, n + 2, 1)


def finish(
    pos, held, mid2, other, force_x, kinv_x, obst_x, clip_x, main, cross,
    moved, residual, v0, v1, v2, mid_x, fine,
):
    par = jnp.bitwise_and(pos[0], 1)
    i, j = rows((128, 256)), lanes((128, 256))
    copy = jnp.where(lax.shift_right_logical(j, 1) == i, 1.0, 0.0)
    for c in range(3):
        mid_x[c, pl.ds(2 * par, 4)] = mid2[c]
        mid_x[c, pl.ds(4 * (1 - par), 2)] = other[c]
    wide = jnp.dot(
        mid_x[...].reshape(3 * 6 * 16, 128), copy, precision=HIGH, preferred_element_type=F32
    )
    for c in range(3):
        for k in range(6):
            x = wide[(c * 6 + k) * 16 : (c * 6 + k) * 16 + 16]
            for h in range(2):
                y = x[:, 128 * h : 128 * h + 128]
                fine[h, pl.ds(0, 16, 2), :] = y
                fine[h, pl.ds(1, 16, 2), :] = y
            up2 = jnp.concatenate([fine[0, 0:24, :], fine[1, 0:24, :]], 1)
            for p in range(10):
                if (p + 1) // 2 == k:
                    add = jnp.where(clip_x[p] == 1.0, 0.0, up2) if c == 0 else up2
                    v0[c, p] = held[c, p] + add
    smooth(v0, force_x, kinv_x, obst_x, v1, v2)
    for p in range(4):
        out = residual_plane(v2, force_x, main, cross, p)
        for c in range(3):
            residual[c, p] = out[c]
            moved[c, p] = v2[c, p + 1, 0:16, :]


def call(kernel, outs, scratch, *args, limit=0):
    vm = pl.BlockSpec(memory_space=pltpu.VMEM)
    source = pl.BlockSpec(memory_space=pltpu.HBM) if limit else vm
    return pl.pallas_call(
        kernel,
        out_shape=[jax.ShapeDtypeStruct(x, F32) for x in outs],
        in_specs=[pl.BlockSpec(memory_space=pltpu.SMEM)] + [source] * (len(args) - 1),
        out_specs=[vm] * len(outs),
        scratch_shapes=[pltpu.VMEM(x, F32) if isinstance(x, tuple) else x for x in scratch],
        compiler_params=pltpu.CompilerParams(vmem_limit_bytes=limit or 32 * 1024 * 1024),
    )(*args)


EVEN = [(i, i ^ 1) for i in range(16)]
ODD = [(i, (((i + 1) ^ 1) - 1) % 16) for i in range(16)]


def swap_even(x, axis):
    return lax.ppermute(x, axis, EVEN)


def swap_odd(x, axis):
    return lax.ppermute(x, axis, ODD)


def local(disp, trac, heat, main, cross, clear, touch, clip):
    pos = jnp.stack([lax.axis_index("grp"), lax.axis_index("brick")]).astype(jnp.int32)
    own, vec, six = (4, 16, 256), (3, 4, 16, 256), (6, 4, 16, 256)
    kinv, obst, me, mo, be, bo, k0 = call(
        load_pack,
        [six, own, (35, 16, 256), (32, 16, 256), (40, 8, 128), (40, 8, 128), (12, 8, 128)],
        [vec, vec, own, vec, vec, own, pltpu.VMEM(own, jnp.int32), pltpu.VMEM(own, jnp.int32),
         (12, 2, 16, 128), (96, 256), pltpu.SemaphoreType.DMA((8,))],
        pos, *[pltpu.with_memory_space_constraint(z, pltpu.HBM) for z in (disp, trac, heat, main, cross, clear, touch, clip)], limit=32 * 1024 * 1024,
    )
    re, ro = swap_even(me, "grp"), swap_odd(mo, "grp")
    re_b, ro_b = swap_even(be, "brick"), swap_odd(bo, "brick")
    ce, co, k01 = call(pack_corner, [(13, 8, 128)] * 2 + [(24, 8, 128)], [], pos, re, ro, k0)
    re_c, ro_c = swap_even(ce, "brick"), swap_odd(co, "brick")
    k23 = swap_odd(k01, "grp")
    force_x, kinv_x, obst_x, pre, b0, planes, pe, po = call(
        presmooth,
        [(3, 8, 24, 256), (6, 8, 24, 256), (8, 24, 256), (3, 6, 24, 256), (8, 8, 128),
         (12, 16, 256), (9, 8, 128), (9, 8, 128)],
        [(3, 10, 24, 256), (10, 24, 256), (3, 8, 24, 256), (4, 2, 16, 128), (64, 256)],
        pos, disp, heat, clip, trac, kinv, obst, main, cross, clear, touch,
        re, ro, re_b, ro_b, re_c, ro_c,
    )
    eb = swap_even(jnp.concatenate([b0, k23], 0), "grp")
    ob = swap_odd(jnp.concatenate([b0, eb], 0), "grp")
    ge, go = swap_even(planes, "grp"), swap_odd(planes, "grp")
    after, go = lax.optimization_barrier((b0, go))
    r1e = swap_even(jnp.concatenate([after, k01, k23, pe], 0), "brick")
    r1o = swap_odd(jnp.concatenate([after, k01, k23, po], 0), "brick")
    after, ge = lax.optimization_barrier((eb, ge))
    middle = jnp.concatenate([after, ob], 0)
    rme, rmo = swap_even(middle, "brick"), swap_odd(middle, "brick")
    b3 = swap_even(ob[:16], "grp")
    b4 = swap_odd(b3, "grp")
    last = jnp.concatenate([b3, b4], 0)
    r2e, r2o = swap_even(last, "brick"), swap_odd(last, "brick")
    field, third = (3, 16, 24, 128), (3, 8, 24, 128)
    gk, ki, k3 = call(
        coarse_blocks,
        [(6, 16, 24, 128), (6, 16, 24, 128), (6, 8, 24, 128)],
        [],
        pos, eb, ob, k01, k23, r1e, r1o, rme, rmo,
    )
    mid2, mine = call(
        coarse,
        [(3, 4, 16, 128), (3, 2, 16, 128)],
        [(4, 16, 24, 128), field, field, third, (8, 24, 128), third],
        pos, b0, eb, ob, b3, b4, r1e, r1o, rme, rmo, r2e, r2o, gk, ki, k3,
    )
    other = swap_even(mine, "grp")
    held, clip_x = call(
        gather_pre, [(3, 10, 24, 256), (10, 24, 256)], [],
        pos, pre, ge, go, r1e, r1o, re_b, ro_b, clip,
    )
    return tuple(
        call(
            finish,
            [vec, vec],
            [(3, 10, 24, 256), (3, 8, 24, 256), (3, 6, 24, 256), (3, 6, 16, 128), (2, 32, 128)],
            pos, held, mid2, other, force_x, kinv_x, obst_x, clip_x, main, cross,
        )
    )


def solution(mesh):
    vector, scalar = P(None, "grp", "brick", None), P("grp", "brick", None)
    return jax.shard_map(
        local,
        mesh=mesh,
        in_specs=(vector, vector, scalar, vector, vector, scalar, scalar, scalar),
        out_specs=(vector, vector),
        check_vma=False,
    )
```

```python
import jax
import jax.numpy as jnp
from jax import lax
from jax.experimental import pallas as pl
from jax.experimental.pallas import tpu as pltpu
from jax.sharding import PartitionSpec as P

OMEGA = 0.6
KEEP = 0.4
FREE = 1000.0
F32 = jnp.float32
HIGH = lax.Precision.HIGHEST
EVEN_SLOTS = (4, 5, 3, 2, 6, 7, 1, 0)


def inverse(a, b, c, d, e, f):
    i00 = b * c - e * e
    i11 = a * c - f * f
    i22 = a * b - d * d
    i01 = f * e - d * c
    i12 = d * f - a * e
    i02 = d * e - b * f
    det = a * i00 + d * i01 + f * i02
    scale = jnp.where(det == 0.0, 0.0, 1.0 / jnp.where(det == 0.0, 1.0, det))
    return [i00 * scale, i11 * scale, i22 * scale, i01 * scale, i12 * scale, i02 * scale]


def symmetric_times(m, r):
    return [
        m[0] * r[0] + m[3] * r[1] + m[5] * r[2],
        m[3] * r[0] + m[1] * r[1] + m[4] * r[2],
        m[5] * r[0] + m[4] * r[1] + m[2] * r[2],
    ]


def lanes(shape):
    return lax.broadcasted_iota(jnp.int32, shape, 1)


def rows(shape):
    return lax.broadcasted_iota(jnp.int32, shape, 0)


def beside(x, step=1):
    n, m = x.shape
    lane = lanes(x.shape)
    left = jnp.where(lane < step, 0.0, pltpu.roll(x, step, axis=1))
    right = jnp.where(lane >= m - step, 0.0, pltpu.roll(x, m - step, axis=1))
    return (left + right) + (pltpu.roll(x, step, axis=0) + pltpu.roll(x, n - step, axis=0))


def sides(g):
    return (jnp.bitwise_and(g, 1) == 0), jnp.logical_and(g > 0, g < 15)


def put(msg, t, r, x):
    n = x.shape[0]
    msg[t, r : r + n, :] = x[:, :128]
    msg[t, r + 4 : r + 4 + n, :] = x[:, 128:]


def put_rows(be, bo, up, t, r, x, n, skip=0):
    low, high = x[skip : skip + n], x[16 - skip - n : 16 - skip]
    put(be, t, r, jnp.where(up, high, low))
    put(bo, t, r, jnp.where(up, low, high))


def get_rows(be, bo, up, inside, t, r, n):
    e = jnp.concatenate([be[t, r : r + n, :], be[t, r + 4 : r + 4 + n, :]], 1)
    o = jnp.concatenate([bo[t, r : r + n, :], bo[t, r + 4 : r + 4 + n, :]], 1)
    o = jnp.where(inside, o, 0.0)
    return jnp.where(up, o, e), jnp.where(up, e, o)


def fields(disp, heat, trac, kinv, obst):
    wide = [lambda p, c=c: disp[c, p] for c in range(3)]
    wide += [lambda p: heat[p]]
    near = [lambda p, c=c: trac[c, p] for c in range(3)]
    near += [lambda p, k=k: kinv[k, p] for k in range(6)]
    near += [lambda p: obst[p]]
    return wide, near


def load_pack(
    pos, disp_h, trac_h, heat_h, main_h, cross_h, clear_h, touch_h, clip_h,
    kinv, obst, me, mo, be, bo, k0,
    disp, trac, heat, main, cross, clear, touch, clip, rest, gath, sem,
):
    pairs = [
        (main_h, main), (cross_h, cross), (clear_h, clear), (touch_h, touch),
        (disp_h, disp), (trac_h, trac), (heat_h, heat), (clip_h, clip),
    ]
    copies = [pltpu.make_async_copy(x, y, sem.at[i]) for i, (x, y) in enumerate(pairs)]
    for c in copies:
        c.start()
    par = jnp.bitwise_and(pos[0], 1)
    up = jnp.bitwise_and(pos[1], 1) == 0
    copies[0].wait()
    copies[1].wait()

    def invert(p, carry):
        inv = inverse(main[0, p], main[1, p], main[2, p], cross[0, p], cross[1, p], cross[2, p])
        for k in range(6):
            kinv[k, p] = inv[k]
        return carry

    lax.fori_loop(0, 4, invert, 0)
    for k in range(6):
        src, c = (main, k) if k < 3 else (cross, k - 3)
        for q in range(2):
            x = 0.125 * (src[c, 2 * q] + src[c, 2 * q + 1])
            gath[(2 * k + q) * 8 : (2 * k + q) * 8 + 8, :] = pair_rows(rest.at[2 * k + q], x, jnp.add)
    k0[...] = pair_lanes(gath[...]).reshape(12, 8, 128)
    copies[2].wait()
    copies[3].wait()
    obst[...] = jnp.where(touch[...] == 1, clear[...], FREE)
    for c in copies[4:]:
        c.wait()
    for msg, at in ((me, 1 - par), (mo, par)):
        for c in range(3):
            msg[3 * c : 3 * c + 3] = disp[c, pl.ds(at, 3)]
        msg[9:12] = heat[pl.ds(at, 3)]
        for c in range(3):
            msg[12 + 2 * c : 14 + 2 * c] = trac[c, pl.ds(2 * at, 2)]
        for k in range(6):
            msg[18 + 2 * k : 20 + 2 * k] = kinv[k, pl.ds(2 * at, 2)]
        msg[30:32] = obst[pl.ds(2 * at, 2)]
    for t in range(12):
        r, h = 8 * (t % 4 // 2), 128 * (t % 2)
        me[32 + t // 4, r : r + 8, h : h + 128] = k0[t]
    wide, near = fields(disp, heat, trac, kinv, obst)
    for f in range(4):
        for p in range(4):
            put_rows(be, bo, up, f * 4 + p, 0, wide[f](p), 3)
    for f in range(10):
        for p in range(4):
            put_rows(be, bo, up, 16 + f * 2 + p // 2, 2 * (p % 2), near[f](p), 2)
    for p in range(4):
        put_rows(be, bo, up, 36 + p, 0, clip[p].astype(F32), 3)


def halo_plane(re, ro, even, inside, low, k):
    e, o = re[k], jnp.where(inside, ro[k], 0.0)
    return jnp.where(even, o, e) if low else jnp.where(even, e, o)


def pack_corner(pos, re, ro, k0, be, bo, k01):
    k01[0:12] = k0[...]
    for t in range(12):
        r, h = 8 * (t % 4 // 2), 128 * (t % 2)
        k01[12 + t] = re[32 + t // 4, r : r + 8, h : h + 128]
    even, inside = sides(pos[0])
    up = jnp.bitwise_and(pos[1], 1) == 0
    for f in range(4):
        for side in range(2):
            low = side == 0
            x = halo_plane(re, ro, even, inside, low, 3 * f + (2 if low else 0))
            put_rows(be, bo, up, f * 2 + side, 0, x, 2)
            x = halo_plane(re, ro, even, inside, low, 3 * f + 1)
            put_rows(be, bo, up, f * 2 + side, 2, x, 1)
    for f in range(10):
        for side in range(2):
            low = side == 0
            n = f * 2 + side
            x = halo_plane(re, ro, even, inside, low, 12 + 2 * f + (1 if low else 0))
            put_rows(be, bo, up, 8 + n // 4, n % 4, x, 1)


def smooth(v0, force, kinv, obst, v1, v2):
    def one(src, dst, shift, planes):
        def body(p, carry):
            rest = []
            for c in range(3):
                near = src[c, p] + src[c, p + 2] + beside(src[c, p + 1])
                rest.append(force[c, p + shift] + near)
            inv = [kinv[k, p + shift] for k in range(6)]
            step = symmetric_times(inv, rest)
            new = [KEEP * src[c, p + 1] + OMEGA * step[c] for c in range(3)]
            dst[0, p] = jnp.minimum(new[0], obst[p + shift])
            dst[1, p] = new[1]
            dst[2, p] = new[2]
            return carry

        lax.fori_loop(0, planes, body, 0, unroll=4)

    one(v0, v1, 0, 8)
    one(v1, v2, 1, 6)


def residual_plane(v2, force, main, cross, p):
    own = [v2[c, p + 1][0:16] for c in range(3)]
    mat = [main[c, p] for c in range(3)] + [cross[c, p] for c in range(3)]
    kv = symmetric_times(mat, own)
    out = []
    for c in range(3):
        near = v2[c, p, 0:16, :] + v2[c, p + 2, 0:16, :] + beside(v2[c, p + 1])[0:16]
        out.append(force[c, p + 2, 0:16, :] - (kv[c] - near))
    return out


def pair_rows(room, x, op):
    for h in range(2):
        room[h] = x[:, 128 * h : 128 * h + 128]
    return jnp.concatenate(
        [op(room[h, pl.ds(0, 8, 2), :], room[h, pl.ds(1, 8, 2), :]) for h in range(2)], 1
    )


def pair_lanes(x):
    i, j = rows((256, 128)), lanes((256, 128))
    pick = jnp.where(lax.shift_right_logical(i, 1) == j, 1.0, 0.0)
    return jnp.dot(x, pick, precision=HIGH, preferred_element_type=F32)


def put_extra(planes, n, x):
    planes[10 + n // 16, n % 16 : n % 16 + x.shape[0], :] = x


def get_extra(ge, go, even, inside, low, n, m):
    e = ge[10 + n // 16, n % 16 : n % 16 + m, :]
    o = jnp.where(inside, go[10 + n // 16, n % 16 : n % 16 + m, :], 0.0)
    return jnp.where(even, o, e) if low else jnp.where(even, e, o)


def presmooth(
    pos, disp, heat, clip, trac, kinv, obst, main, cross, clear, touch,
    re, ro, be, bo, ce, co,
    force_x, kinv_x, obst_x, v2, small_out, planes_out, pe, po,
    v0, heat_x, v1, rest, gath,
):
    even, inside = sides(pos[0])
    up, inner = sides(pos[1])
    wide, near = fields(disp, heat, trac, kinv, obst)
    wide_to = [lambda p, c=c: v0.at[c, p] for c in range(3)]
    wide_to += [lambda p: heat_x.at[p]]
    near_to = [lambda p, c=c: force_x.at[c, p] for c in range(3)]
    near_to += [lambda p, k=k: kinv_x.at[k, p] for k in range(6)]
    near_to += [lambda p: obst_x.at[p]]
    for f in range(4):
        for p in range(4):
            to = wide_to[f](p + 3)
            to[0:16, :] = wide[f](p)
            to[21:24, :], to[16:19, :] = get_rows(be, bo, up, inner, f * 4 + p, 0, 3)
        for side in range(2):
            low = side == 0
            for k in range(3):
                to = wide_to[f](k if low else 7 + k)
                to[0:16, :] = halo_plane(re, ro, even, inside, low, 3 * f + k)
            to = wide_to[f](2 if low else 7)
            to[22:24, :], to[16:18, :] = get_rows(ce, co, up, inner, f * 2 + side, 0, 2)
            to = wide_to[f](1 if low else 8)
            to[23:24, :], to[16:17, :] = get_rows(ce, co, up, inner, f * 2 + side, 2, 1)
    for f in range(10):
        for p in range(4):
            to = near_to[f](p + 2)
            to[0:16, :] = near[f](p)
            to[22:24, :], to[16:18, :] = get_rows(be, bo, up, inner, 16 + f * 2 + p // 2, 2 * (p % 2), 2)
        for side in range(2):
            low = side == 0
            for k in range(2):
                to = near_to[f](k if low else 6 + k)
                to[0:16, :] = halo_plane(re, ro, even, inside, low, 12 + 2 * f + k)
            n = f * 2 + side
            to = near_to[f](1 if low else 6)
            to[23:24, :], to[16:17, :] = get_rows(ce, co, up, inner, 8 + n // 4, n % 4, 1)

    def drift(p, carry):
        h = heat_x[p + 1]
        lane = lanes(h.shape)
        right = jnp.where(lane == 255, 0.0, pltpu.roll(h, 255, axis=1))
        left = jnp.where(lane == 0, 0.0, pltpu.roll(h, 1, axis=1))
        force_x[0, p] = force_x[0, p] - (heat_x[p + 2] - heat_x[p])
        force_x[1, p] = force_x[1, p] - (pltpu.roll(h, 23, axis=0) - pltpu.roll(h, 1, axis=0))
        force_x[2, p] = force_x[2, p] - (right - left)
        return carry

    lax.fori_loop(0, 8, drift, 0, unroll=4)
    smooth(v0, force_x, kinv_x, obst_x, v1, v2)

    shape = (16, 256)
    first = jnp.bitwise_and(lanes(shape), 1) == 0
    for q in range(2):
        low = None
        for p in (2 * q, 2 * q + 1):
            out = residual_plane(v2, force_x, main, cross, p)
            cut = clip[p] == 1
            out[0] = jnp.where(cut, 0.0, out[0])
            gap = jnp.logical_and(touch[p] == 1, clip[p] != 1)
            room = jnp.where(gap, clear[p] - v2[0, p + 1, 0:16, :], FREE)
            part = out + [room]
            if low is None:
                low = part
            else:
                low = [jnp.minimum(x, y) if i == 3 else x + y for i, (x, y) in enumerate(zip(low, part))]
        for i in range(4):
            x = pair_rows(rest.at[i], low[i] if i == 3 else 0.25 * low[i], jnp.minimum if i == 3 else jnp.add)
            if i == 3:
                x = jnp.minimum(x, pltpu.roll(x, 255, axis=1))
                x = jnp.where(first[0:8], x, 0.0)
            gath[(2 * i + q) * 8 : (2 * i + q) * 8 + 8, :] = x
    small_out[...] = pair_lanes(gath[...]).reshape(8, 8, 128)
    for c in range(3):
        for k in range(2):
            planes_out[2 * c + k] = v2[c, k + 2, 0:16, :]
            for side in range(2):
                put_extra(planes_out, (c * 2 + k) * 2 + side, v2[c, k + 2, 16 if side else 23 : 17 if side else 24, :])
    for p in range(4):
        planes_out[6 + p] = clip[p].astype(F32)
        low, high = get_rows(be, bo, up, inner, 36 + p, 0, 3)
        put_extra(planes_out, 12 + 4 * p, low[1:3])
        put_extra(planes_out, 14 + 4 * p, high[0:2])
    for c in range(3):
        for p in range(4):
            put_rows(pe, po, up, c * 2 + p // 2, 2 * (p % 2), v2[c, p + 1, 0:16, :], 2, 1)
        for side in range(2):
            n = 2 * c + side
            put_rows(pe, po, up, 6 + n // 2, 2 * (n % 2), v2[c, 5 * side, 0:16, :], 2)


def pair_spread(x, op):
    n, m = x.shape
    even = jnp.bitwise_and(lanes(x.shape), 1) == 0
    x = op(x, jnp.where(even, pltpu.roll(x, m - 1, axis=1), pltpu.roll(x, 1, axis=1)))
    even = jnp.bitwise_and(rows(x.shape), 1) == 0
    return op(x, jnp.where(even, pltpu.roll(x, n - 1, axis=0), pltpu.roll(x, 1, axis=0)))


SLOTS = (
    ("b0", 0, "one", 0, "k01", 0, "one", 8), ("eb", 0, "mid", 0, "k01", 12, "one", 20),
    ("ob", 0, "mid", 32, "k23", 0, "one", 32), ("ob", 8, "mid", 40, "k23", 12, "one", 44),
    ("b3", 0, "two", 0, "eb", 8, "mid", 8), ("b3", 8, "two", 8, "eb", 20, "mid", 20),
    ("b4", 0, "two", 16, "ob", 16, "mid", 48), ("b4", 8, "two", 24, "ob", 28, "mid", 60),
)


def lay_window(pos, refs, g, force):
    par = jnp.bitwise_and(pos[0], 1)
    up, inner = sides(pos[1])
    grp = pos[0]
    for s, (mine, m, row, r, mat, k, krow, kr) in enumerate(SLOTS):
        if not force:
            mine, m, row, r = mat, k, krow, kr
        mine, (re, ro) = refs[mine], refs[row]
        place = jnp.where(par == 0, EVEN_SLOTS[s], 7 - EVEN_SLOTS[s])
        where = grp + place - jnp.where(par == 0, 4, 3)
        real = jnp.logical_and(where >= 0, where < 16)
        real_o = jnp.logical_and(real, inner)

        def fill(f, carry):
            for q in range(2):
                t = 2 * f + q
                a = jnp.where(real, re[r + t], 0.0)
                b = jnp.where(real_o, ro[r + t], 0.0)
                to = g.at[f, 2 * place + q]
                to[0:8, :] = jnp.where(real, mine[m + t], 0.0)
                to[8:16, :] = jnp.where(up, a, b)
                to[16:24, :] = jnp.where(up, b, a)
            return carry

        lax.fori_loop(0, 4 if force else 6, fill, 0, unroll=True)


def coarse_blocks(pos, eb, ob, k01, k23, r1e, r1o, rme, rmo, gk, ki, k3):
    refs = dict(eb=eb, ob=ob, k01=k01, k23=k23, one=(r1e, r1o), mid=(rme, rmo))
    lay_window(pos, refs, gk, False)

    def invert(p, carry):
        inv = inverse(*[gk[k, p] for k in range(6)])
        for k in range(6):
            ki[k, p] = inv[k]
        return carry

    lax.fori_loop(0, 16, invert, 0, unroll=4)

    def third(q, carry):
        mat = [0.125 * pair_spread(gk[k, 2 * q] + gk[k, 2 * q + 1], jnp.add) for k in range(6)]
        inv = inverse(*mat)
        for k in range(6):
            k3[k, q] = inv[k]
        return carry

    lax.fori_loop(1, 7, third, 0, unroll=2)


def coarse(
    pos, b0, eb, ob, b3, b4, r1e, r1o, rme, rmo, r2e, r2o, gk, ki, k3,
    mid2, own, g, va, vb, f3, o3, l3,
):
    par = jnp.bitwise_and(pos[0], 1)
    refs = dict(b0=b0, eb=eb, ob=ob, b3=b3, b4=b4, one=(r1e, r1o), mid=(rme, rmo), two=(r2e, r2o))
    lay_window(pos, refs, g, True)

    def start(p, carry):
        v = symmetric_times([ki[k, p] for k in range(6)], [OMEGA * g[c, p] for c in range(3)])
        va[0, p] = jnp.minimum(v[0], g[3, p])
        va[1, p] = v[1]
        va[2, p] = v[2]
        return carry

    lax.fori_loop(0, 16, start, 0, unroll=4)

    def sweep(src, dst):
        def body(p, carry):
            rest = []
            for c in range(3):
                near = src[c, p - 1] + src[c, p + 1] + beside(src[c, p])
                rest.append(g[c, p] + near)
            step = symmetric_times([ki[k, p] for k in range(6)], rest)
            new = [KEEP * src[c, p] + OMEGA * step[c] for c in range(3)]
            dst[0, p] = jnp.minimum(new[0], g[3, p])
            dst[1, p] = new[1]
            dst[2, p] = new[2]
            return carry

        return body

    lax.fori_loop(1, 15, sweep(va, vb), 0, unroll=4)

    def third(q, carry):
        total = None
        for p in (2 * q, 2 * q + 1):
            mat = [gk[k, p] for k in range(6)]
            kv = symmetric_times(mat, [vb[c, p] for c in range(3)])
            part = []
            for c in range(3):
                near = vb[c, p - 1] + vb[c, p + 1] + beside(vb[c, p])
                part.append(g[c, p] - (kv[c] - near))
            part.append(g[3, p] - vb[0, p])
            if total is None:
                total = part
            else:
                total = [jnp.minimum(x, y) if i == 3 else x + y for i, (x, y) in enumerate(zip(total, part))]
        force = [0.25 * pair_spread(total[c], jnp.add) for c in range(3)]
        room = pair_spread(total[3], jnp.minimum)
        v = symmetric_times([k3[k, q] for k in range(6)], [OMEGA * x for x in force])
        v[0] = jnp.minimum(v[0], room)
        for c in range(3):
            f3[c, q] = force[c]
            l3[c, q] = v[c]
        o3[q] = room
        return carry

    lax.fori_loop(1, 7, third, 0, unroll=3)

    def lowest(q, carry):
        rest = []
        for c in range(3):
            near = l3[c, q - 1] + l3[c, q + 1] + beside(l3[c, q], 2)
            rest.append(f3[c, q] + near)
        step = symmetric_times([k3[k, q] for k in range(6)], rest)
        new = [KEEP * l3[c, q] + OMEGA * step[c] for c in range(3)]
        new[0] = jnp.minimum(new[0], o3[q])
        for c in range(3):
            for p in (2 * q, 2 * q + 1):
                va[c, p] = vb[c, p] + new[c]
        return carry

    lax.fori_loop(2, 6, lowest, 0, unroll=4)
    lax.fori_loop(5, 11, sweep(va, vb), 0, unroll=3)
    lax.fori_loop(6, 10, sweep(vb, va), 0, unroll=4)
    for c in range(3):
        for k in range(4):
            mid2[c, k, 0:10, :] = va[c, 6 + k, 0:10, :]
            mid2[c, k, 10:12, :] = va[c, 6 + k, 22:24, :]
        for k in range(2):
            own[c, k, 0:10, :] = va[c, 8 - 2 * par + k, 0:10, :]
            own[c, k, 10:12, :] = va[c, 8 - 2 * par + k, 22:24, :]


def gather_pre(pos, pre, ge, go, r1e, r1o, be, bo, clip, v0, clip_x):
    even, inside = sides(pos[0])
    up, inner = sides(pos[1])
    for c in range(3):
        for p in range(6):
            v0[c, p + 2] = pre[c, p]
        for p in range(4):
            to = v0.at[c, p + 3]
            to[21:23, :], to[17:19, :] = get_rows(r1e, r1o, up, inner, 56 + c * 2 + p // 2, 2 * (p % 2), 2)
        for side in range(2):
            low = side == 0
            n = 2 * c + side
            to = v0.at[c, 2 if low else 7]
            to[22:24, :], to[16:18, :] = get_rows(r1e, r1o, up, inner, 56 + 6 + n // 2, 2 * (n % 2), 2)
            for k in range(2):
                to = v0.at[c, k if low else 8 + k]
                to[0:16, :] = halo_plane(ge, go, even, inside, low, 2 * c + k)
            k = 1 if low else 0
            to = v0.at[c, 1 if low else 8]
            to[23:24, :] = get_extra(ge, go, even, inside, low, (c * 2 + k) * 2, 1)
            to[16:17, :] = get_extra(ge, go, even, inside, low, (c * 2 + k) * 2 + 1, 1)
    for p in range(4):
        to = clip_x.at[p + 3]
        to[0:16, :] = clip[p].astype(F32)
        to[21:24, :], to[16:19, :] = get_rows(be, bo, up, inner, 36 + p, 0, 3)
    for side in range(2):
        low = side == 0
        for k in range(3):
            to = clip_x.at[k if low else 7 + k]
            to[0:16, :] = halo_plane(ge, go, even, inside, low, 6 + k + (1 if low else 0))
        to = clip_x.at[2 if low else 7]
        n = 12 + 4 * (3 if low else 0)
        to[22:24, :] = get_extra(ge, go, even, inside, low, n, 2)
        to[16:18, :] = get_extra(ge, go, even, inside, low, n + 2, 2)
        n = 12 + 4 * (2 if low else 1)
        to = clip_x.at[1 if low else 8]
        to[23:24, :] = get_extra(ge, go, even, inside, low, n + 1, 1)
        to[16:17, :] = get_extra(ge, go, even, inside, low, n + 2, 1)


def finish(
    pos, held, mid2, other, force_x, kinv_x, obst_x, clip_x, main, cross,
    moved, residual, v0, v1, v2, mid_x, fine,
):
    par = jnp.bitwise_and(pos[0], 1)
    i, j = rows((128, 256)), lanes((128, 256))
    copy = jnp.where(lax.shift_right_logical(j, 1) == i, 1.0, 0.0)
    for c in range(3):
        mid_x[c, pl.ds(2 * par, 4)] = mid2[c]
        mid_x[c, pl.ds(4 * (1 - par), 2)] = other[c]
    wide = jnp.dot(
        mid_x[...].reshape(3 * 6 * 16, 128), copy, precision=HIGH, preferred_element_type=F32
    )
    for c in range(3):
        for k in range(6):
            x = wide[(c * 6 + k) * 16 : (c * 6 + k) * 16 + 16]
            for h in range(2):
                y = x[:, 128 * h : 128 * h + 128]
                fine[h, pl.ds(0, 16, 2), :] = y
                fine[h, pl.ds(1, 16, 2), :] = y
            up2 = jnp.concatenate([fine[0, 0:24, :], fine[1, 0:24, :]], 1)
            for p in range(10):
                if (p + 1) // 2 == k:
                    add = jnp.where(clip_x[p] == 1.0, 0.0, up2) if c == 0 else up2
                    v0[c, p] = held[c, p] + add
    smooth(v0, force_x, kinv_x, obst_x, v1, v2)
    for p in range(4):
        out = residual_plane(v2, force_x, main, cross, p)
        for c in range(3):
            residual[c, p] = out[c]
            moved[c, p] = v2[c, p + 1, 0:16, :]


def call(kernel, outs, scratch, *args, limit=0):
    vm = pl.BlockSpec(memory_space=pltpu.VMEM)
    source = pl.BlockSpec(memory_space=pltpu.HBM) if limit else vm
    return pl.pallas_call(
        kernel,
        out_shape=[jax.ShapeDtypeStruct(x, F32) for x in outs],
        in_specs=[pl.BlockSpec(memory_space=pltpu.SMEM)] + [source] * (len(args) - 1),
        out_specs=[vm] * len(outs),
        scratch_shapes=[pltpu.VMEM(x, F32) if isinstance(x, tuple) else x for x in scratch],
        compiler_params=pltpu.CompilerParams(vmem_limit_bytes=limit or 32 * 1024 * 1024),
    )(*args)


EVEN = [(i, i ^ 1) for i in range(16)]
ODD = [(i, (((i + 1) ^ 1) - 1) % 16) for i in range(16)]


def swap_even(x, axis):
    return lax.ppermute(x, axis, EVEN)


def swap_odd(x, axis):
    return lax.ppermute(x, axis, ODD)


def local(disp, trac, heat, main, cross, clear, touch, clip):
    pos = jnp.stack([lax.axis_index("grp"), lax.axis_index("brick")]).astype(jnp.int32)
    own, vec, six = (4, 16, 256), (3, 4, 16, 256), (6, 4, 16, 256)
    kinv, obst, me, mo, be, bo, k0 = call(
        load_pack,
        [six, own, (35, 16, 256), (32, 16, 256), (40, 8, 128), (40, 8, 128), (12, 8, 128)],
        [vec, vec, own, vec, vec, own, pltpu.VMEM(own, jnp.int32), pltpu.VMEM(own, jnp.int32),
         (12, 2, 16, 128), (96, 256), pltpu.SemaphoreType.DMA((8,))],
        pos, *[pltpu.with_memory_space_constraint(z, pltpu.HBM) for z in (disp, trac, heat, main, cross, clear, touch, clip)], limit=32 * 1024 * 1024,
    )
    re, ro = swap_even(me, "grp"), swap_odd(mo, "grp")
    re_b, ro_b = swap_even(be, "brick"), swap_odd(bo, "brick")
    ce, co, k01 = call(pack_corner, [(13, 8, 128)] * 2 + [(24, 8, 128)], [], pos, re, ro, k0)
    re_c, ro_c = swap_even(ce, "brick"), swap_odd(co, "brick")
    k23 = swap_odd(k01, "grp")
    force_x, kinv_x, obst_x, pre, b0, planes, pe, po = call(
        presmooth,
        [(3, 8, 24, 256), (6, 8, 24, 256), (8, 24, 256), (3, 6, 24, 256), (8, 8, 128),
         (12, 16, 256), (9, 8, 128), (9, 8, 128)],
        [(3, 10, 24, 256), (10, 24, 256), (3, 8, 24, 256), (4, 2, 16, 128), (64, 256)],
        pos, disp, heat, clip, trac, kinv, obst, main, cross, clear, touch,
        re, ro, re_b, ro_b, re_c, ro_c,
    )
    eb = swap_even(jnp.concatenate([b0, k23], 0), "grp")
    ob = swap_odd(jnp.concatenate([b0, eb], 0), "grp")
    go = swap_odd(planes, "grp")
    planes, eb = lax.optimization_barrier((planes, eb))
    ge = swap_even(planes, "grp")
    after, go = lax.optimization_barrier((b0, go))
    r1e = swap_even(jnp.concatenate([after, k01, k23, pe], 0), "brick")
    r1o = swap_odd(jnp.concatenate([after, k01, k23, po], 0), "brick")
    after, ge = lax.optimization_barrier((eb, ge))
    middle = jnp.concatenate([after, ob], 0)
    rme, rmo = swap_even(middle, "brick"), swap_odd(middle, "brick")
    b3 = swap_even(ob[:16], "grp")
    b4 = swap_odd(b3, "grp")
    last = jnp.concatenate([b3, b4], 0)
    r2e, r2o = swap_even(last, "brick"), swap_odd(last, "brick")
    field, third = (3, 16, 24, 128), (3, 8, 24, 128)
    gk, ki, k3 = call(
        coarse_blocks,
        [(6, 16, 24, 128), (6, 16, 24, 128), (6, 8, 24, 128)],
        [],
        pos, eb, ob, k01, k23, r1e, r1o, rme, rmo,
    )
    mid2, mine = call(
        coarse,
        [(3, 4, 16, 128), (3, 2, 16, 128)],
        [(4, 16, 24, 128), field, field, third, (8, 24, 128), third],
        pos, b0, eb, ob, b3, b4, r1e, r1o, rme, rmo, r2e, r2o, gk, ki, k3,
    )
    other = swap_even(mine, "grp")
    held, clip_x = call(
        gather_pre, [(3, 10, 24, 256), (10, 24, 256)], [],
        pos, pre, ge, go, r1e, r1o, re_b, ro_b, clip,
    )
    return tuple(
        call(
            finish,
            [vec, vec],
            [(3, 10, 24, 256), (3, 8, 24, 256), (3, 6, 24, 256), (3, 6, 16, 128), (2, 32, 128)],
            pos, held, mid2, other, force_x, kinv_x, obst_x, clip_x, main, cross,
        )
    )


def solution(mesh):
    vector, scalar = P(None, "grp", "brick", None), P("grp", "brick", None)
    return jax.shard_map(
        local,
        mesh=mesh,
        in_specs=(vector, vector, scalar, vector, vector, scalar, scalar, scalar),
        out_specs=(vector, vector),
        check_vma=False,
    )
```

```python
import jax
import jax.numpy as jnp
from jax import lax
from jax.experimental import pallas as pl
from jax.experimental.pallas import tpu as pltpu
from jax.sharding import PartitionSpec as P

OMEGA = 0.6
KEEP = 0.4
FREE = 1000.0
F32 = jnp.float32
HIGH = lax.Precision.HIGHEST
EVEN_SLOTS = (4, 5, 3, 2, 6, 7, 1, 0)


def inverse(a, b, c, d, e, f):
    i00 = b * c - e * e
    i11 = a * c - f * f
    i22 = a * b - d * d
    i01 = f * e - d * c
    i12 = d * f - a * e
    i02 = d * e - b * f
    det = a * i00 + d * i01 + f * i02
    scale = jnp.where(det == 0.0, 0.0, 1.0 / jnp.where(det == 0.0, 1.0, det))
    return [i00 * scale, i11 * scale, i22 * scale, i01 * scale, i12 * scale, i02 * scale]


def symmetric_times(m, r):
    return [
        m[0] * r[0] + m[3] * r[1] + m[5] * r[2],
        m[3] * r[0] + m[1] * r[1] + m[4] * r[2],
        m[5] * r[0] + m[4] * r[1] + m[2] * r[2],
    ]


def lanes(shape):
    return lax.broadcasted_iota(jnp.int32, shape, 1)


def rows(shape):
    return lax.broadcasted_iota(jnp.int32, shape, 0)


def beside(x, step=1):
    n, m = x.shape
    lane = lanes(x.shape)
    left = jnp.where(lane < step, 0.0, pltpu.roll(x, step, axis=1))
    right = jnp.where(lane >= m - step, 0.0, pltpu.roll(x, m - step, axis=1))
    return (left + right) + (pltpu.roll(x, step, axis=0) + pltpu.roll(x, n - step, axis=0))


def sides(g):
    return (jnp.bitwise_and(g, 1) == 0), jnp.logical_and(g > 0, g < 15)


def put(msg, t, r, x):
    n = x.shape[0]
    msg[t, r : r + n, :] = x[:, :128]
    msg[t, r + 4 : r + 4 + n, :] = x[:, 128:]


def put_rows(be, bo, up, t, r, x, n, skip=0):
    low, high = x[skip : skip + n], x[16 - skip - n : 16 - skip]
    put(be, t, r, jnp.where(up, high, low))
    put(bo, t, r, jnp.where(up, low, high))


def get_rows(be, bo, up, inside, t, r, n):
    e = jnp.concatenate([be[t, r : r + n, :], be[t, r + 4 : r + 4 + n, :]], 1)
    o = jnp.concatenate([bo[t, r : r + n, :], bo[t, r + 4 : r + 4 + n, :]], 1)
    o = jnp.where(inside, o, 0.0)
    return jnp.where(up, o, e), jnp.where(up, e, o)


def fields(disp, heat, trac, kinv, obst):
    wide = [lambda p, c=c: disp[c, p] for c in range(3)]
    wide += [lambda p: heat[p]]
    near = [lambda p, c=c: trac[c, p] for c in range(3)]
    near += [lambda p, k=k: kinv[k, p] for k in range(6)]
    near += [lambda p: obst[p]]
    return wide, near


def load_pack(
    pos, disp_h, trac_h, heat_h, main_h, cross_h, clear_h, touch_h, clip_h,
    kinv, obst, me, mo, be, bo, k0,
    disp, trac, heat, main, cross, clear, touch, clip, rest, gath, sem,
):
    pairs = [
        (main_h, main), (cross_h, cross), (clear_h, clear), (touch_h, touch),
        (disp_h, disp), (trac_h, trac), (heat_h, heat), (clip_h, clip),
    ]
    copies = [pltpu.make_async_copy(x, y, sem.at[i]) for i, (x, y) in enumerate(pairs)]
    for c in copies:
        c.start()
    par = jnp.bitwise_and(pos[0], 1)
    up = jnp.bitwise_and(pos[1], 1) == 0
    copies[0].wait()
    copies[1].wait()

    def invert(p, carry):
        inv = inverse(main[0, p], main[1, p], main[2, p], cross[0, p], cross[1, p], cross[2, p])
        for k in range(6):
            kinv[k, p] = inv[k]
        return carry

    lax.fori_loop(0, 4, invert, 0)
    for k in range(6):
        src, c = (main, k) if k < 3 else (cross, k - 3)
        for q in range(2):
            x = 0.125 * (src[c, 2 * q] + src[c, 2 * q + 1])
            gath[(2 * k + q) * 8 : (2 * k + q) * 8 + 8, :] = pair_rows(rest.at[2 * k + q], x, jnp.add)
    k0[...] = pair_lanes(gath[...]).reshape(12, 8, 128)
    copies[2].wait()
    copies[3].wait()
    obst[...] = jnp.where(touch[...] == 1, clear[...], FREE)
    for c in copies[4:]:
        c.wait()
    for msg, at in ((me, 1 - par), (mo, par)):
        for c in range(3):
            msg[3 * c : 3 * c + 3] = disp[c, pl.ds(at, 3)]
        msg[9:12] = heat[pl.ds(at, 3)]
        for c in range(3):
            msg[12 + 2 * c : 14 + 2 * c] = trac[c, pl.ds(2 * at, 2)]
        for k in range(6):
            msg[18 + 2 * k : 20 + 2 * k] = kinv[k, pl.ds(2 * at, 2)]
        msg[30:32] = obst[pl.ds(2 * at, 2)]
    for t in range(12):
        r, h = 8 * (t % 4 // 2), 128 * (t % 2)
        me[32 + t // 4, r : r + 8, h : h + 128] = k0[t]
    wide, near = fields(disp, heat, trac, kinv, obst)
    for f in range(4):
        for p in range(4):
            put_rows(be, bo, up, f * 4 + p, 0, wide[f](p), 3)
    for f in range(10):
        for p in range(4):
            put_rows(be, bo, up, 16 + f * 2 + p // 2, 2 * (p % 2), near[f](p), 2)
    for p in range(4):
        put_rows(be, bo, up, 36 + p, 0, clip[p].astype(F32), 3)


def halo_plane(re, ro, even, inside, low, k):
    e, o = re[k], jnp.where(inside, ro[k], 0.0)
    return jnp.where(even, o, e) if low else jnp.where(even, e, o)


def pack_corner(pos, re, ro, k0, be, bo, k01):
    k01[0:12] = k0[...]
    for t in range(12):
        r, h = 8 * (t % 4 // 2), 128 * (t % 2)
        k01[12 + t] = re[32 + t // 4, r : r + 8, h : h + 128]
    even, inside = sides(pos[0])
    up = jnp.bitwise_and(pos[1], 1) == 0
    for f in range(4):
        for side in range(2):
            low = side == 0
            x = halo_plane(re, ro, even, inside, low, 3 * f + (2 if low else 0))
            put_rows(be, bo, up, f * 2 + side, 0, x, 2)
            x = halo_plane(re, ro, even, inside, low, 3 * f + 1)
            put_rows(be, bo, up, f * 2 + side, 2, x, 1)
    for f in range(10):
        for side in range(2):
            low = side == 0
            n = f * 2 + side
            x = halo_plane(re, ro, even, inside, low, 12 + 2 * f + (1 if low else 0))
            put_rows(be, bo, up, 8 + n // 4, n % 4, x, 1)


def smooth(v0, force, kinv, obst, v1, v2):
    def one(src, dst, shift, planes):
        def body(p, carry):
            rest = []
            for c in range(3):
                near = src[c, p] + src[c, p + 2] + beside(src[c, p + 1])
                rest.append(force[c, p + shift] + near)
            inv = [kinv[k, p + shift] for k in range(6)]
            step = symmetric_times(inv, rest)
            new = [KEEP * src[c, p + 1] + OMEGA * step[c] for c in range(3)]
            dst[0, p] = jnp.minimum(new[0], obst[p + shift])
            dst[1, p] = new[1]
            dst[2, p] = new[2]
            return carry

        lax.fori_loop(0, planes, body, 0, unroll=4)

    one(v0, v1, 0, 8)
    one(v1, v2, 1, 6)


def residual_plane(v2, force, main, cross, p):
    own = [v2[c, p + 1][0:16] for c in range(3)]
    mat = [main[c, p] for c in range(3)] + [cross[c, p] for c in range(3)]
    kv = symmetric_times(mat, own)
    out = []
    for c in range(3):
        near = v2[c, p, 0:16, :] + v2[c, p + 2, 0:16, :] + beside(v2[c, p + 1])[0:16]
        out.append(force[c, p + 2, 0:16, :] - (kv[c] - near))
    return out


def pair_rows(room, x, op):
    for h in range(2):
        room[h] = x[:, 128 * h : 128 * h + 128]
    return jnp.concatenate(
        [op(room[h, pl.ds(0, 8, 2), :], room[h, pl.ds(1, 8, 2), :]) for h in range(2)], 1
    )


def pair_lanes(x):
    i, j = rows((256, 128)), lanes((256, 128))
    pick = jnp.where(lax.shift_right_logical(i, 1) == j, 1.0, 0.0)
    return jnp.dot(x, pick, precision=HIGH, preferred_element_type=F32)


def put_extra(planes, n, x):
    planes[10 + n // 16, n % 16 : n % 16 + x.shape[0], :] = x


def get_extra(ge, go, even, inside, low, n, m):
    e = ge[10 + n // 16, n % 16 : n % 16 + m, :]
    o = jnp.where(inside, go[10 + n // 16, n % 16 : n % 16 + m, :], 0.0)
    return jnp.where(even, o, e) if low else jnp.where(even, e, o)


def presmooth(
    pos, disp, heat, clip, trac, kinv, obst, main, cross, clear, touch,
    re, ro, be, bo, ce, co,
    force_x, kinv_x, obst_x, v2, small_out, planes_out, pe, po,
    v0, heat_x, v1, rest, gath,
):
    even, inside = sides(pos[0])
    up, inner = sides(pos[1])
    wide, near = fields(disp, heat, trac, kinv, obst)
    wide_to = [lambda p, c=c: v0.at[c, p] for c in range(3)]
    wide_to += [lambda p: heat_x.at[p]]
    near_to = [lambda p, c=c: force_x.at[c, p] for c in range(3)]
    near_to += [lambda p, k=k: kinv_x.at[k, p] for k in range(6)]
    near_to += [lambda p: obst_x.at[p]]
    for f in range(4):
        for p in range(4):
            to = wide_to[f](p + 3)
            to[0:16, :] = wide[f](p)
            to[21:24, :], to[16:19, :] = get_rows(be, bo, up, inner, f * 4 + p, 0, 3)
        for side in range(2):
            low = side == 0
            for k in range(3):
                to = wide_to[f](k if low else 7 + k)
                to[0:16, :] = halo_plane(re, ro, even, inside, low, 3 * f + k)
            to = wide_to[f](2 if low else 7)
            to[22:24, :], to[16:18, :] = get_rows(ce, co, up, inner, f * 2 + side, 0, 2)
            to = wide_to[f](1 if low else 8)
            to[23:24, :], to[16:17, :] = get_rows(ce, co, up, inner, f * 2 + side, 2, 1)
    for f in range(10):
        for p in range(4):
            to = near_to[f](p + 2)
            to[0:16, :] = near[f](p)
            to[22:24, :], to[16:18, :] = get_rows(be, bo, up, inner, 16 + f * 2 + p // 2, 2 * (p % 2), 2)
        for side in range(2):
            low = side == 0
            for k in range(2):
                to = near_to[f](k if low else 6 + k)
                to[0:16, :] = halo_plane(re, ro, even, inside, low, 12 + 2 * f + k)
            n = f * 2 + side
            to = near_to[f](1 if low else 6)
            to[23:24, :], to[16:17, :] = get_rows(ce, co, up, inner, 8 + n // 4, n % 4, 1)

    def drift(p, carry):
        h = heat_x[p + 1]
        lane = lanes(h.shape)
        right = jnp.where(lane == 255, 0.0, pltpu.roll(h, 255, axis=1))
        left = jnp.where(lane == 0, 0.0, pltpu.roll(h, 1, axis=1))
        force_x[0, p] = force_x[0, p] - (heat_x[p + 2] - heat_x[p])
        force_x[1, p] = force_x[1, p] - (pltpu.roll(h, 23, axis=0) - pltpu.roll(h, 1, axis=0))
        force_x[2, p] = force_x[2, p] - (right - left)
        return carry

    lax.fori_loop(0, 8, drift, 0, unroll=4)
    smooth(v0, force_x, kinv_x, obst_x, v1, v2)

    shape = (16, 256)
    first = jnp.bitwise_and(lanes(shape), 1) == 0
    for q in range(2):
        low = None
        for p in (2 * q, 2 * q + 1):
            out = residual_plane(v2, force_x, main, cross, p)
            cut = clip[p] == 1
            out[0] = jnp.where(cut, 0.0, out[0])
            gap = jnp.logical_and(touch[p] == 1, clip[p] != 1)
            room = jnp.where(gap, clear[p] - v2[0, p + 1, 0:16, :], FREE)
            part = out + [room]
            if low is None:
                low = part
            else:
                low = [jnp.minimum(x, y) if i == 3 else x + y for i, (x, y) in enumerate(zip(low, part))]
        for i in range(4):
            x = pair_rows(rest.at[i], low[i] if i == 3 else 0.25 * low[i], jnp.minimum if i == 3 else jnp.add)
            if i == 3:
                x = jnp.minimum(x, pltpu.roll(x, 255, axis=1))
                x = jnp.where(first[0:8], x, 0.0)
            gath[(2 * i + q) * 8 : (2 * i + q) * 8 + 8, :] = x
    small_out[...] = pair_lanes(gath[...]).reshape(8, 8, 128)
    for c in range(3):
        for k in range(2):
            planes_out[2 * c + k] = v2[c, k + 2, 0:16, :]
            for side in range(2):
                put_extra(planes_out, (c * 2 + k) * 2 + side, v2[c, k + 2, 16 if side else 23 : 17 if side else 24, :])
    for p in range(4):
        planes_out[6 + p] = clip[p].astype(F32)
        low, high = get_rows(be, bo, up, inner, 36 + p, 0, 3)
        put_extra(planes_out, 12 + 4 * p, low[1:3])
        put_extra(planes_out, 14 + 4 * p, high[0:2])
    for c in range(3):
        for p in range(4):
            put_rows(pe, po, up, c * 2 + p // 2, 2 * (p % 2), v2[c, p + 1, 0:16, :], 2, 1)
        for side in range(2):
            n = 2 * c + side
            put_rows(pe, po, up, 6 + n // 2, 2 * (n % 2), v2[c, 5 * side, 0:16, :], 2)


def pair_spread(x, op):
    n, m = x.shape
    even = jnp.bitwise_and(lanes(x.shape), 1) == 0
    x = op(x, jnp.where(even, pltpu.roll(x, m - 1, axis=1), pltpu.roll(x, 1, axis=1)))
    even = jnp.bitwise_and(rows(x.shape), 1) == 0
    return op(x, jnp.where(even, pltpu.roll(x, n - 1, axis=0), pltpu.roll(x, 1, axis=0)))


SLOTS = (
    ("b0", 0, "one", 0, "k01", 0, "one", 8), ("eb", 0, "mid", 0, "k01", 12, "one", 20),
    ("ob", 0, "mid", 32, "k23", 0, "one", 32), ("ob", 8, "mid", 40, "k23", 12, "one", 44),
    ("b3", 0, "two", 0, "eb", 8, "mid", 8), ("b3", 8, "two", 8, "eb", 20, "mid", 20),
    ("b4", 0, "two", 16, "ob", 16, "mid", 48), ("b4", 8, "two", 24, "ob", 28, "mid", 60),
)


def lay_window(pos, refs, g, force):
    par = jnp.bitwise_and(pos[0], 1)
    up, inner = sides(pos[1])
    grp = pos[0]
    for s, (mine, m, row, r, mat, k, krow, kr) in enumerate(SLOTS):
        if not force:
            mine, m, row, r = mat, k, krow, kr
        mine, (re, ro) = refs[mine], refs[row]
        place = jnp.where(par == 0, EVEN_SLOTS[s], 7 - EVEN_SLOTS[s])
        where = grp + place - jnp.where(par == 0, 4, 3)
        real = jnp.logical_and(where >= 0, where < 16)
        real_o = jnp.logical_and(real, inner)

        def fill(f, carry):
            for q in range(2):
                t = 2 * f + q
                a = jnp.where(real, re[r + t], 0.0)
                b = jnp.where(real_o, ro[r + t], 0.0)
                to = g.at[f, 2 * place + q]
                to[0:8, :] = jnp.where(real, mine[m + t], 0.0)
                to[8:16, :] = jnp.where(up, a, b)
                to[16:24, :] = jnp.where(up, b, a)
            return carry

        lax.fori_loop(0, 4 if force else 6, fill, 0, unroll=True)


def coarse_blocks(pos, eb, ob, k01, k23, r1e, r1o, rme, rmo, gk, ki, k3):
    refs = dict(eb=eb, ob=ob, k01=k01, k23=k23, one=(r1e, r1o), mid=(rme, rmo))
    lay_window(pos, refs, gk, False)

    def invert(p, carry):
        inv = inverse(*[gk[k, p] for k in range(6)])
        for k in range(6):
            ki[k, p] = inv[k]
        return carry

    lax.fori_loop(0, 16, invert, 0, unroll=4)

    def third(q, carry):
        mat = [0.125 * pair_spread(gk[k, 2 * q] + gk[k, 2 * q + 1], jnp.add) for k in range(6)]
        inv = inverse(*mat)
        for k in range(6):
            k3[k, q] = inv[k]
        return carry

    lax.fori_loop(1, 7, third, 0, unroll=2)


def coarse(
    pos, b0, eb, ob, b3, b4, r1e, r1o, rme, rmo, r2e, r2o, gk, ki, k3,
    mid2, own, g, va, vb, f3, o3, l3,
):
    par = jnp.bitwise_and(pos[0], 1)
    refs = dict(b0=b0, eb=eb, ob=ob, b3=b3, b4=b4, one=(r1e, r1o), mid=(rme, rmo), two=(r2e, r2o))
    lay_window(pos, refs, g, True)

    def start(p, carry):
        v = symmetric_times([ki[k, p] for k in range(6)], [OMEGA * g[c, p] for c in range(3)])
        va[0, p] = jnp.minimum(v[0], g[3, p])
        va[1, p] = v[1]
        va[2, p] = v[2]
        return carry

    lax.fori_loop(0, 16, start, 0, unroll=4)

    def sweep(src, dst):
        def body(p, carry):
            rest = []
            for c in range(3):
                near = src[c, p - 1] + src[c, p + 1] + beside(src[c, p])
                rest.append(g[c, p] + near)
            step = symmetric_times([ki[k, p] for k in range(6)], rest)
            new = [KEEP * src[c, p] + OMEGA * step[c] for c in range(3)]
            dst[0, p] = jnp.minimum(new[0], g[3, p])
            dst[1, p] = new[1]
            dst[2, p] = new[2]
            return carry

        return body

    lax.fori_loop(1, 15, sweep(va, vb), 0, unroll=4)

    def third(q, carry):
        total = None
        for p in (2 * q, 2 * q + 1):
            mat = [gk[k, p] for k in range(6)]
            kv = symmetric_times(mat, [vb[c, p] for c in range(3)])
            part = []
            for c in range(3):
                near = vb[c, p - 1] + vb[c, p + 1] + beside(vb[c, p])
                part.append(g[c, p] - (kv[c] - near))
            part.append(g[3, p] - vb[0, p])
            if total is None:
                total = part
            else:
                total = [jnp.minimum(x, y) if i == 3 else x + y for i, (x, y) in enumerate(zip(total, part))]
        force = [0.25 * pair_spread(total[c], jnp.add) for c in range(3)]
        room = pair_spread(total[3], jnp.minimum)
        v = symmetric_times([k3[k, q] for k in range(6)], [OMEGA * x for x in force])
        v[0] = jnp.minimum(v[0], room)
        for c in range(3):
            f3[c, q] = force[c]
            l3[c, q] = v[c]
        o3[q] = room
        return carry

    lax.fori_loop(1, 7, third, 0, unroll=4)

    def lowest(q, carry):
        rest = []
        for c in range(3):
            near = l3[c, q - 1] + l3[c, q + 1] + beside(l3[c, q], 2)
            rest.append(f3[c, q] + near)
        step = symmetric_times([k3[k, q] for k in range(6)], rest)
        new = [KEEP * l3[c, q] + OMEGA * step[c] for c in range(3)]
        new[0] = jnp.minimum(new[0], o3[q])
        for c in range(3):
            for p in (2 * q, 2 * q + 1):
                va[c, p] = vb[c, p] + new[c]
        return carry

    lax.fori_loop(2, 6, lowest, 0, unroll=4)
    lax.fori_loop(5, 11, sweep(va, vb), 0, unroll=4)
    lax.fori_loop(6, 10, sweep(vb, va), 0, unroll=4)
    for c in range(3):
        for k in range(4):
            mid2[c, k, 0:10, :] = va[c, 6 + k, 0:10, :]
            mid2[c, k, 10:12, :] = va[c, 6 + k, 22:24, :]
        for k in range(2):
            own[c, k, 0:10, :] = va[c, 8 - 2 * par + k, 0:10, :]
            own[c, k, 10:12, :] = va[c, 8 - 2 * par + k, 22:24, :]


def gather_pre(pos, pre, ge, go, r1e, r1o, be, bo, clip, v0, clip_x):
    even, inside = sides(pos[0])
    up, inner = sides(pos[1])
    for c in range(3):
        for p in range(6):
            v0[c, p + 2] = pre[c, p]
        for p in range(4):
            to = v0.at[c, p + 3]
            to[21:23, :], to[17:19, :] = get_rows(r1e, r1o, up, inner, 56 + c * 2 + p // 2, 2 * (p % 2), 2)
        for side in range(2):
            low = side == 0
            n = 2 * c + side
            to = v0.at[c, 2 if low else 7]
            to[22:24, :], to[16:18, :] = get_rows(r1e, r1o, up, inner, 56 + 6 + n // 2, 2 * (n % 2), 2)
            for k in range(2):
                to = v0.at[c, k if low else 8 + k]
                to[0:16, :] = halo_plane(ge, go, even, inside, low, 2 * c + k)
            k = 1 if low else 0
            to = v0.at[c, 1 if low else 8]
            to[23:24, :] = get_extra(ge, go, even, inside, low, (c * 2 + k) * 2, 1)
            to[16:17, :] = get_extra(ge, go, even, inside, low, (c * 2 + k) * 2 + 1, 1)
    for p in range(4):
        to = clip_x.at[p + 3]
        to[0:16, :] = clip[p].astype(F32)
        to[21:24, :], to[16:19, :] = get_rows(be, bo, up, inner, 36 + p, 0, 3)
    for side in range(2):
        low = side == 0
        for k in range(3):
            to = clip_x.at[k if low else 7 + k]
            to[0:16, :] = halo_plane(ge, go, even, inside, low, 6 + k + (1 if low else 0))
        to = clip_x.at[2 if low else 7]
        n = 12 + 4 * (3 if low else 0)
        to[22:24, :] = get_extra(ge, go, even, inside, low, n, 2)
        to[16:18, :] = get_extra(ge, go, even, inside, low, n + 2, 2)
        n = 12 + 4 * (2 if low else 1)
        to = clip_x.at[1 if low else 8]
        to[23:24, :] = get_extra(ge, go, even, inside, low, n + 1, 1)
        to[16:17, :] = get_extra(ge, go, even, inside, low, n + 2, 1)


def finish(
    pos, held, mid2, other, force_x, kinv_x, obst_x, clip_x, main, cross,
    moved, residual, v0, v1, v2, mid_x, fine,
):
    par = jnp.bitwise_and(pos[0], 1)
    i, j = rows((128, 256)), lanes((128, 256))
    copy = jnp.where(lax.shift_right_logical(j, 1) == i, 1.0, 0.0)
    for c in range(3):
        mid_x[c, pl.ds(2 * par, 4)] = mid2[c]
        mid_x[c, pl.ds(4 * (1 - par), 2)] = other[c]
    wide = jnp.dot(
        mid_x[...].reshape(3 * 6 * 16, 128), copy, precision=HIGH, preferred_element_type=F32
    )
    for c in range(3):
        for k in range(6):
            x = wide[(c * 6 + k) * 16 : (c * 6 + k) * 16 + 16]
            for h in range(2):
                y = x[:, 128 * h : 128 * h + 128]
                fine[h, pl.ds(0, 16, 2), :] = y
                fine[h, pl.ds(1, 16, 2), :] = y
            up2 = jnp.concatenate([fine[0, 0:24, :], fine[1, 0:24, :]], 1)
            for p in range(10):
                if (p + 1) // 2 == k:
                    add = jnp.where(clip_x[p] == 1.0, 0.0, up2) if c == 0 else up2
                    v0[c, p] = held[c, p] + add
    smooth(v0, force_x, kinv_x, obst_x, v1, v2)
    for p in range(4):
        out = residual_plane(v2, force_x, main, cross, p)
        for c in range(3):
            residual[c, p] = out[c]
            moved[c, p] = v2[c, p + 1, 0:16, :]


def call(kernel, outs, scratch, *args, limit=0):
    vm = pl.BlockSpec(memory_space=pltpu.VMEM)
    source = pl.BlockSpec(memory_space=pltpu.HBM) if limit else vm
    return pl.pallas_call(
        kernel,
        out_shape=[jax.ShapeDtypeStruct(x, F32) for x in outs],
        in_specs=[pl.BlockSpec(memory_space=pltpu.SMEM)] + [source] * (len(args) - 1),
        out_specs=[vm] * len(outs),
        scratch_shapes=[pltpu.VMEM(x, F32) if isinstance(x, tuple) else x for x in scratch],
        compiler_params=pltpu.CompilerParams(vmem_limit_bytes=limit or 32 * 1024 * 1024),
    )(*args)


EVEN = [(i, i ^ 1) for i in range(16)]
ODD = [(i, (((i + 1) ^ 1) - 1) % 16) for i in range(16)]


def swap_even(x, axis):
    return lax.ppermute(x, axis, EVEN)


def swap_odd(x, axis):
    return lax.ppermute(x, axis, ODD)


def local(disp, trac, heat, main, cross, clear, touch, clip):
    pos = jnp.stack([lax.axis_index("grp"), lax.axis_index("brick")]).astype(jnp.int32)
    own, vec, six = (4, 16, 256), (3, 4, 16, 256), (6, 4, 16, 256)
    kinv, obst, me, mo, be, bo, k0 = call(
        load_pack,
        [six, own, (35, 16, 256), (32, 16, 256), (40, 8, 128), (40, 8, 128), (12, 8, 128)],
        [vec, vec, own, vec, vec, own, pltpu.VMEM(own, jnp.int32), pltpu.VMEM(own, jnp.int32),
         (12, 2, 16, 128), (96, 256), pltpu.SemaphoreType.DMA((8,))],
        pos, *[pltpu.with_memory_space_constraint(z, pltpu.HBM) for z in (disp, trac, heat, main, cross, clear, touch, clip)], limit=32 * 1024 * 1024,
    )
    re, ro = swap_even(me, "grp"), swap_odd(mo, "grp")
    re_b, ro_b = swap_even(be, "brick"), swap_odd(bo, "brick")
    ce, co, k01 = call(pack_corner, [(13, 8, 128)] * 2 + [(24, 8, 128)], [], pos, re, ro, k0)
    re_c, ro_c = swap_even(ce, "brick"), swap_odd(co, "brick")
    k23 = swap_odd(k01, "grp")
    force_x, kinv_x, obst_x, pre, b0, planes, pe, po = call(
        presmooth,
        [(3, 8, 24, 256), (6, 8, 24, 256), (8, 24, 256), (3, 6, 24, 256), (8, 8, 128),
         (12, 16, 256), (9, 8, 128), (9, 8, 128)],
        [(3, 10, 24, 256), (10, 24, 256), (3, 8, 24, 256), (4, 2, 16, 128), (64, 256)],
        pos, disp, heat, clip, trac, kinv, obst, main, cross, clear, touch,
        re, ro, re_b, ro_b, re_c, ro_c,
    )
    eb = swap_even(jnp.concatenate([b0, k23], 0), "grp")
    ob = swap_odd(jnp.concatenate([b0, eb], 0), "grp")
    ge, go = swap_even(planes, "grp"), swap_odd(planes, "grp")
    after, go = lax.optimization_barrier((b0, go))
    r1e = swap_even(jnp.concatenate([after, k01, k23, pe], 0), "brick")
    r1o = swap_odd(jnp.concatenate([after, k01, k23, po], 0), "brick")
    after, ge = lax.optimization_barrier((eb, ge))
    middle = jnp.concatenate([after, ob], 0)
    rme, rmo = swap_even(middle, "brick"), swap_odd(middle, "brick")
    b3 = swap_even(ob[:16], "grp")
    b4 = swap_odd(b3, "grp")
    last = jnp.concatenate([b3, b4], 0)
    r2e, r2o = swap_even(last, "brick"), swap_odd(last, "brick")
    field, third = (3, 16, 24, 128), (3, 8, 24, 128)
    gk, ki, k3 = call(
        coarse_blocks,
        [(6, 16, 24, 128), (6, 16, 24, 128), (6, 8, 24, 128)],
        [],
        pos, eb, ob, k01, k23, r1e, r1o, rme, rmo,
    )
    mid2, mine = call(
        coarse,
        [(3, 4, 16, 128), (3, 2, 16, 128)],
        [(4, 16, 24, 128), field, field, third, (8, 24, 128), third],
        pos, b0, eb, ob, b3, b4, r1e, r1o, rme, rmo, r2e, r2o, gk, ki, k3,
    )
    other = swap_even(mine, "grp")
    held, clip_x = call(
        gather_pre, [(3, 10, 24, 256), (10, 24, 256)], [],
        pos, pre, ge, go, r1e, r1o, re_b, ro_b, clip,
    )
    return tuple(
        call(
            finish,
            [vec, vec],
            [(3, 10, 24, 256), (3, 8, 24, 256), (3, 6, 24, 256), (3, 6, 16, 128), (2, 32, 128)],
            pos, held, mid2, other, force_x, kinv_x, obst_x, clip_x, main, cross,
        )
    )


def solution(mesh):
    vector, scalar = P(None, "grp", "brick", None), P("grp", "brick", None)
    return jax.shard_map(
        local,
        mesh=mesh,
        in_specs=(vector, vector, scalar, vector, vector, scalar, scalar, scalar),
        out_specs=(vector, vector),
        check_vma=False,
    )
```
